128 devices in a mesh: aa: 8 (over x, z_lo), ba: 16 (over y, z_hi, core).
Axes of the slice: x: 4, y: 4, z: 4 (z_hi: 2, z_lo: 2; z = z_hi * 2 + z_lo), core: 2. Of those that a mesh axis runs over, the one named last changes fastest.
Arguments:
- grid: bfloat16 [4, 4, 640, 2596], P(None, None, ('aa', 'ba')), may hold values from -6 to 6
- dep_row: int32 [640, 2596], P(('aa', 'ba')), may hold values from 0 to 1276, as said below
- dep_lon: int32 [4, 640, 2596], P(None, ('aa', 'ba')), may hold values from 0 to 2575, as said below
- lon_frac: float32 [4, 640, 2596], P(None, ('aa', 'ba')), may hold values from 0 to 1
- lat_frac: float32 [640, 2596], P(('aa', 'ba')), may hold values from 0 to 1
- wave_slot: int32 [640], replicated, may hold values from 0 to 639, each once
- legendre: bfloat16 [640, 2, 320, 640], P(('aa', 'ba')), may hold values from -6 to 6
Outputs:
- interpolated: bfloat16 [4, 4, 640, 2596], P(None, None, ('aa', 'ba'))
- spectral: float32 [16, 640, 640], P(None, ('aa', 'ba'))
The draws below stay inside these ranges and needn't reach their ends.
Inputs may be any that keep to these rules, and one draw needn't show every extreme that they name: For the arrival point in global row g, dep_row is g - 2 or g - 1, clipped to the range; the four stencil rows are dep_row to dep_row + 3. dep_lon[r] is a point index of global row dep_row + r, below that row's number of points. `wave_slot`: each wavenumber 0 to 639 stands in exactly one slot.
All inputs are finite; a program needn't handle non-finite values.
Results may differ from the reference program's by a relative error of at most 0.0062.
Values may be sent and summed in bfloat16 or wider, within the bound.
A program may use at most 64 MiB of HBM per device.

```python
import math
import jax
import jax.numpy as jnp
from jax import lax

LEV = 4
FIELDS = 4
HROWS = 640
PAIRLEN = 2596


def arrival_points():
    pair_index = jnp.arange(HROWS, dtype=jnp.int32)[:, None]
    column = jnp.arange(PAIRLEN, dtype=jnp.int32)[None, :]
    northern = pair_index < HROWS // 2
    inner_index = jnp.where(northern, pair_index, HROWS - 1 - pair_index)
    first_len = 16 + 4 * (HROWS // 2 - inner_index)
    first_half = column < first_len
    row_number = jnp.where(first_half, HROWS // 2 - inner_index, HROWS // 2 + 1 + inner_index)
    position = jnp.where(first_half, column, column - first_len)
    global_row = jnp.where(northern, row_number - 1, 2 * HROWS - row_number)
    grid_shape = (HROWS, PAIRLEN)
    return (jnp.broadcast_to(global_row, grid_shape), jnp.broadcast_to(position, grid_shape), jnp.broadcast_to(16 + 4 * row_number, grid_shape))


def row_size(global_row):
    number = jnp.where(global_row < HROWS, global_row + 1, 2 * HROWS - global_row)
    return 16 + 4 * number


def departures(key):
    global_row, position, own_length = arrival_points()
    grid_shape = (HROWS, PAIRLEN)
    row_drift = jax.random.randint(jax.random.fold_in(key, 7), grid_shape, -1, 1)
    cycle_phase = jnp.remainder(position, 5)
    row_drift = jnp.where(cycle_phase == 0, -1, jnp.where(cycle_phase == 1, 0, row_drift))
    base_row = jnp.clip(global_row + row_drift - 1, 0, 2 * HROWS - 4)
    jitter = jax.random.randint(jax.random.fold_in(key, 8), (4, HROWS, PAIRLEN), -2, 3)
    stencil_rows = base_row[None] + jnp.arange(4, dtype=jnp.int32)[:, None, None]
    lengths = row_size(stencil_rows)
    longitude = jnp.remainder(position[None] * lengths // own_length[None] + jitter, lengths)
    return (base_row.astype(jnp.int32), longitude.astype(jnp.int32))


def draw_dep_row(key, part):
    return departures(key)[0]


def draw_dep_lon(key, part):
    return departures(key)[1]


def block_scale(stream_key, shape, split, smallest, high):
    loudness = 1.0
    for axis_at, shards_of in split:
        steps = jax.random.uniform(jax.random.fold_in(jax.random.fold_in(stream_key, 6), axis_at), (shards_of,), jnp.float32, smallest / len(split), high / len(split))
        loudness = loudness * jnp.repeat(jnp.exp(steps), shape[axis_at] // shards_of).reshape((-1,) + (1,) * (len(shape) - 1 - axis_at))
    return loudness


def noise(stream_key, shape, spread, bound, shards=(), kind=jnp.bfloat16):
    factor_of = block_scale(stream_key, shape, shards, -0.22, 0.18) if shards else 1.0
    entries = jax.random.normal(stream_key, shape, jnp.float32) * spread * factor_of
    return jnp.minimum(jnp.maximum(entries, -bound), bound).astype(kind)


def setup_inputs(seed: int = 0) -> dict:
    arg_keys = jax.random.split(jax.random.key(seed), 8)
    return {
        "grid": noise(arg_keys[0], (FIELDS, LEV, HROWS, PAIRLEN), 1.0, 6.0, ((2, 128),)),
        "dep_row": draw_dep_row(jax.random.fold_in(arg_keys[7], 71), 0),
        "dep_lon": draw_dep_lon(jax.random.fold_in(arg_keys[7], 71), 0),
        "lon_frac": jnp.clip(1.0 * jax.random.uniform(arg_keys[3], (4, HROWS, PAIRLEN), jnp.float32) ** block_scale(arg_keys[3], (4, HROWS, PAIRLEN), ((1, 128),), -0.2, 0.2), 0.0, 1.0),
        "lat_frac": jnp.clip(1.0 * jax.random.uniform(arg_keys[4], (HROWS, PAIRLEN), jnp.float32) ** block_scale(arg_keys[4], (HROWS, PAIRLEN), ((0, 128),), -0.2, 0.2), 0.0, 1.0),
        "wave_slot": jax.random.permutation(arg_keys[5], HROWS).astype(jnp.int32),
        "legendre": noise(arg_keys[6], (HROWS, 2, HROWS // 2, HROWS), 1.0, 6.0, ((0, 128),)),
    }


def lagrange(fraction):
    return (-fraction * (fraction - 1.0) * (fraction - 2.0) / 6.0,
            (fraction + 1.0) * (fraction - 1.0) * (fraction - 2.0) / 2.0,
            -(fraction + 1.0) * fraction * (fraction - 2.0) / 2.0,
            (fraction + 1.0) * fraction * (fraction - 1.0) / 6.0)


def locate(global_row):
    northern = global_row < HROWS
    row_number = jnp.where(northern, global_row + 1, 2 * HROWS - global_row)
    first_half = row_number <= HROWS // 2
    inner_index = jnp.where(first_half, HROWS // 2 - row_number, row_number - HROWS // 2 - 1)
    pair_row = jnp.where(northern, inner_index, HROWS - 1 - inner_index)
    row_start = jnp.where(first_half, 0, 16 + 4 * (HROWS // 2 - inner_index))
    return pair_row, row_start, 16 + 4 * row_number


def fourier_pair(pair_index, values, waves):
    inner_index = jnp.where(pair_index < HROWS // 2, pair_index, HROWS - 1 - pair_index)
    first_len = 16 + 4 * (HROWS // 2 - inner_index)
    second_len = 16 + 4 * (HROWS // 2 + 1 + inner_index)
    column = jnp.arange(PAIRLEN, dtype=jnp.int32)
    first_half = column < first_len
    row_length = jnp.where(first_half, first_len, second_len)
    position = jnp.where(first_half, column, column - first_len)
    residue = jnp.remainder(position[:, None] * waves[None, :], row_length[:, None])
    angle = (2.0 * math.pi) * residue.astype(jnp.float32) / row_length[:, None].astype(jnp.float32)
    keeping = (2 * waves[None, :] < row_length[:, None]).astype(jnp.float32)
    table = jnp.concatenate([jnp.cos(angle) * keeping, -jnp.sin(angle) * keeping], axis=1).astype(jnp.bfloat16)
    zeros = jnp.zeros_like(values)
    stacked = jnp.concatenate([jnp.where(first_half[None, :], values, zeros),
                               jnp.where(first_half[None, :], zeros, values)], axis=0)
    product = jnp.dot(stacked, table, preferred_element_type=jnp.float32)
    scaling = 1.0 / jnp.stack([first_len, second_len]).astype(jnp.float32)
    product = product.reshape(2, values.shape[0], 2, waves.shape[0]) * scaling[:, None, None, None]
    return jnp.transpose(product, (2, 1, 0, 3)).astype(jnp.bfloat16)


def reference(grid, dep_row, dep_lon, lon_frac, lat_frac, wave_slot, legendre):
    lat_weights = lagrange(lat_frac)
    indices = []
    factors = []
    for stencil_row in range(4):
        pair_row, row_start, row_length = locate(dep_row + stencil_row)
        base_index = pair_row * PAIRLEN + row_start
        lon_weights = lagrange(lon_frac[stencil_row])
        for offset in range(4):
            point = base_index + jnp.remainder(dep_lon[stencil_row] + (offset - 1), row_length)
            indices.append(point.reshape(-1).astype(jnp.int32))
            factors.append((lat_weights[stencil_row] * lon_weights[offset]).reshape(-1))
    results = []
    for field_index in range(FIELDS):
        flattened = grid[field_index].reshape(LEV, HROWS * PAIRLEN)
        running = jnp.zeros((LEV, HROWS * PAIRLEN), jnp.float32)
        for term_index in range(16):
            running = running + jnp.take(flattened, indices[term_index], axis=1).astype(jnp.float32) * factors[term_index]
        results.append(running.astype(jnp.bfloat16).reshape(LEV, HROWS, PAIRLEN))
    interpolated = jnp.stack(results)

    spec_in = interpolated[:2].reshape(2 * LEV, HROWS, PAIRLEN)
    by_pair = jnp.moveaxis(spec_in, 1, 0)

    def transform_one(operands):
        return fourier_pair(operands[0], operands[1], wave_slot)

    fourier = lax.map(transform_one, (jnp.arange(HROWS, dtype=jnp.int32), by_pair))
    fourier = jnp.transpose(fourier, (1, 2, 0, 3, 4)).reshape(4 * LEV, HROWS, 2, HROWS)
    northern = fourier[:, :HROWS // 2].astype(jnp.float32)
    southern = fourier[:, HROWS // 2:][:, ::-1].astype(jnp.float32)
    sym = (northern + southern).astype(jnp.bfloat16).reshape(4 * LEV, HROWS, HROWS)
    anti = (northern - southern).astype(jnp.bfloat16).reshape(4 * LEV, HROWS, HROWS)
    sym_slots = jnp.moveaxis(sym, 2, 0)
    anti_slots = jnp.moveaxis(anti, 2, 0)

    def per_slot(operands):
        sym_part, anti_part, table_part, wave = operands
        even = jnp.dot(sym_part, table_part[0].T, preferred_element_type=jnp.float32)
        odd = jnp.dot(anti_part, table_part[1].T, preferred_element_type=jnp.float32)
        merged = jnp.stack([even, odd], axis=2).reshape(sym_part.shape[0], HROWS)
        keeping = jnp.arange(HROWS, dtype=jnp.int32) < HROWS - wave
        return jnp.where(keeping[None, :], merged, 0.0)

    spectral = lax.map(per_slot, (sym_slots, anti_slots, legendre, wave_slot))
    spectral = jnp.transpose(spectral, (1, 0, 2))
    return interpolated, spectral
```

```python
import functools

import jax
import jax.numpy as jnp
from jax import lax
from jax.experimental import pallas as pl
from jax.experimental.pallas import tpu as pltpu
from jax.sharding import PartitionSpec as P

LANES = 128
WIN = 256
ETILES = 24
EW = ETILES * LANES
MARGIN = 60


def row_place(global_row, half_rows):
    northern = global_row < half_rows
    number = jnp.where(northern, global_row + 1, 2 * half_rows - global_row)
    second = number > half_rows // 2
    inner = jnp.where(second, number - half_rows // 2 - 1, half_rows // 2 - number)
    pair_row = jnp.where(northern, inner, half_rows - 1 - inner)
    return pair_row, second, 16 + 4 * number


def cubic(t):
    return (
        -t * (t - 1.0) * (t - 2.0) * (1.0 / 6.0),
        (t + 1.0) * (t - 1.0) * (t - 2.0) * 0.5,
        -(t + 1.0) * t * (t - 2.0) * 0.5,
        (t + 1.0) * t * (t - 1.0) * (1.0 / 6.0),
    )


def interp_kernel(half_rows, pair_length, first_ref, before_ref, own_ref, after_ref,
                  row_ref, lon_ref, lonf_ref, latf_ref, out_ref,
                  rows_s, ext_s, lon_s, wgt_s, row_p, lon_p, lonf_p, latf_p):
    pairs = own_ref.shape[0]
    fields = own_ref.shape[1]
    near = pairs + 4
    tiles = pl.cdiv(pair_length, LANES)
    first = first_ref[0]

    rows_s[...] = jnp.zeros_like(rows_s)
    for j in range(near):
        src = before_ref[j] if j < 2 else (own_ref[j - 2] if j < 2 + pairs else after_ref[j - 2 - pairs])
        rows_s[j, :, pl.ds(LANES, pair_length)] = src

    row_p[...] = jnp.zeros_like(row_p)
    lon_p[...] = jnp.zeros_like(lon_p)
    lonf_p[...] = jnp.zeros_like(lonf_p)
    latf_p[...] = jnp.zeros_like(latf_p)
    row_p[pl.ds(0, pairs), pl.ds(0, pair_length)] = row_ref[...]
    latf_p[pl.ds(0, pairs), pl.ds(0, pair_length)] = latf_ref[...]
    for r in range(4):
        lon_p[r, pl.ds(0, pairs), pl.ds(0, pair_length)] = lon_ref[r]
        lonf_p[r, pl.ds(0, pairs), pl.ds(0, pair_length)] = lonf_ref[r]

    lane = lax.broadcasted_iota(jnp.int32, (fields, LANES), 1)

    def half_lengths(pair):
        inner = jnp.where(pair < half_rows // 2, pair, half_rows - 1 - pair)
        return 16 + 4 * (half_rows // 2 - inner), 16 + 4 * (half_rows // 2 + 1 + inner)

    def unaligned(j, lanes_at):
        tile = pl.multiple_of((lanes_at >> 7) * LANES, LANES)
        two = rows_s[j, :, pl.ds(tile, 2 * LANES)].astype(jnp.float32)
        shift = (2 * LANES - (lanes_at & 127)) & 255
        return pltpu.roll(two, shift, 1)[:, :LANES]

    for half in range(2):
        @pl.loop(0, ETILES)
        def _(tile):
            k0 = (tile - 1) * LANES
            for j in range(near):
                len0, len1 = half_lengths(first + j - 2)
                start = len0 if half else 0
                length = len1 if half else len0
                here = start + k0 + jnp.where(tile == 0, length, 0) + LANES
                over = jnp.maximum(start + k0 - length + LANES, 0)
                here = jnp.clip(here, 0, EW - 2 * LANES)
                over = jnp.clip(over, 0, EW - 2 * LANES)
                a = unaligned(j, here)
                b = unaligned(j, over)
                e = jnp.where(lane + k0 >= length, b, a)
                ext_s[2 * j + half, :, pl.ds(pl.multiple_of(tile * LANES, LANES), LANES)] = e.astype(jnp.bfloat16)

    sub8 = lax.broadcasted_iota(jnp.int32, (8, LANES), 0)
    lane8 = lax.broadcasted_iota(jnp.int32, (8, LANES), 1)

    def weigh(tile, fits):
        at = pl.ds(pl.multiple_of(tile * LANES, LANES), LANES)
        col = tile * LANES + lane8
        pair = first + sub8
        northern = pair < half_rows // 2
        len0, len1 = half_lengths(pair)
        second = col >= len0
        inner = jnp.where(northern, pair, half_rows - 1 - pair)
        number = jnp.where(second, half_rows // 2 + 1 + inner, half_rows // 2 - inner)
        g = jnp.where(northern, number - 1, 2 * half_rows - number)
        base = jnp.clip(g - 2, 0, 2 * half_rows - 4)
        later = (row_p[:, at] - base) > 0
        k0 = jnp.where(second, jnp.maximum(tile * LANES - len0, 0), tile * LANES)
        base_k = k0 - MARGIN
        inside = (col < pair_length) & (sub8 < pairs)
        latw = cubic(latf_p[:, at])
        lons = [lon_p[r, :, at] for r in range(4)]
        lonfs = [lonf_p[r, :, at] for r in range(4)]
        zero = jnp.zeros((8, LANES), jnp.float32)
        for d in range(5):
            hi, lo = min(d, 3), max(d - 1, 0)
            lon = jnp.where(later, lons[lo], lons[hi])
            frac = jnp.where(later, lonfs[lo], lonfs[hi])
            lat = jnp.where(later, latw[lo] if d >= 1 else zero, latw[hi] if d <= 3 else zero)
            _, _, length = row_place(jnp.minimum(base + d, 2 * half_rows - 1), half_rows)
            rel = lon - 1 - base_k
            rel = jnp.where(rel < 0, rel + length, jnp.where(rel >= length, rel - length, rel))
            rel = jnp.where(length <= WIN - 4, lon, rel)
            bad = inside & (lat != 0.0) & ((rel < 0) | (rel > WIN - 4))
            fits = jnp.maximum(fits, bad.astype(jnp.int32))
            lon_s[d, :, at] = lon
            ws = cubic(frac)
            for o in range(4):
                wgt_s[d * 4 + o, :, at] = lat * ws[o]
        return fits

    worst = lax.fori_loop(0, tiles, weigh, jnp.zeros((8, LANES), jnp.int32))
    local = jnp.max(worst) == 0

    sub16 = lax.broadcasted_iota(jnp.int32, (16, LANES), 0)
    zero16 = jnp.zeros((16, LANES), jnp.bfloat16)

    def spread(d, q, at, place, fold):
        w = [jnp.broadcast_to(wgt_s[d * 4 + o, pl.ds(q, 1), at], (16, LANES)) for o in range(4)]
        off = (sub16 - place) & 15
        v = jnp.where(off == 0, w[0], jnp.where(off == 1, w[1], jnp.where(off == 2, w[2], jnp.where(off == 3, w[3], 0.0))))
        block = (place + 15 - sub16) >> 4
        if fold:
            block = jnp.where(block >= 16, block - 16, block)
        v = v.astype(jnp.bfloat16)
        block = block.astype(jnp.float32).astype(jnp.bfloat16)
        return [jnp.where(block == jnp.bfloat16(a), v, zero16) for a in range(WIN // 16)]

    def unit_scalars(q, u):
        pair = first + q
        northern = pair < half_rows // 2
        len0, _ = half_lengths(pair)
        straddle = len0 >> 7
        half = (u > straddle).astype(jnp.int32)
        tile = u - half
        inner = jnp.where(northern, pair, half_rows - 1 - pair)
        number = jnp.where(half == 1, half_rows // 2 + 1 + inner, half_rows // 2 - inner)
        g = jnp.where(northern, number - 1, 2 * half_rows - number)
        base = jnp.clip(g - 2, 0, 2 * half_rows - 4)
        k0 = jnp.where(half == 1, jnp.maximum(tile * LANES - len0, 0), tile * LANES)
        return len0, straddle, half, tile, base, k0

    def place_of(base, d):
        pair_row, second, length = row_place(jnp.minimum(base + d, 2 * half_rows - 1), half_rows)
        return 2 * jnp.clip(pair_row - first + 2, 0, near - 1) + second.astype(jnp.int32), length

    lane1 = lax.broadcasted_iota(jnp.int32, (1, LANES), 1)

    def finish(q, u, straddle, tile, total, carry):
        total = total + jnp.where(u == straddle + 1, carry, 0.0)
        out_ref[q, :, pl.ds(pl.multiple_of(tile * LANES, LANES), LANES)] = total.astype(jnp.bfloat16)
        return total

    @pl.when(local)
    def _():
        def unit(q, u, carry):
            len0, straddle, half, tile, base, k0 = unit_scalars(q, u)
            at = pl.ds(pl.multiple_of(tile * LANES, LANES), LANES)
            col = tile * LANES + lane1
            mine = ((col >= len0).astype(jnp.int32) == half) & (col < pair_length)
            rows, weights = [], []
            for d in range(5):
                where_row, length = place_of(base, d)
                short = length <= WIN - 4
                base_k = jnp.where(short, -1, k0 - MARGIN)
                begin = base_k + LANES
                s = begin & 127
                first_tile = pl.multiple_of((begin >> 7) * LANES, LANES)
                rel = lon_s[d, pl.ds(q, 1), at] - 1 - base_k
                rel = jnp.where(rel < 0, rel + length, jnp.where(rel >= length, rel - length, rel))
                place = jnp.where(mine, s + rel, -4096)
                weights += spread(d, q, at, jnp.broadcast_to(place, (16, LANES)), True)
                three = ext_s[where_row, :, pl.ds(first_tile, 3 * LANES)]
                rows += [jnp.where(lane >= s, three[:, :LANES], three[:, 2 * LANES:]), three[:, LANES:2 * LANES]]
            total = jnp.dot(jnp.concatenate(rows, axis=1), jnp.concatenate(weights, axis=0),
                            preferred_element_type=jnp.float32)
            return finish(q, u, straddle, tile, total, carry)

        lax.fori_loop(0, tiles + 1, lambda u, carry: tuple(unit(q, u, carry[q]) for q in range(pairs)),
                      (jnp.zeros((fields, LANES), jnp.float32),) * pairs)

    @pl.when(jnp.logical_not(local))
    def _():
        def unit(q, u, carry):
            len0, straddle, half, tile, base, _ = unit_scalars(q, u)
            at = pl.ds(pl.multiple_of(tile * LANES, LANES), LANES)
            col = tile * LANES + lane1
            mine = ((col >= len0).astype(jnp.int32) == half) & (col < pair_length)

            def window(w, total):
                rows, weights = [], []
                for d in range(5):
                    where_row, length = place_of(base, d)
                    place = lon_s[d, pl.ds(q, 1), at] - 1 + LANES - w * WIN
                    place = jnp.where(mine, place, -4096)
                    weights += spread(d, q, at, jnp.broadcast_to(place, (16, LANES)), False)
                    rows.append(ext_s[where_row, :, pl.ds(pl.multiple_of(w * WIN, WIN), WIN)])
                return total + jnp.dot(jnp.concatenate(rows, axis=1), jnp.concatenate(weights, axis=0),
                                       preferred_element_type=jnp.float32)

            total = lax.fori_loop(0, EW // WIN, window, jnp.zeros((fields, LANES), jnp.float32))
            return finish(q, u, straddle, tile, total, carry)

        lax.fori_loop(0, tiles + 1, lambda u, carry: tuple(unit(q, u, carry[q]) for q in range(pairs)),
                      (jnp.zeros((fields, LANES), jnp.float32),) * pairs)


def interpolate(first, before, own, after, dep_row, dep_lon, lon_frac, lat_frac, half_rows):
    pairs, fields, pair_length = own.shape
    tiles = pl.cdiv(pair_length, LANES)
    padded = tiles * LANES
    near = pairs + 4
    vm = pl.BlockSpec(memory_space=pltpu.VMEM)
    return pl.pallas_call(
        functools.partial(interp_kernel, half_rows, pair_length),
        out_shape=jax.ShapeDtypeStruct((pairs, fields, padded), jnp.bfloat16),
        in_specs=[pl.BlockSpec(memory_space=pltpu.SMEM)] + [vm] * 7,
        out_specs=vm,
        scratch_shapes=[
            pltpu.VMEM((near, fields, EW), jnp.bfloat16),
            pltpu.VMEM((2 * near, fields, EW), jnp.bfloat16),
            pltpu.VMEM((5, 8, padded), jnp.int32),
            pltpu.VMEM((20, 8, padded), jnp.float32),
            pltpu.VMEM((8, padded), jnp.int32),
            pltpu.VMEM((4, 8, padded), jnp.int32),
            pltpu.VMEM((4, 8, padded), jnp.float32),
            pltpu.VMEM((8, padded), jnp.float32),
        ],
        name="interp",
    )(first, before, own, after, dep_row, dep_lon, lon_frac, lat_frac)


def cos_sin_turns(prod, length, inverse):
    turns = jnp.floor(prod * inverse + 0.5)
    t = (prod - turns * length) * inverse
    x = t * t
    c = jnp.full_like(x, COS[-1])
    for a in COS[-2::-1]:
        c = c * x + a
    s = jnp.full_like(x, SIN[-1])
    for a in SIN[-2::-1]:
        s = s * x + a
    return c, s * t


COS = (1, -19.7392087, 64.9393842, -85.4565372, 60.2407014, -26.3960673, 7.77462739, -1.42354417)
SIN = (6.28318531, -41.3417022, 81.6052456, -76.7057546, 42.0572162, -15.0833301, 3.7717259, -0.609657301)


def fourier_kernel(half_rows, pair_length, first_ref, y_ref, order_ref, out_ref, table_s, sums_s, four_s, mix_s, send_s):
    pairs = y_ref.shape[0]
    tiles = pl.cdiv(pair_length, LANES)
    first = first_ref[0]
    north = first < half_rows // 2
    parts = 8

    def one(i, _):
        q = i >> 1
        half = i & 1
        pair = first + q
        inner = jnp.where(north, pair, half_rows - 1 - pair)
        len0 = 16 + 4 * (half_rows // 2 - inner)
        start = jnp.where(half == 1, len0, 0)
        whole = jnp.where(half == 1, 16 + 4 * (half_rows // 2 + 1 + inner), len0)
        def waves(rows):
            return lax.broadcasted_iota(jnp.int32, (rows, half_rows), 1)
        def line(rows):
            return lax.broadcasted_iota(jnp.int32, (rows, half_rows), 0)
        length = jnp.full((1, half_rows), whole, jnp.int32).astype(jnp.float32)
        inverse = 1.0 / length
        fine_c, fine_s = cos_sin_turns((waves(16) * line(16)).astype(jnp.float32), length, inverse)
        step_c, step_s = cos_sin_turns((waves(8) * (16 * line(8))).astype(jnp.float32), length, inverse)
        for a in range(8):
            ca, sa = step_c[a:a + 1], step_s[a:a + 1]
            table_s[pl.ds(16 * a, 16), pl.ds(0, half_rows)] = (ca * fine_c - sa * fine_s).astype(jnp.bfloat16)
            table_s[pl.ds(16 * a, 16), pl.ds(half_rows, half_rows)] = (sa * fine_c + ca * fine_s).astype(jnp.bfloat16)
        lane = lax.broadcasted_iota(jnp.int32, (parts, LANES), 1)
        blocks = []
        for t in range(tiles):
            col = lane + t * LANES
            mine = (col >= start) & (col < start + whole)
            blocks.append(jnp.where(mine, y_ref[q, :, pl.ds(t * LANES, LANES)].astype(jnp.float32)[:parts], 0.0))
        stacked = jnp.concatenate(blocks, axis=0).astype(jnp.bfloat16)
        sums_s[...] = jnp.dot(stacked, table_s[...], preferred_element_type=jnp.float32)
        tile_c, tile_s = cos_sin_turns((waves(24) * (LANES * line(24) - start)).astype(jnp.float32), length, inverse)
        real = jnp.zeros((parts, half_rows), jnp.float32)
        imag = jnp.zeros((parts, half_rows), jnp.float32)
        for t in range(tiles):
            c = sums_s[pl.ds(parts * t, parts), pl.ds(0, half_rows)]
            s = sums_s[pl.ds(parts * t, parts), pl.ds(half_rows, half_rows)]
            tc, ts = tile_c[t:t + 1], tile_s[t:t + 1]
            real = real + (tc * c - ts * s)
            imag = imag - (ts * c + tc * s)
        keep = jnp.where(2 * waves(1) < whole, inverse, 0.0)
        place = 2 * jnp.where(north, q, pairs - 1 - q) + half
        four_s[pl.ds(pl.multiple_of(place * 16, 16), 16), :] = jnp.concatenate([real * keep, imag * keep], axis=0).astype(jnp.bfloat16)
        return 0

    lax.fori_loop(0, 2 * pairs, one, 0)

    hot = (lax.broadcasted_iota(jnp.int32, (half_rows, half_rows), 0) == order_ref[...]).astype(jnp.float32).astype(jnp.bfloat16)
    moved = jnp.dot(four_s[...], hot, preferred_element_type=jnp.float32)
    slots = half_rows // LANES
    mix_s[...] = jnp.zeros_like(mix_s)
    send_s[...] = jnp.zeros_like(send_s)
    for r in range(2 * pairs):
        for s in range(slots):
            mix_s[pl.ds(s, 16, stride=8), :] = moved[16 * r:16 * r + 16, s * LANES:(s + 1) * LANES]
        send_s[pl.ds(r, LANES, stride=16), :] = mix_s[...].T
    out_ref[...] = send_s[...].astype(jnp.bfloat16).reshape(out_ref.shape)


def fourier(first, y, order, half_rows, pair_length):
    pairs = y.shape[0]
    tiles = pl.cdiv(pair_length, LANES)
    vm = pl.BlockSpec(memory_space=pltpu.VMEM)
    return pl.pallas_call(
        functools.partial(fourier_kernel, half_rows, pair_length),
        out_shape=jax.ShapeDtypeStruct((LANES, 16, LANES), jnp.bfloat16),
        in_specs=[pl.BlockSpec(memory_space=pltpu.SMEM), vm, vm],
        out_specs=vm,
        scratch_shapes=[
            pltpu.VMEM((LANES, 2 * half_rows), jnp.bfloat16),
            pltpu.VMEM((8 * tiles, 2 * half_rows), jnp.float32),
            pltpu.VMEM((32 * pairs, half_rows), jnp.bfloat16),
            pltpu.VMEM((LANES, LANES), jnp.float32),
            pltpu.VMEM((16 * LANES, LANES), jnp.float32),
        ],
        name="fourier",
    )(first, y, order)


def spectral_kernel(half_rows, waves_ref, got_ref, legendre_ref, out_ref, sym_f, anti_f, sym_b, anti_b, acc_s, z_s):
    s = pl.program_id(0)
    slots = pl.num_programs(0)
    devices = got_ref.shape[0]
    rows = 2 * half_rows // devices

    @pl.when(s == 0)
    def _():
        for d in range(devices // 2):
            n = got_ref[d].astype(jnp.float32)
            o = got_ref[devices - 1 - d].astype(jnp.float32)
            sym_f[pl.ds(rows * d, 16), :] = n + o
            anti_f[pl.ds(rows * d, 16), :] = n - o
        sym_b[...] = sym_f[pl.ds(0, half_rows), :].astype(jnp.bfloat16)
        anti_b[...] = anti_f[pl.ds(0, half_rows), :].astype(jnp.bfloat16)
        acc_s[...] = jnp.zeros_like(acc_s)

    lane = lax.broadcasted_iota(jnp.int32, (half_rows, LANES), 1)
    mine = (lane & 7) == s
    for par, values in ((0, sym_b), (1, anti_b)):
        chosen = jnp.where(mine, values[...].astype(jnp.float32), 0.0).astype(jnp.bfloat16)
        acc_s[par] = acc_s[par] + jnp.dot(legendre_ref[0, par], chosen, preferred_element_type=jnp.float32)

    @pl.when(s == slots - 1)
    def _():
        for par in range(2):
            z_s[pl.ds(par, half_rows // 2, stride=2), :] = acc_s[par]
        z = z_s[...].T.reshape(16, 8, half_rows)
        sub = lax.broadcasted_iota(jnp.int32, (8, half_rows), 0)
        j = lax.broadcasted_iota(jnp.int32, (8, half_rows), 1)
        limit = jnp.zeros((8, half_rows), jnp.int32)
        for i in range(5):
            limit = jnp.where(sub == i, half_rows - waves_ref[i], limit)
        z = jnp.where((j < limit)[None], z, 0.0)
        out_ref[...] = z[:, :out_ref.shape[1], :]


def spectral(waves, got, legendre, half_rows):
    slots = legendre.shape[0]
    return pl.pallas_call(
        functools.partial(spectral_kernel, half_rows),
        grid=(slots,),
        out_shape=jax.ShapeDtypeStruct((16, slots, half_rows), jnp.float32),
        in_specs=[
            pl.BlockSpec(memory_space=pltpu.SMEM),
            pl.BlockSpec(got.shape, lambda s: (0, 0, 0)),
            pl.BlockSpec((1,) + legendre.shape[1:], lambda s: (s, 0, 0, 0)),
        ],
        out_specs=pl.BlockSpec((16, slots, half_rows), lambda s: (0, 0, 0)),
        scratch_shapes=[
            pltpu.VMEM((half_rows + 16, LANES), jnp.float32),
            pltpu.VMEM((half_rows + 16, LANES), jnp.float32),
            pltpu.VMEM((half_rows, LANES), jnp.bfloat16),
            pltpu.VMEM((half_rows, LANES), jnp.bfloat16),
            pltpu.VMEM((2, half_rows // 2, LANES), jnp.float32),
            pltpu.VMEM((half_rows, LANES), jnp.float32),
        ],
        name="spectral",
    )(waves, got, legendre)


def exchange_kernel(across, send_ref, got_ref, send_sem, recv_sem, own_sem):
    devices = send_ref.shape[0]
    me = lax.axis_index("aa") * across + lax.axis_index("ba")

    def partner(i):
        other = lax.rem(me + i, devices)
        return other, (other // across, lax.rem(other, across))

    barrier = pltpu.get_barrier_semaphore()

    def greet(i, _):
        pl.semaphore_signal(barrier, inc=1, device_id=partner(i)[1], device_id_type=pl.DeviceIdType.MESH)
        return 0

    lax.fori_loop(1, devices, greet, 0)
    pl.semaphore_wait(barrier, devices - 1)

    def post(i, _):
        other, where = partner(i)
        pltpu.make_async_remote_copy(
            src_ref=send_ref.at[other], dst_ref=got_ref.at[me], send_sem=send_sem, recv_sem=recv_sem,
            device_id=where, device_id_type=pl.DeviceIdType.MESH).start()
        return 0

    lax.fori_loop(1, devices, post, 0)
    own = pltpu.make_async_copy(send_ref.at[me], got_ref.at[me], own_sem)
    own.start()
    rest = pl.ds(0, devices - 1)
    every = pltpu.make_async_remote_copy(
        src_ref=send_ref.at[rest], dst_ref=got_ref.at[rest], send_sem=send_sem, recv_sem=recv_sem,
        device_id=partner(1)[1], device_id_type=pl.DeviceIdType.MESH)
    every.wait_send()
    every.wait_recv()
    own.wait()


def exchange(send, across):
    anywhere = pl.BlockSpec(memory_space=pl.ANY)
    return pl.pallas_call(
        functools.partial(exchange_kernel, across),
        out_shape=jax.ShapeDtypeStruct(send.shape, send.dtype),
        in_specs=[anywhere],
        out_specs=anywhere,
        scratch_shapes=[pltpu.SemaphoreType.DMA, pltpu.SemaphoreType.DMA, pltpu.SemaphoreType.DMA],
        compiler_params=pltpu.CompilerParams(collective_id=0, has_side_effects=True),
        name="exchange",
    )(send)


def on_device(grid, dep_row, dep_lon, lon_frac, lat_frac, wave_slot, legendre):
    half_rows = wave_slot.shape[0]
    fields, levels, pairs, pair_length = grid.shape
    slots = legendre.shape[0]
    axes = ("aa", "ba")
    devices = lax.axis_size(axes)
    device = lax.axis_index(axes)
    first = (device * pairs).astype(jnp.int32).reshape(1)
    own = jnp.transpose(grid.reshape(fields * levels, pairs, pair_length), (1, 0, 2))
    up = [(i, i + 1) for i in range(devices - 1)]
    down = [(j, i) for i, j in up]
    before = lax.ppermute(own[pairs - 2:], axes, up)
    after = lax.ppermute(own[:2], axes, down)
    order = jnp.transpose(wave_slot.reshape(devices, slots)).reshape(1, half_rows)
    waves = lax.dynamic_slice_in_dim(wave_slot, device * slots, slots)
    y = interpolate(first, before, own, after, dep_row, dep_lon, lon_frac, lat_frac, half_rows)
    send = fourier(first, y, order, half_rows, pair_length)
    got = exchange(send, lax.axis_size("ba"))
    result = spectral(waves, got, legendre, half_rows)
    interpolated = jnp.transpose(y[:, :, :pair_length], (1, 0, 2)).reshape(grid.shape)
    return (interpolated, result)


def solution(mesh):
    return jax.shard_map(
        on_device,
        mesh=mesh,
        in_specs=(
            P(None, None, ("aa", "ba"), None),
            P(("aa", "ba"), None),
            P(None, ("aa", "ba"), None),
            P(None, ("aa", "ba"), None),
            P(("aa", "ba"), None),
            P(),
            P(("aa", "ba"), None, None, None),
        ),
        out_specs=(P(None, None, ("aa", "ba"), None), P(None, ("aa", "ba"), None)),
        check_vma=False,
    )
```

```python
import functools

import jax
import jax.numpy as jnp
from jax import lax
from jax.experimental import pallas as pl
from jax.experimental.pallas import tpu as pltpu
from jax.sharding import PartitionSpec as P

LANES = 128
WIN = 256
ETILES = 24
EW = ETILES * LANES
MARGIN = 60
ROWS = 11
NOWHERE = 192.0


def row_place(global_row, half_rows):
    northern = global_row < half_rows
    number = jnp.where(northern, global_row + 1, 2 * half_rows - global_row)
    second = number > half_rows // 2
    inner = jnp.where(second, number - half_rows // 2 - 1, half_rows // 2 - number)
    begin = jnp.where(second, 16 + 4 * (half_rows // 2 - inner), 0)
    return jnp.where(northern, inner, half_rows - 1 - inner), begin, 16 + 4 * number


def cubic(t):
    return (
        -t * (t - 1.0) * (t - 2.0) * (1.0 / 6.0),
        (t + 1.0) * (t - 1.0) * (t - 2.0) * 0.5,
        -(t + 1.0) * t * (t - 2.0) * 0.5,
        (t + 1.0) * t * (t - 1.0) * (1.0 / 6.0),
    )


def interp_kernel(half_rows, pair_length, first_ref, before_ref, own_ref, after_ref,
                  row_ref, lon_ref, lonf_ref, latf_ref, out_ref,
                  place_t, ext_s, plan_s, row_p, lon_p, lonf_p, latf_p):
    pairs = own_ref.shape[0]
    fields = own_ref.shape[1]
    near = pairs + 4
    tiles = pl.cdiv(pair_length, LANES)
    first = first_ref[0]

    ext_s[:, :, pl.ds(0, LANES)] = jnp.zeros((2 * near, fields, LANES), jnp.bfloat16)
    ext_s[:, :, pl.ds(tiles * LANES, EW - tiles * LANES)] = jnp.zeros((2 * near, fields, EW - tiles * LANES), jnp.bfloat16)
    for j in range(near):
        src = before_ref[j] if j < 2 else (own_ref[j - 2] if j < 2 + pairs else after_ref[j - 2 - pairs])
        ext_s[2 * j, :, pl.ds(LANES, pair_length)] = src
        ext_s[2 * j + 1, :, pl.ds(LANES, pair_length)] = src

    row_p[...] = jnp.zeros_like(row_p)
    lon_p[...] = jnp.zeros_like(lon_p)
    lonf_p[...] = jnp.zeros_like(lonf_p)
    latf_p[...] = jnp.zeros_like(latf_p)
    row_p[pl.ds(0, pairs), pl.ds(0, pair_length)] = row_ref[...]
    latf_p[pl.ds(0, pairs), pl.ds(0, pair_length)] = latf_ref[...]
    for r in range(4):
        lon_p[r, pl.ds(0, pairs), pl.ds(0, pair_length)] = lon_ref[r]
        lonf_p[r, pl.ds(0, pairs), pl.ds(0, pair_length)] = lonf_ref[r]

    lane = lax.broadcasted_iota(jnp.int32, (fields, LANES), 1)

    def half_lengths(pair):
        inner = jnp.where(pair < half_rows // 2, pair, half_rows - 1 - pair)
        return 16 + 4 * (half_rows // 2 - inner), 16 + 4 * (half_rows // 2 + 1 + inner)

    def wrap(copy, tile, shift, low, edge):
        at = pl.ds(pl.multiple_of(tile * LANES, LANES), LANES)
        begin = tile * LANES + shift
        two = ext_s[copy, :, pl.ds(pl.multiple_of((begin >> 7) * LANES, LANES), 2 * LANES)].astype(jnp.float32)
        moved = pltpu.roll(two, (2 * LANES - (begin & 127)) & 255, 1)[:, :LANES]
        spot = lane + tile * LANES
        beyond = spot < edge if low else spot >= edge
        return copy, at, jnp.where(beyond, moved, ext_s[copy, :, at].astype(jnp.float32)).astype(jnp.bfloat16)

    for j in range(near):
        len0, len1 = half_lengths(first + j - 2)
        wraps = []
        for half in range(2):
            start, length = (len0, len1) if half else (0, len0)
            for i in range(1 + half):
                wraps.append(wrap(2 * j + half, ((start >> 7) if half else 0) + i, length, True, start + LANES))
            for i in range(3):
                wraps.append(wrap(2 * j + half, ((start + length) >> 7) + 1 + i, -length, False, start + length + LANES))
        for copy, at, tile in wraps:
            ext_s[copy, :, at] = tile

    sub8 = lax.broadcasted_iota(jnp.int32, (8, LANES), 0)
    lane8 = lax.broadcasted_iota(jnp.int32, (8, LANES), 1)

    def weigh(tile, fits):
        at = pl.ds(pl.multiple_of(tile * LANES, LANES), LANES)
        col = tile * LANES + lane8
        pair = first + sub8
        northern = pair < half_rows // 2
        len0, len1 = half_lengths(pair)
        second = col >= len0
        inner = jnp.where(northern, pair, half_rows - 1 - pair)
        number = jnp.where(second, half_rows // 2 + 1 + inner, half_rows // 2 - inner)
        g = jnp.where(northern, number - 1, 2 * half_rows - number)
        base = jnp.clip(g - 2, 0, 2 * half_rows - 4)
        later = (row_p[:, at] - base) > 0
        k0 = jnp.where(second, jnp.maximum(tile * LANES - len0, 0), tile * LANES)
        base_k = k0 - MARGIN
        inside = (col < pair_length) & (sub8 < pairs)
        latw = cubic(latf_p[:, at])
        lons = [lon_p[r, :, at] for r in range(4)]
        lonfs = [lonf_p[r, :, at] for r in range(4)]
        zero = jnp.zeros((8, LANES), jnp.float32)
        for d in range(5):
            hi, lo = min(d, 3), max(d - 1, 0)
            lon = jnp.where(later, lons[lo], lons[hi])
            frac = jnp.where(later, lonfs[lo], lonfs[hi])
            lat = jnp.where(later, latw[lo] if d >= 1 else zero, latw[hi] if d <= 3 else zero)
            _, begin, length = row_place(jnp.minimum(base + d, 2 * half_rows - 1), half_rows)
            rel = lon - 1 - base_k
            rel = jnp.where(rel < 0, rel + length, jnp.where(rel >= length, rel - length, rel))
            short = length <= WIN - 4
            rel = jnp.where(short, lon, rel)
            bad = inside & (lat != 0.0) & ((rel < 0) | (rel > WIN - 4))
            fits = jnp.maximum(fits, bad.astype(jnp.int32))
            place = ((begin + jnp.where(short, -1, base_k) + LANES) & 127) + rel
            block = (place >> 4) & 15
            lat = jnp.where(inside, lat, 0.0)
            ws = cubic(frac)
            for o in range(4):
                plan_s[d * ROWS + o, :, at] = lat * ws[o]
                plan_s[d * ROWS + 4 + o, :, at] = ((place + o) & 15).astype(jnp.float32)
            plan_s[d * ROWS + 8, :, at] = block.astype(jnp.float32)
            plan_s[d * ROWS + 9, :, at] = ((block + 1) & 15).astype(jnp.float32)
            plan_s[d * ROWS + 10, :, at] = (lon + begin).astype(jnp.float32)
        return fits

    worst = lax.fori_loop(0, tiles, weigh, jnp.zeros((8, LANES), jnp.int32))
    local = jnp.max(worst) == 0

    node = lax.broadcasted_iota(jnp.int32, (16, LANES), 0).astype(jnp.float32).astype(jnp.bfloat16)
    zero16 = jnp.zeros((16, LANES), jnp.bfloat16)

    def spread(mine, weight, rest, block, after):
        v = zero16
        for o in (3, 2, 1, 0):
            v = jnp.where(node == rest[o], weight[o], v)
        block = jnp.where(mine, jnp.where(node < rest[0], after, block), jnp.bfloat16(NOWHERE))
        return [jnp.where(block == jnp.bfloat16(a), v, zero16) for a in range(WIN // 16)]

    def plan(d, i, q, at):
        return jnp.broadcast_to(plan_s[d * ROWS + i, pl.ds(q, 1), at], (16, LANES))

    def packed(x):
        return x.astype(jnp.bfloat16)

    for q in range(pairs):
        pair = first + q
        northern = pair < half_rows // 2
        inner = jnp.where(northern, pair, half_rows - 1 - pair)
        for half in range(2):
            number = half_rows // 2 + 1 + inner if half else half_rows // 2 - inner
            g = jnp.where(northern, number - 1, 2 * half_rows - number)
            base = jnp.clip(g - 2, 0, 2 * half_rows - 4)
            for d in range(5):
                pair_row, begin, length = row_place(jnp.minimum(base + d, 2 * half_rows - 1), half_rows)
                short = length <= WIN - 4
                copy = 2 * jnp.clip(pair_row - first + 2, 0, near - 1) + (begin > 0).astype(jnp.int32)
                at = 3 * ((2 * q + half) * 5 + d)
                place_t[at] = copy
                place_t[at + 1] = begin + LANES + jnp.where(short, -1, -MARGIN)
                place_t[at + 2] = jnp.where(short, 0, 1)

    def unit_scalars(q, u):
        len0, _ = half_lengths(first + q)
        straddle = len0 >> 7
        half = (u > straddle).astype(jnp.int32)
        tile = u - half
        k0 = jnp.where(half == 1, jnp.maximum(tile * LANES - len0, 0), tile * LANES)
        return len0, straddle, half, tile, 15 * (2 * q + half), k0

    lane16 = lax.broadcasted_iota(jnp.int32, (16, LANES), 1).astype(jnp.float32).astype(jnp.bfloat16)

    def own_half(half, tile, len0):
        edge = jnp.clip(len0 - tile * LANES, 0, LANES)
        low = jnp.where(half == 1, edge, 0).astype(jnp.float32)
        high = jnp.where(half == 1, LANES, edge).astype(jnp.float32)
        spread_low = jnp.full((16, LANES), low, jnp.float32).astype(jnp.bfloat16)
        spread_high = jnp.full((16, LANES), high, jnp.float32).astype(jnp.bfloat16)
        return (lane16 >= spread_low) & (lane16 < spread_high)

    def finish(q, u, straddle, tile, total, carry):
        total = total + jnp.where(u == straddle + 1, carry, 0.0)
        out_ref[q, :, pl.ds(pl.multiple_of(tile * LANES, LANES), LANES)] = total.astype(jnp.bfloat16)
        return total

    @pl.when(local)
    def _():
        def unit(q, u, carry):
            len0, straddle, half, tile, base, k0 = unit_scalars(q, u)
            at = pl.ds(pl.multiple_of(tile * LANES, LANES), LANES)
            mine = own_half(half, tile, len0)
            rows, weights = [], []
            for d in range(5):
                where_row = place_t[base + 3 * d]
                begin = place_t[base + 3 * d + 1] + place_t[base + 3 * d + 2] * k0
                s = begin & 127
                first_tile = pl.multiple_of((begin >> 7) * LANES, LANES)
                row = [packed(plan(d, i, q, at)) for i in range(10)]
                weights += spread(mine, row[:4], row[4:8], row[8], row[9])
                three = ext_s[where_row, :, pl.ds(first_tile, 3 * LANES)]
                rows += [jnp.where(lane >= s, three[:, :LANES], three[:, 2 * LANES:]), three[:, LANES:2 * LANES]]
            total = jnp.dot(jnp.concatenate(rows, axis=1), jnp.concatenate(weights, axis=0),
                            preferred_element_type=jnp.float32)
            return finish(q, u, straddle, tile, total, carry)

        lax.fori_loop(0, tiles + 1, lambda u, carry: tuple(unit(q, u, carry[q]) for q in range(pairs)),
                      (jnp.zeros((fields, LANES), jnp.float32),) * pairs)

    @pl.when(jnp.logical_not(local))
    def _():
        def unit(q, u, carry):
            len0, straddle, half, tile, base, _ = unit_scalars(q, u)
            at = pl.ds(pl.multiple_of(tile * LANES, LANES), LANES)
            mine = own_half(half, tile, len0)

            def window(w, total):
                rows, weights = [], []
                for d in range(5):
                    where_row = place_t[base + 3 * d]
                    place = (plan(d, 10, q, at) + (LANES - 1)).astype(jnp.int32) - w * WIN
                    block = jnp.clip(place >> 4, -2, 18)
                    rest = [packed(((place + o) & 15).astype(jnp.float32)) for o in range(4)]
                    weight = [packed(plan(d, o, q, at)) for o in range(4)]
                    weights += spread(mine, weight, rest, packed(block.astype(jnp.float32)), packed((block + 1).astype(jnp.float32)))
                    rows.append(ext_s[where_row, :, pl.ds(pl.multiple_of(w * WIN, WIN), WIN)])
                return total + jnp.dot(jnp.concatenate(rows, axis=1), jnp.concatenate(weights, axis=0),
                                       preferred_element_type=jnp.float32)

            total = lax.fori_loop(0, EW // WIN, window, jnp.zeros((fields, LANES), jnp.float32))
            return finish(q, u, straddle, tile, total, carry)

        lax.fori_loop(0, tiles + 1, lambda u, carry: tuple(unit(q, u, carry[q]) for q in range(pairs)),
                      (jnp.zeros((fields, LANES), jnp.float32),) * pairs)


def interpolate(first, before, own, after, dep_row, dep_lon, lon_frac, lat_frac, half_rows):
    pairs, fields, pair_length = own.shape
    tiles = pl.cdiv(pair_length, LANES)
    padded = tiles * LANES
    near = pairs + 4
    vm = pl.BlockSpec(memory_space=pltpu.VMEM)
    return pl.pallas_call(
        functools.partial(interp_kernel, half_rows, pair_length),
        out_shape=jax.ShapeDtypeStruct((pairs, fields, padded), jnp.bfloat16),
        in_specs=[pl.BlockSpec(memory_space=pltpu.SMEM)] + [vm] * 7,
        out_specs=vm,
        scratch_shapes=[
            pltpu.SMEM((30 * pairs,), jnp.int32),
            pltpu.VMEM((2 * near, fields, EW), jnp.bfloat16),
            pltpu.VMEM((5 * ROWS, 8, padded), jnp.float32),
            pltpu.VMEM((8, padded), jnp.int32),
            pltpu.VMEM((4, 8, padded), jnp.int32),
            pltpu.VMEM((4, 8, padded), jnp.float32),
            pltpu.VMEM((8, padded), jnp.float32),
        ],
        name="interp",
    )(first, before, own, after, dep_row, dep_lon, lon_frac, lat_frac)


COS = (1, -19.7392087, 64.9393842, -85.4565372, 60.2407014, -26.3960673, 7.77462739, -1.42354417)
SIN = (6.28318531, -41.3417022, 81.6052456, -76.7057546, 42.0572162, -15.0833301, 3.7717259, -0.609657301)


def cos_sin_turns(prod, length, inverse):
    turns = jnp.floor(prod * inverse + 0.5)
    t = (prod - turns * length) * inverse
    x = t * t
    c = jnp.full_like(x, COS[-1])
    for a in COS[-2::-1]:
        c = c * x + a
    s = jnp.full_like(x, SIN[-1])
    for a in SIN[-2::-1]:
        s = s * x + a
    return c, s * t


def transform_kernel(sizes, pair_length, y_ref, order_ref, waves_ref, legendre_hbm, out_ref,
                     table_s, sums_s, four_s, mix_s, stage_s, send_s, got_s, plain_s, anti_s, kept_s, keptanti_s, turn_s, legendre_s,
                     legendre_sem, own_sem, send_sem, recv_sem):
    along, across = sizes
    devices = along * across
    pairs = y_ref.shape[0]
    slots = legendre_s.shape[0]
    half_rows = slots * devices
    rows = 2 * pairs
    tiles = pl.cdiv(pair_length, LANES)
    my_a = lax.axis_index("aa")
    my_b = lax.axis_index("ba")
    me = my_a * across + my_b
    first = me * pairs
    north = me < devices // 2
    parts = 8

    weights_in = pltpu.make_async_copy(legendre_hbm, legendre_s, legendre_sem)
    weights_in.start()

    columns = [lax.rem(my_b + i, across) for i in range(across)]

    def partners(act):
        for b in range(1, across):
            act(my_a, columns[b])

        def others(i, _):
            a = lax.rem(my_a + i, along)
            for b in range(across):
                act(a, columns[b])
            return 0

        lax.fori_loop(1, along, others, 0)

    barrier = pltpu.get_barrier_semaphore()
    partners(lambda a, b: pl.semaphore_signal(barrier, inc=1, device_id=(a, b), device_id_type=pl.DeviceIdType.MESH))

    def one(i, _):
        q = i // 2
        half = i - 2 * q
        pair = first + q
        inner = jnp.where(north, pair, half_rows - 1 - pair)
        len0 = 16 + 4 * (half_rows // 2 - inner)
        start = jnp.where(half == 1, len0, 0)
        whole = jnp.where(half == 1, 16 + 4 * (half_rows // 2 + 1 + inner), len0)
        length = jnp.full((1, LANES), whole, jnp.int32).astype(jnp.float32)
        inverse = 1.0 / length

        def line(n):
            return lax.broadcasted_iota(jnp.int32, (n, LANES), 0)

        def waves(n, w):
            return lax.broadcasted_iota(jnp.int32, (n, LANES), 1) + w * LANES

        for w in range(slots):
            fine_c, fine_s = cos_sin_turns((waves(16, w) * line(16)).astype(jnp.float32), length, inverse)
            step_c, step_s = cos_sin_turns((waves(8, w) * (16 * line(8))).astype(jnp.float32), length, inverse)
            for a in range(8):
                ca, sa = step_c[a:a + 1], step_s[a:a + 1]
                table_s[pl.ds(16 * a, 16), pl.ds(w * LANES, LANES)] = (ca * fine_c - sa * fine_s).astype(jnp.bfloat16)
                table_s[pl.ds(16 * a, 16), pl.ds(half_rows + w * LANES, LANES)] = (sa * fine_c + ca * fine_s).astype(jnp.bfloat16)
        lane = lax.broadcasted_iota(jnp.int32, (parts, LANES), 1)
        blocks = []
        for t in range(tiles):
            col = lane + t * LANES
            mine = (col >= start) & (col < start + whole)
            blocks.append(jnp.where(mine, y_ref[q, :, pl.ds(t * LANES, LANES)].astype(jnp.float32)[:parts], 0.0))
        stacked = jnp.concatenate(blocks, axis=0).astype(jnp.bfloat16)
        sums_s[...] = jnp.dot(stacked, table_s[...], preferred_element_type=jnp.float32)
        place = 2 * jnp.where(north, q, pairs - 1 - q) + half
        for w in range(slots):
            tile_c, tile_s = cos_sin_turns((waves(24, w) * (LANES * line(24) - start)).astype(jnp.float32), length, inverse)
            real = jnp.zeros((parts, LANES), jnp.float32)
            imag = jnp.zeros((parts, LANES), jnp.float32)
            for t in range(tiles):
                c = sums_s[pl.ds(parts * t, parts), pl.ds(w * LANES, LANES)]
                s = sums_s[pl.ds(parts * t, parts), pl.ds(half_rows + w * LANES, LANES)]
                tc, ts = tile_c[t:t + 1], tile_s[t:t + 1]
                real = real + (tc * c - ts * s)
                imag = imag - (ts * c + tc * s)
            keep = jnp.where(2 * waves(1, w) < whole, inverse, 0.0)
            four_s[pl.ds(pl.multiple_of(place * 16, 16), 16), pl.ds(w * LANES, LANES)] = jnp.concatenate(
                [real * keep, imag * keep], axis=0).astype(jnp.bfloat16)
        return 0

    lax.fori_loop(0, rows, one, 0)

    hot = (lax.broadcasted_iota(jnp.int32, (half_rows, half_rows), 0) == order_ref[...]).astype(jnp.float32).astype(jnp.bfloat16)
    moved = jnp.dot(four_s[...], hot, preferred_element_type=jnp.float32)
    mix_s[...] = jnp.zeros_like(mix_s)
    for r in range(8):
        for s in range(slots):
            mix_s[r, pl.ds(s, 16, stride=8), :] = moved[16 * r:16 * r + 16, s * LANES:(s + 1) * LANES]
        if r < slots:
            for e in range(rows - 8):
                mix_s[r, pl.ds(slots + e, 16, stride=8), :] = moved[16 * (8 + e):16 * (8 + e) + 16, r * LANES:(r + 1) * LANES]
        stage_s[pl.ds(r, LANES, stride=8), :] = mix_s[r].T
    send_s[...] = stage_s[...].astype(jnp.bfloat16).reshape(send_s.shape)

    pl.semaphore_wait(barrier, devices - 1)

    def post(a, b):
        pltpu.make_async_remote_copy(
            src_ref=send_s.at[a * across + b], dst_ref=got_s.at[me], send_sem=send_sem, recv_sem=recv_sem,
            device_id=(a, b), device_id_type=pl.DeviceIdType.MESH).start()

    partners(post)
    own = pltpu.make_async_copy(send_s.at[me], got_s.at[me], own_sem)
    own.start()

    src = lax.broadcasted_iota(jnp.int32, (slots * LANES, 2 * LANES), 0)
    dst = lax.broadcasted_iota(jnp.int32, (slots * LANES, 2 * LANES), 1)
    unfold = ((dst & 7) == (src >> 7)) & ((src & 127) == (dst & 127) - (src >> 7) + slots + (dst >> 7))
    unfold = unfold.astype(jnp.float32).astype(jnp.bfloat16)
    slot_of = (lax.broadcasted_iota(jnp.int32, (half_rows, LANES), 1) & 7).astype(jnp.float32).astype(jnp.bfloat16)
    sub = lax.broadcasted_iota(jnp.int32, (8, half_rows), 0)
    j = lax.broadcasted_iota(jnp.int32, (8, half_rows), 1)
    limit = jnp.zeros((8, half_rows), jnp.int32)
    for i in range(slots):
        limit = jnp.where(sub == i, half_rows - waves_ref[i], limit)

    rest = pl.ds(0, devices - 1)
    every = pltpu.make_async_remote_copy(
        src_ref=send_s.at[rest], dst_ref=got_s.at[rest], send_sem=send_sem, recv_sem=recv_sem,
        device_id=(my_a, columns[1]), device_id_type=pl.DeviceIdType.MESH)
    every.wait_send()
    every.wait_recv()
    own.wait()

    for d in range(devices // 2):
        n = got_s[d].astype(jnp.float32)
        o = got_s[devices - 1 - d].astype(jnp.float32)
        plain_s[pl.ds(rows * d, 8), :] = n + o
        anti_s[pl.ds(rows * d, 8), :] = n - o
        kept_s[pl.ds(8 * d, 8), :] = n + o
        keptanti_s[pl.ds(8 * d, 8), :] = n - o
    weights_in.wait()
    for par, wide, kept in ((0, plain_s, kept_s), (1, anti_s, keptanti_s)):
        folded = jnp.concatenate([kept[pl.ds(s, devices // 2, stride=8), :] for s in range(slots)], axis=1).astype(jnp.bfloat16)
        extra = jnp.dot(folded, unfold, preferred_element_type=jnp.float32)
        for e in range(rows - 8):
            wide[pl.ds(8 + e, devices // 2, stride=rows), :] = extra[:, e * LANES:(e + 1) * LANES]
        values = wide[...].astype(jnp.bfloat16)
        zero = jnp.zeros_like(values)
        picked = jnp.concatenate([jnp.where(slot_of == jnp.bfloat16(s), values, zero) for s in range(slots)], axis=0)
        table = jnp.concatenate([legendre_s[s, par] for s in range(slots)], axis=1)
        turn_s[pl.ds(par, half_rows // 2, stride=2), :] = jnp.dot(table, picked, preferred_element_type=jnp.float32)
    z = turn_s[...].T.reshape(16, 8, half_rows)
    z = jnp.where((j < limit)[None], z, 0.0)
    out_ref[...] = z[:, :slots, :]


def transform(y, order, waves, legendre, half_rows, pair_length, sizes):
    pairs = y.shape[0]
    slots = legendre.shape[0]
    tiles = pl.cdiv(pair_length, LANES)
    vm = pl.BlockSpec(memory_space=pltpu.VMEM)
    f32, b16 = jnp.float32, jnp.bfloat16
    return pl.pallas_call(
        functools.partial(transform_kernel, sizes, pair_length),
        out_shape=jax.ShapeDtypeStruct((16, slots, half_rows), f32),
        in_specs=[vm, vm, pl.BlockSpec(memory_space=pltpu.SMEM), pl.BlockSpec(memory_space=pl.ANY)],
        out_specs=vm,
        scratch_shapes=[
            pltpu.VMEM((LANES, 2 * half_rows), b16),
            pltpu.VMEM((8 * tiles, 2 * half_rows), f32),
            pltpu.VMEM((32 * pairs, half_rows), b16),
            pltpu.VMEM((8, LANES, LANES), f32),
            pltpu.VMEM((8 * LANES, LANES), f32),
            pltpu.VMEM((LANES, 8, LANES), b16),
            pltpu.VMEM((LANES, 8, LANES), b16),
            pltpu.VMEM((half_rows, LANES), f32),
            pltpu.VMEM((half_rows, LANES), f32),
            pltpu.VMEM((8 * LANES // 2, LANES), f32),
            pltpu.VMEM((8 * LANES // 2, LANES), f32),
            pltpu.VMEM((half_rows, LANES), f32),
            pltpu.VMEM(legendre.shape, b16),
            pltpu.SemaphoreType.DMA, pltpu.SemaphoreType.DMA, pltpu.SemaphoreType.DMA, pltpu.SemaphoreType.DMA,
        ],
        compiler_params=pltpu.CompilerParams(collective_id=0, has_side_effects=True),
        name="transform",
    )(y, order, waves, legendre)


def on_device(grid, dep_row, dep_lon, lon_frac, lat_frac, wave_slot, legendre):
    half_rows = wave_slot.shape[0]
    fields, levels, pairs, pair_length = grid.shape
    slots = legendre.shape[0]
    axes = ("aa", "ba")
    sizes = (lax.axis_size("aa"), lax.axis_size("ba"))
    devices = sizes[0] * sizes[1]
    device = lax.axis_index(axes)
    first = (device * pairs).astype(jnp.int32).reshape(1)
    own = jnp.transpose(grid.reshape(fields * levels, pairs, pair_length), (1, 0, 2))
    up = [(i, i + 1) for i in range(devices - 1)]
    down = [(j, i) for i, j in up]
    before = lax.ppermute(own[pairs - 2:], axes, up)
    after = lax.ppermute(own[:2], axes, down)
    order = jnp.transpose(wave_slot.reshape(devices, slots)).reshape(1, half_rows)
    waves = lax.dynamic_slice_in_dim(wave_slot, device * slots, slots)
    y = interpolate(first, before, own, after, dep_row, dep_lon, lon_frac, lat_frac, half_rows)
    result = transform(y, order, waves, legendre, half_rows, pair_length, sizes)
    interpolated = jnp.transpose(y[:, :, :pair_length], (1, 0, 2)).reshape(grid.shape)
    return (interpolated, result)


def solution(mesh):
    return jax.shard_map(
        on_device,
        mesh=mesh,
        in_specs=(
            P(None, None, ("aa", "ba"), None),
            P(("aa", "ba"), None),
            P(None, ("aa", "ba"), None),
            P(None, ("aa", "ba"), None),
            P(("aa", "ba"), None),
            P(),
            P(("aa", "ba"), None, None, None),
        ),
        out_specs=(P(None, None, ("aa", "ba"), None), P(None, ("aa", "ba"), None)),
        check_vma=False,
    )
```

```python
import functools

import jax
import jax.numpy as jnp
from jax import lax
from jax.experimental import pallas as pl
from jax.experimental.pallas import tpu as pltpu
from jax.sharding import PartitionSpec as P

LANES = 128
WIN = 256
ETILES = 24
EW = ETILES * LANES
MARGIN = 60
ROWS = 11
NOWHERE = 192.0


def row_place(global_row, half_rows):
    northern = global_row < half_rows
    number = jnp.where(northern, global_row + 1, 2 * half_rows - global_row)
    second = number > half_rows // 2
    inner = jnp.where(second, number - half_rows // 2 - 1, half_rows // 2 - number)
    begin = jnp.where(second, 16 + 4 * (half_rows // 2 - inner), 0)
    return jnp.where(northern, inner, half_rows - 1 - inner), begin, 16 + 4 * number


def cubic(t):
    return (
        -t * (t - 1.0) * (t - 2.0) * (1.0 / 6.0),
        (t + 1.0) * (t - 1.0) * (t - 2.0) * 0.5,
        -(t + 1.0) * t * (t - 2.0) * 0.5,
        (t + 1.0) * t * (t - 1.0) * (1.0 / 6.0),
    )


def interp_kernel(half_rows, pair_length, first_ref, before_ref, own_ref, after_ref,
                  row_ref, lon_ref, lonf_ref, latf_ref, out_ref, head_ref,
                  place_t, ext_s, plan_s, y_s):
    groups, pairs, levels, _ = own_ref.shape
    fields = groups * levels
    near = pairs + 4
    tiles = pl.cdiv(pair_length, LANES)
    first = first_ref[0]

    ext_s[:, :, pl.ds(0, LANES)] = jnp.zeros((2 * near, fields, LANES), jnp.bfloat16)
    ext_s[:, :, pl.ds(tiles * LANES, EW - tiles * LANES)] = jnp.zeros((2 * near, fields, EW - tiles * LANES), jnp.bfloat16)
    for j in range(near):
        ref, at = (before_ref, j) if j < 2 else ((own_ref, j - 2) if j < 2 + pairs else (after_ref, j - 2 - pairs))
        for f in range(groups):
            src = ref[f, at]
            for copy in range(2):
                ext_s[2 * j + copy, pl.ds(levels * f, levels), pl.ds(LANES, pair_length)] = src

    lane = lax.broadcasted_iota(jnp.int32, (fields, LANES), 1)

    def half_lengths(pair):
        inner = jnp.where(pair < half_rows // 2, pair, half_rows - 1 - pair)
        return 16 + 4 * (half_rows // 2 - inner), 16 + 4 * (half_rows // 2 + 1 + inner)

    def wrap(copy, tile, shift, low, edge):
        at = pl.ds(pl.multiple_of(tile * LANES, LANES), LANES)
        begin = tile * LANES + shift
        two = ext_s[copy, :, pl.ds(pl.multiple_of((begin >> 7) * LANES, LANES), 2 * LANES)].astype(jnp.float32)
        moved = pltpu.roll(two, (2 * LANES - (begin & 127)) & 255, 1)[:, :LANES]
        spot = lane + tile * LANES
        beyond = spot < edge if low else spot >= edge
        return copy, at, jnp.where(beyond, moved, ext_s[copy, :, at].astype(jnp.float32)).astype(jnp.bfloat16)

    for j in range(near):
        len0, len1 = half_lengths(first + j - 2)
        wraps = []
        for half in range(2):
            start, length = (len0, len1) if half else (0, len0)
            for i in range(1 + half):
                wraps.append(wrap(2 * j + half, ((start >> 7) if half else 0) + i, length, True, start + LANES))
            for i in range(3):
                wraps.append(wrap(2 * j + half, ((start + length) >> 7) + 1 + i, -length, False, start + length + LANES))
        for copy, at, tile in wraps:
            ext_s[copy, :, at] = tile

    sub8 = lax.broadcasted_iota(jnp.int32, (8, LANES), 0)
    lane8 = lax.broadcasted_iota(jnp.int32, (8, LANES), 1)

    def weigh(tile, fits, width=LANES):
        at = pl.ds(pl.multiple_of(tile * LANES, LANES), LANES)
        some = pl.ds(pl.multiple_of(tile * LANES, LANES), width)
        col = tile * LANES + lane8
        inside = col < pair_length

        def wide(x):
            if width < LANES:
                x = jnp.concatenate([x, jnp.zeros((x.shape[0], LANES - width), x.dtype)], axis=1)
            return x

        for q in range(pairs):
            pair = first + q
            northern = pair < half_rows // 2
            len0, _ = half_lengths(pair)
            second = col >= len0
            inner = jnp.where(northern, pair, half_rows - 1 - pair)

            def base_of(number):
                return jnp.clip(jnp.where(northern, number - 1, 2 * half_rows - number) - 2, 0, 2 * half_rows - 4)

            base = jnp.where(second, base_of(half_rows // 2 + 1 + inner), base_of(half_rows // 2 - inner))
            later = jnp.broadcast_to(wide(row_ref[pl.ds(q, 1), some]), (8, LANES)) > base
            base_k = jnp.where(second, jnp.maximum(tile * LANES - len0, 0), tile * LANES) - MARGIN
            lon = wide(lon_ref[q, :, some])
            lon = jnp.concatenate([lon, lon], axis=0)
            lon = jnp.where(later, pltpu.roll(lon, 1, 0), lon)
            frac = wide(lonf_ref[q, :, some])
            frac = jnp.concatenate([frac, frac], axis=0)
            frac = jnp.where(later, pltpu.roll(frac, 1, 0), frac)
            latw = cubic(jnp.broadcast_to(wide(latf_ref[pl.ds(q, 1), some]), (8, LANES)))
            r = jnp.where(later, sub8 - 1, sub8)
            lat = jnp.zeros((8, LANES), jnp.float32)
            for i in range(4):
                lat = jnp.where(inside & (r == i), latw[i], lat)
            _, begin, length = row_place(jnp.minimum(base + sub8, 2 * half_rows - 1), half_rows)
            rel = lon - 1 - base_k
            rel = jnp.where(rel < 0, rel + length, jnp.where(rel >= length, rel - length, rel))
            short = length <= WIN - 4
            rel = jnp.where(short, lon, rel)
            bad = (lat != 0.0) & ((rel < 0) | (rel > WIN - 4))
            fits = jnp.maximum(fits, bad.astype(jnp.int32))
            place = ((begin + jnp.where(short, -1, base_k) + LANES) & 127) + rel
            block = (place >> 4) & 15
            ws = cubic(frac)
            for o in range(4):
                plan_s[q * ROWS + o, :, at] = lat * ws[o]
                plan_s[q * ROWS + 4 + o, :, at] = ((place + o) & 15).astype(jnp.float32)
            plan_s[q * ROWS + 8, :, at] = block.astype(jnp.float32)
            plan_s[q * ROWS + 9, :, at] = ((block + 1) & 15).astype(jnp.float32)
            plan_s[q * ROWS + 10, :, at] = (lon + begin).astype(jnp.float32)
        return fits

    worst = lax.fori_loop(0, pair_length // LANES, weigh, jnp.zeros((8, LANES), jnp.int32))
    if pair_length % LANES:
        worst = weigh(tiles - 1, worst, pair_length % LANES)
    local = jnp.max(worst) == 0

    node = lax.broadcasted_iota(jnp.int32, (16, LANES), 0).astype(jnp.float32).astype(jnp.bfloat16)
    zero16 = jnp.zeros((16, LANES), jnp.bfloat16)

    def spread(mine, weight, rest, block, after):
        v = zero16
        for o in (3, 2, 1, 0):
            v = jnp.where(node == rest[o], weight[o], v)
        block = jnp.where(mine, jnp.where(node < rest[0], after, block), jnp.bfloat16(NOWHERE))
        return [jnp.where(block == jnp.bfloat16(a), v, zero16) for a in range(WIN // 16)]

    def plan(d, i, q, at):
        return jnp.broadcast_to(plan_s[q * ROWS + i, pl.ds(d, 1), at], (16, LANES))

    def packed(x):
        return x.astype(jnp.bfloat16)

    for q in range(pairs):
        pair = first + q
        northern = pair < half_rows // 2
        inner = jnp.where(northern, pair, half_rows - 1 - pair)
        for half in range(2):
            number = half_rows // 2 + 1 + inner if half else half_rows // 2 - inner
            g = jnp.where(northern, number - 1, 2 * half_rows - number)
            base = jnp.clip(g - 2, 0, 2 * half_rows - 4)
            for d in range(5):
                pair_row, begin, length = row_place(jnp.minimum(base + d, 2 * half_rows - 1), half_rows)
                short = length <= WIN - 4
                copy = 2 * jnp.clip(pair_row - first + 2, 0, near - 1) + (begin > 0).astype(jnp.int32)
                at = 3 * ((2 * q + half) * 5 + d)
                place_t[at] = copy
                place_t[at + 1] = begin + LANES + jnp.where(short, -1, -MARGIN)
                place_t[at + 2] = jnp.where(short, 0, 1)

    def unit_scalars(q, u):
        len0, _ = half_lengths(first + q)
        straddle = len0 >> 7
        half = (u > straddle).astype(jnp.int32)
        tile = u - half
        k0 = jnp.where(half == 1, jnp.maximum(tile * LANES - len0, 0), tile * LANES)
        return len0, straddle, half, tile, 15 * (2 * q + half), k0

    lane16 = lax.broadcasted_iota(jnp.int32, (16, LANES), 1).astype(jnp.float32).astype(jnp.bfloat16)

    def own_half(half, tile, len0):
        edge = jnp.clip(len0 - tile * LANES, 0, LANES)
        low = jnp.where(half == 1, edge, 0).astype(jnp.float32)
        high = jnp.where(half == 1, LANES, edge).astype(jnp.float32)
        spread_low = jnp.full((16, LANES), low, jnp.float32).astype(jnp.bfloat16)
        spread_high = jnp.full((16, LANES), high, jnp.float32).astype(jnp.bfloat16)
        return (lane16 >= spread_low) & (lane16 < spread_high)

    def finish(q, u, straddle, tile, total, carry):
        total = total + jnp.where(u == straddle + 1, carry, 0.0)
        at = pl.ds(pl.multiple_of(tile * LANES, LANES), LANES)
        y_s[q, :, at] = total.astype(jnp.bfloat16)
        head_ref[q, :, at] = total[:head_ref.shape[1]].astype(jnp.bfloat16)
        return total

    @pl.when(local)
    def _():
        def unit(q, u, carry):
            len0, straddle, half, tile, base, k0 = unit_scalars(q, u)
            at = pl.ds(pl.multiple_of(tile * LANES, LANES), LANES)
            mine = own_half(half, tile, len0)
            rows, weights = [], []
            for d in range(5):
                where_row = place_t[base + 3 * d]
                begin = place_t[base + 3 * d + 1] + place_t[base + 3 * d + 2] * k0
                s = begin & 127
                first_tile = pl.multiple_of((begin >> 7) * LANES, LANES)
                row = [packed(plan(d, i, q, at)) for i in range(10)]
                weights += spread(mine, row[:4], row[4:8], row[8], row[9])
                three = ext_s[where_row, :, pl.ds(first_tile, 3 * LANES)]
                rows += [jnp.where(lane >= s, three[:, :LANES], three[:, 2 * LANES:]), three[:, LANES:2 * LANES]]
            total = jnp.dot(jnp.concatenate(rows, axis=1), jnp.concatenate(weights, axis=0),
                            preferred_element_type=jnp.float32)
            return finish(q, u, straddle, tile, total, carry)

        lax.fori_loop(0, tiles + 1, lambda u, carry: tuple(unit(q, u, carry[q]) for q in range(pairs)),
                      (jnp.zeros((fields, LANES), jnp.float32),) * pairs)

    @pl.when(jnp.logical_not(local))
    def _():
        def unit(q, u, carry):
            len0, straddle, half, tile, base, _ = unit_scalars(q, u)
            at = pl.ds(pl.multiple_of(tile * LANES, LANES), LANES)
            mine = own_half(half, tile, len0)

            def window(w, total):
                rows, weights = [], []
                for d in range(5):
                    where_row = place_t[base + 3 * d]
                    place = (plan(d, 10, q, at) + (LANES - 1)).astype(jnp.int32) - w * WIN
                    block = jnp.clip(place >> 4, -2, 18)
                    rest = [packed(((place + o) & 15).astype(jnp.float32)) for o in range(4)]
                    weight = [packed(plan(d, o, q, at)) for o in range(4)]
                    weights += spread(mine, weight, rest, packed(block.astype(jnp.float32)), packed((block + 1).astype(jnp.float32)))
                    rows.append(ext_s[where_row, :, pl.ds(pl.multiple_of(w * WIN, WIN), WIN)])
                return total + jnp.dot(jnp.concatenate(rows, axis=1), jnp.concatenate(weights, axis=0),
                                       preferred_element_type=jnp.float32)

            total = lax.fori_loop(0, EW // WIN, window, jnp.zeros((fields, LANES), jnp.float32))
            return finish(q, u, straddle, tile, total, carry)

        lax.fori_loop(0, tiles + 1, lambda u, carry: tuple(unit(q, u, carry[q]) for q in range(pairs)),
                      (jnp.zeros((fields, LANES), jnp.float32),) * pairs)

    for f in range(groups):
        for q in range(pairs):
            out_ref[f, q] = y_s[q, pl.ds(levels * f, levels), pl.ds(0, pair_length)]


def interpolate(first, before, own, after, dep_row, dep_lon, lon_frac, lat_frac, half_rows, spectral_fields):
    groups, pairs, levels, pair_length = own.shape
    fields = groups * levels
    padded = pl.cdiv(pair_length, LANES) * LANES
    near = pairs + 4
    vm = pl.BlockSpec(memory_space=pltpu.VMEM)
    return pl.pallas_call(
        functools.partial(interp_kernel, half_rows, pair_length),
        out_shape=(
            jax.ShapeDtypeStruct(own.shape, jnp.bfloat16),
            jax.ShapeDtypeStruct((pairs, spectral_fields, padded), jnp.bfloat16),
        ),
        in_specs=[pl.BlockSpec(memory_space=pltpu.SMEM)] + [vm] * 7,
        out_specs=(vm, vm),
        scratch_shapes=[
            pltpu.SMEM((30 * pairs,), jnp.int32),
            pltpu.VMEM((2 * near, fields, EW), jnp.bfloat16),
            pltpu.VMEM((pairs * ROWS, 8, padded), jnp.float32),
            pltpu.VMEM((pairs, fields, padded), jnp.bfloat16),
        ],
        name="interp",
    )(first, before, own, after, dep_row, dep_lon, lon_frac, lat_frac)


COS = (1, -19.7392087, 64.9393842, -85.4565372, 60.2407014, -26.3960673, 7.77462739, -1.42354417)
SIN = (6.28318531, -41.3417022, 81.6052456, -76.7057546, 42.0572162, -15.0833301, 3.7717259, -0.609657301)


def cos_sin_turns(prod, length, inverse):
    turns = jnp.floor(prod * inverse + 0.5)
    t = (prod - turns * length) * inverse
    x = t * t
    c = jnp.full_like(x, COS[-1])
    for a in COS[-2::-1]:
        c = c * x + a
    s = jnp.full_like(x, SIN[-1])
    for a in SIN[-2::-1]:
        s = s * x + a
    return c, s * t


def transform_kernel(sizes, pair_length, y_ref, order_ref, waves_ref, legendre_hbm, out_ref,
                     table_s, sums_s, four_s, mix_s, stage_s, send_s, got_s, plain_s, anti_s, kept_s, keptanti_s, turn_s, legendre_s,
                     legendre_sem, own_sem, send_sem, recv_sem):
    along, across = sizes
    devices = along * across
    pairs = y_ref.shape[0]
    slots = legendre_s.shape[0]
    half_rows = slots * devices
    rows = 2 * pairs
    tiles = pl.cdiv(pair_length, LANES)
    my_a = lax.axis_index("aa")
    my_b = lax.axis_index("ba")
    me = my_a * across + my_b
    first = me * pairs
    north = me < devices // 2
    parts = 8

    weights_in = pltpu.make_async_copy(legendre_hbm, legendre_s, legendre_sem)
    weights_in.start()

    columns = [lax.rem(my_b + i, across) for i in range(across)]

    def partners(act):
        for b in range(1, across):
            act(my_a, columns[b])

        def others(i, _):
            a = lax.rem(my_a + i, along)
            for b in range(across):
                act(a, columns[b])
            return 0

        lax.fori_loop(1, along, others, 0)

    barrier = pltpu.get_barrier_semaphore()
    partners(lambda a, b: pl.semaphore_signal(barrier, inc=1, device_id=(a, b), device_id_type=pl.DeviceIdType.MESH))

    def one(i, _):
        q = i // 2
        half = i - 2 * q
        pair = first + q
        inner = jnp.where(north, pair, half_rows - 1 - pair)
        len0 = 16 + 4 * (half_rows // 2 - inner)
        start = jnp.where(half == 1, len0, 0)
        whole = jnp.where(half == 1, 16 + 4 * (half_rows // 2 + 1 + inner), len0)
        length = jnp.full((1, LANES), whole, jnp.int32).astype(jnp.float32)
        inverse = 1.0 / length

        def line(n):
            return lax.broadcasted_iota(jnp.int32, (n, LANES), 0)

        def waves(n, w):
            return lax.broadcasted_iota(jnp.int32, (n, LANES), 1) + w * LANES

        for w in range(slots):
            fine_c, fine_s = cos_sin_turns((waves(16, w) * line(16)).astype(jnp.float32), length, inverse)
            step_c, step_s = cos_sin_turns((waves(8, w) * (16 * line(8))).astype(jnp.float32), length, inverse)
            for a in range(8):
                ca, sa = step_c[a:a + 1], step_s[a:a + 1]
                table_s[pl.ds(16 * a, 16), pl.ds(w * LANES, LANES)] = (ca * fine_c - sa * fine_s).astype(jnp.bfloat16)
                table_s[pl.ds(16 * a, 16), pl.ds(half_rows + w * LANES, LANES)] = (sa * fine_c + ca * fine_s).astype(jnp.bfloat16)
        lane = lax.broadcasted_iota(jnp.int32, (parts, LANES), 1)
        blocks = []
        for t in range(tiles):
            col = lane + t * LANES
            mine = (col >= start) & (col < start + whole)
            blocks.append(jnp.where(mine, y_ref[q, :, pl.ds(t * LANES, LANES)].astype(jnp.float32)[:parts], 0.0))
        stacked = jnp.concatenate(blocks, axis=0).astype(jnp.bfloat16)
        sums_s[...] = jnp.dot(stacked, table_s[...], preferred_element_type=jnp.float32)
        place = 2 * jnp.where(north, q, pairs - 1 - q) + half
        for w in range(slots):
            tile_c, tile_s = cos_sin_turns((waves(24, w) * (LANES * line(24) - start)).astype(jnp.float32), length, inverse)
            real = jnp.zeros((parts, LANES), jnp.float32)
            imag = jnp.zeros((parts, LANES), jnp.float32)
            for t in range(tiles):
                c = sums_s[pl.ds(parts * t, parts), pl.ds(w * LANES, LANES)]
                s = sums_s[pl.ds(parts * t, parts), pl.ds(half_rows + w * LANES, LANES)]
                tc, ts = tile_c[t:t + 1], tile_s[t:t + 1]
                real = real + (tc * c - ts * s)
                imag = imag - (ts * c + tc * s)
            keep = jnp.where(2 * waves(1, w) < whole, inverse, 0.0)
            four_s[pl.ds(pl.multiple_of(place * 16, 16), 16), pl.ds(w * LANES, LANES)] = jnp.concatenate(
                [real * keep, imag * keep], axis=0).astype(jnp.bfloat16)
        return 0

    lax.fori_loop(0, rows, one, 0)

    hot = (lax.broadcasted_iota(jnp.int32, (half_rows, half_rows), 0) == order_ref[...]).astype(jnp.float32).astype(jnp.bfloat16)
    moved = jnp.dot(four_s[...], hot, preferred_element_type=jnp.float32)
    mix_s[...] = jnp.zeros_like(mix_s)
    for r in range(8):
        for s in range(slots):
            mix_s[r, pl.ds(16 * s, 16), :] = moved[16 * r:16 * r + 16, s * LANES:(s + 1) * LANES]
        if r < slots:
            for e in range(rows - 8):
                mix_s[r, pl.ds(16 * (slots + e), 16), :] = moved[16 * (8 + e):16 * (8 + e) + 16, r * LANES:(r + 1) * LANES]
        stage_s[pl.ds(r, LANES, stride=8), :] = mix_s[r].T
    send_s[...] = stage_s[...].astype(jnp.bfloat16).reshape(send_s.shape)

    pl.semaphore_wait(barrier, devices - 1)

    def post(a, b):
        pltpu.make_async_remote_copy(
            src_ref=send_s.at[a * across + b], dst_ref=got_s.at[me], send_sem=send_sem, recv_sem=recv_sem,
            device_id=(a, b), device_id_type=pl.DeviceIdType.MESH).start()

    partners(post)
    own = pltpu.make_async_copy(send_s.at[me], got_s.at[me], own_sem)
    own.start()

    src = lax.broadcasted_iota(jnp.int32, (slots * LANES, 2 * LANES), 0)
    dst = lax.broadcasted_iota(jnp.int32, (slots * LANES, 2 * LANES), 1)
    unfold = (((dst & 127) >> 4) == (src >> 7)) & ((src & 127) == 16 * (slots + (dst >> 7)) + (dst & 15))
    unfold = unfold.astype(jnp.float32).astype(jnp.bfloat16)
    slot_of = (lax.broadcasted_iota(jnp.int32, (half_rows, LANES), 1) >> 4).astype(jnp.float32).astype(jnp.bfloat16)
    rest = pl.ds(0, devices - 1)
    every = pltpu.make_async_remote_copy(
        src_ref=send_s.at[rest], dst_ref=got_s.at[rest], send_sem=send_sem, recv_sem=recv_sem,
        device_id=(my_a, columns[1]), device_id_type=pl.DeviceIdType.MESH)
    every.wait_send()
    every.wait_recv()
    own.wait()

    for d in range(devices // 2):
        n = got_s[d].astype(jnp.float32)
        o = got_s[devices - 1 - d].astype(jnp.float32)
        plain_s[pl.ds(rows * d, 8), :] = n + o
        anti_s[pl.ds(rows * d, 8), :] = n - o
        kept_s[pl.ds(8 * d, 8), :] = n + o
        keptanti_s[pl.ds(8 * d, 8), :] = n - o
    weights_in.wait()
    for par, wide, kept in ((0, plain_s, kept_s), (1, anti_s, keptanti_s)):
        folded = jnp.concatenate([kept[pl.ds(s, devices // 2, stride=8), :] for s in range(slots)], axis=1).astype(jnp.bfloat16)
        extra = jnp.dot(folded, unfold, preferred_element_type=jnp.float32)
        for e in range(rows - 8):
            wide[pl.ds(8 + e, devices // 2, stride=rows), :] = extra[:, e * LANES:(e + 1) * LANES]
        values = wide[...].astype(jnp.bfloat16)
        zero = jnp.zeros_like(values)
        picked = jnp.concatenate([jnp.where(slot_of == jnp.bfloat16(s), values, zero) for s in range(slots)], axis=0)
        table = jnp.concatenate([legendre_s[s, par] for s in range(slots)], axis=1)
        turn_s[pl.ds(par, half_rows // 2, stride=2), :] = jnp.dot(table, picked, preferred_element_type=jnp.float32)
    z = turn_s[...].T
    degree = lax.broadcasted_iota(jnp.int32, (16, half_rows), 1)
    for s in range(slots):
        limit = half_rows - waves_ref[me * slots + s]
        out_ref[s] = jnp.where(degree < limit, z[16 * s:16 * s + 16], 0.0)


def transform(y, order, waves, legendre, half_rows, pair_length, sizes):
    pairs = y.shape[0]
    slots = legendre.shape[0]
    tiles = pl.cdiv(pair_length, LANES)
    vm = pl.BlockSpec(memory_space=pltpu.VMEM)
    f32, b16 = jnp.float32, jnp.bfloat16
    return pl.pallas_call(
        functools.partial(transform_kernel, sizes, pair_length),
        out_shape=jax.ShapeDtypeStruct((slots, 16, half_rows), f32),
        in_specs=[vm, vm, pl.BlockSpec(memory_space=pltpu.SMEM), pl.BlockSpec(memory_space=pl.ANY)],
        out_specs=vm,
        scratch_shapes=[
            pltpu.VMEM((LANES, 2 * half_rows), b16),
            pltpu.VMEM((8 * tiles, 2 * half_rows), f32),
            pltpu.VMEM((32 * pairs, half_rows), b16),
            pltpu.VMEM((8, LANES, LANES), f32),
            pltpu.VMEM((8 * LANES, LANES), f32),
            pltpu.VMEM((LANES, 8, LANES), b16),
            pltpu.VMEM((LANES, 8, LANES), b16),
            pltpu.VMEM((half_rows, LANES), f32),
            pltpu.VMEM((half_rows, LANES), f32),
            pltpu.VMEM((8 * LANES // 2, LANES), f32),
            pltpu.VMEM((8 * LANES // 2, LANES), f32),
            pltpu.VMEM((half_rows, LANES), f32),
            pltpu.VMEM(legendre.shape, b16),
            pltpu.SemaphoreType.DMA, pltpu.SemaphoreType.DMA, pltpu.SemaphoreType.DMA, pltpu.SemaphoreType.DMA,
        ],
        compiler_params=pltpu.CompilerParams(collective_id=0, has_side_effects=True),
        name="transform",
    )(y, order, waves, legendre)


def on_device(grid, dep_row, dep_lon, lon_frac, lat_frac, wave_slot, legendre):
    half_rows = wave_slot.shape[0]
    fields, levels, pairs, pair_length = grid.shape
    slots = legendre.shape[0]
    axes = ("aa", "ba")
    sizes = (lax.axis_size("aa"), lax.axis_size("ba"))
    devices = sizes[0] * sizes[1]
    device = lax.axis_index(axes)
    first = (device * pairs).astype(jnp.int32).reshape(1)
    own = jnp.transpose(grid, (0, 2, 1, 3))
    up = [(i, i + 1) for i in range(devices - 1)]
    down = [(j, i) for i, j in up]
    before = lax.ppermute(own[:, pairs - 2:], axes, up)
    after = lax.ppermute(own[:, :2], axes, down)
    order = jnp.transpose(wave_slot.reshape(devices, slots)).reshape(1, half_rows)
    out, head = interpolate(first, before, own, after, dep_row, jnp.transpose(dep_lon, (1, 0, 2)),
                            jnp.transpose(lon_frac, (1, 0, 2)), lat_frac, half_rows, 2 * levels)
    result = transform(head, order, wave_slot, legendre, half_rows, pair_length, sizes)
    return (jnp.transpose(out, (0, 2, 1, 3)), jnp.transpose(result, (1, 0, 2)))


def solution(mesh):
    return jax.shard_map(
        on_device,
        mesh=mesh,
        in_specs=(
            P(None, None, ("aa", "ba"), None),
            P(("aa", "ba"), None),
            P(None, ("aa", "ba"), None),
            P(None, ("aa", "ba"), None),
            P(("aa", "ba"), None),
            P(),
            P(("aa", "ba"), None, None, None),
        ),
        out_specs=(P(None, None, ("aa", "ba"), None), P(None, ("aa", "ba"), None)),
        check_vma=False,
    )
```

```python
import functools

import jax
import jax.numpy as jnp
from jax import lax
from jax.experimental import pallas as pl
from jax.experimental.pallas import tpu as pltpu
from jax.sharding import PartitionSpec as P

LANES = 128
WIN = 256
ETILES = 24
EW = ETILES * LANES
MARGIN = 60
ROWS = 11
NOWHERE = 192.0


def row_place(global_row, half_rows):
    northern = global_row < half_rows
    number = jnp.where(northern, global_row + 1, 2 * half_rows - global_row)
    second = number > half_rows // 2
    inner = jnp.where(second, number - half_rows // 2 - 1, half_rows // 2 - number)
    begin = jnp.where(second, 16 + 4 * (half_rows // 2 - inner), 0)
    return jnp.where(northern, inner, half_rows - 1 - inner), begin, 16 + 4 * number


def cubic(t):
    return (
        -t * (t - 1.0) * (t - 2.0) * (1.0 / 6.0),
        (t + 1.0) * (t - 1.0) * (t - 2.0) * 0.5,
        -(t + 1.0) * t * (t - 2.0) * 0.5,
        (t + 1.0) * t * (t - 1.0) * (1.0 / 6.0),
    )


class Stencil:
    pass


def stencil_steps(half_rows, pair_length, first, sources, row_ref, lon_ref, lonf_ref, latf_ref, place_t, ext_s, plan_s, y_s, head_s):
    groups, pairs, levels, _ = sources[1].shape
    fields = groups * levels
    near = pairs + 4
    tiles = pl.cdiv(pair_length, LANES)
    steps = Stencil()

    lane = lax.broadcasted_iota(jnp.int32, (fields, LANES), 1)

    def half_lengths(pair):
        inner = jnp.where(pair < half_rows // 2, pair, half_rows - 1 - pair)
        return 16 + 4 * (half_rows // 2 - inner), 16 + 4 * (half_rows // 2 + 1 + inner)

    def clear():
        ext_s[:, :, pl.ds(0, LANES)] = jnp.zeros((2 * near, fields, LANES), jnp.bfloat16)
        ext_s[:, :, pl.ds(tiles * LANES, EW - tiles * LANES)] = jnp.zeros((2 * near, fields, EW - tiles * LANES), jnp.bfloat16)

    def fill(j):
        ref, at = (sources[0], j) if j < 2 else ((sources[1], j - 2) if j < 2 + pairs else (sources[2], j - 2 - pairs))
        for f in range(groups):
            src = ref[f, at]
            for copy in range(2):
                ext_s[2 * j + copy, pl.ds(levels * f, levels), pl.ds(LANES, pair_length)] = src

    def wrap(copy, tile, shift, low, edge):
        at = pl.ds(pl.multiple_of(tile * LANES, LANES), LANES)
        begin = tile * LANES + shift
        two = ext_s[copy, :, pl.ds(pl.multiple_of((begin >> 7) * LANES, LANES), 2 * LANES)].astype(jnp.float32)
        moved = pltpu.roll(two, (2 * LANES - (begin & 127)) & 255, 1)[:, :LANES]
        spot = lane + tile * LANES
        beyond = spot < edge if low else spot >= edge
        return copy, at, jnp.where(beyond, moved, ext_s[copy, :, at].astype(jnp.float32)).astype(jnp.bfloat16)

    def close(j):
        len0, len1 = half_lengths(first + j - 2)
        wraps = []
        for half in range(2):
            start, length = (len0, len1) if half else (0, len0)
            for i in range(1 + half):
                wraps.append(wrap(2 * j + half, ((start >> 7) if half else 0) + i, length, True, start + LANES))
            for i in range(3):
                wraps.append(wrap(2 * j + half, ((start + length) >> 7) + 1 + i, -length, False, start + length + LANES))
        for copy, at, tile in wraps:
            ext_s[copy, :, at] = tile

    sub8 = lax.broadcasted_iota(jnp.int32, (8, LANES), 0)
    lane8 = lax.broadcasted_iota(jnp.int32, (8, LANES), 1)

    def weigh(tile, fits, width=LANES):
        at = pl.ds(pl.multiple_of(tile * LANES, LANES), LANES)
        some = pl.ds(pl.multiple_of(tile * LANES, LANES), width)
        col = tile * LANES + lane8
        inside = col < pair_length

        def wide(x):
            if width < LANES:
                x = jnp.concatenate([x, jnp.zeros((x.shape[0], LANES - width), x.dtype)], axis=1)
            return x

        for q in range(pairs):
            pair = first + q
            northern = pair < half_rows // 2
            len0, _ = half_lengths(pair)
            second = col >= len0
            inner = jnp.where(northern, pair, half_rows - 1 - pair)

            def base_of(number):
                return jnp.clip(jnp.where(northern, number - 1, 2 * half_rows - number) - 2, 0, 2 * half_rows - 4)

            base = jnp.where(second, base_of(half_rows // 2 + 1 + inner), base_of(half_rows // 2 - inner))
            later = jnp.broadcast_to(wide(row_ref[pl.ds(q, 1), some]), (8, LANES)) > base
            base_k = jnp.where(second, jnp.maximum(tile * LANES - len0, 0), tile * LANES) - MARGIN
            lon = wide(lon_ref[q, :, some])
            lon = jnp.concatenate([lon, lon], axis=0)
            lon = jnp.where(later, pltpu.roll(lon, 1, 0), lon)
            frac = wide(lonf_ref[q, :, some])
            frac = jnp.concatenate([frac, frac], axis=0)
            frac = jnp.where(later, pltpu.roll(frac, 1, 0), frac)
            latw = cubic(jnp.broadcast_to(wide(latf_ref[pl.ds(q, 1), some]), (8, LANES)))
            r = jnp.where(later, sub8 - 1, sub8)
            lat = jnp.zeros((8, LANES), jnp.float32)
            for i in range(4):
                lat = jnp.where(inside & (r == i), latw[i], lat)
            _, begin, length = row_place(jnp.minimum(base + sub8, 2 * half_rows - 1), half_rows)
            rel = lon - 1 - base_k
            rel = jnp.where(rel < 0, rel + length, jnp.where(rel >= length, rel - length, rel))
            short = length <= WIN - 4
            rel = jnp.where(short, lon, rel)
            bad = (lat != 0.0) & ((rel < 0) | (rel > WIN - 4))
            fits = jnp.maximum(fits, bad.astype(jnp.int32))
            place = ((begin + jnp.where(short, -1, base_k) + LANES) & 127) + rel
            block = (place >> 4) & 15
            ws = cubic(frac)
            for o in range(4):
                plan_s[q * ROWS + o, :, at] = lat * ws[o]
                plan_s[q * ROWS + 4 + o, :, at] = ((place + o) & 15).astype(jnp.float32)
            plan_s[q * ROWS + 8, :, at] = block.astype(jnp.float32)
            plan_s[q * ROWS + 9, :, at] = ((block + 1) & 15).astype(jnp.float32)
            plan_s[q * ROWS + 10, :, at] = (lon + begin).astype(jnp.float32)
        return fits

    def weigh_all():
        worst = lax.fori_loop(0, pair_length // LANES, weigh, jnp.zeros((8, LANES), jnp.int32))
        if pair_length % LANES:
            worst = weigh(tiles - 1, worst, pair_length % LANES)
        return worst

    node = lax.broadcasted_iota(jnp.int32, (16, LANES), 0).astype(jnp.float32).astype(jnp.bfloat16)
    zero16 = jnp.zeros((16, LANES), jnp.bfloat16)

    def spread(mine, weight, rest, block, after):
        v = zero16
        for o in (3, 2, 1, 0):
            v = jnp.where(node == rest[o], weight[o], v)
        block = jnp.where(mine, jnp.where(node < rest[0], after, block), jnp.bfloat16(NOWHERE))
        return [jnp.where(block == jnp.bfloat16(a), v, zero16) for a in range(WIN // 16)]

    def plan(d, i, q, at):
        return jnp.broadcast_to(plan_s[q * ROWS + i, pl.ds(d, 1), at], (16, LANES))

    def packed(x):
        return x.astype(jnp.bfloat16)

    def locate():
        for q in range(pairs):
            pair = first + q
            northern = pair < half_rows // 2
            inner = jnp.where(northern, pair, half_rows - 1 - pair)
            for half in range(2):
                number = half_rows // 2 + 1 + inner if half else half_rows // 2 - inner
                g = jnp.where(northern, number - 1, 2 * half_rows - number)
                base = jnp.clip(g - 2, 0, 2 * half_rows - 4)
                for d in range(5):
                    pair_row, begin, length = row_place(jnp.minimum(base + d, 2 * half_rows - 1), half_rows)
                    short = length <= WIN - 4
                    copy = 2 * jnp.clip(pair_row - first + 2, 0, near - 1) + (begin > 0).astype(jnp.int32)
                    at = 3 * ((2 * q + half) * 5 + d)
                    place_t[at] = copy
                    place_t[at + 1] = begin + LANES + jnp.where(short, -1, -MARGIN)
                    place_t[at + 2] = jnp.where(short, 0, 1)

    def unit_scalars(q, u):
        len0, _ = half_lengths(first + q)
        straddle = len0 >> 7
        half = (u > straddle).astype(jnp.int32)
        tile = u - half
        k0 = jnp.where(half == 1, jnp.maximum(tile * LANES - len0, 0), tile * LANES)
        return len0, straddle, half, tile, 15 * (2 * q + half), k0

    lane16 = lax.broadcasted_iota(jnp.int32, (16, LANES), 1).astype(jnp.float32).astype(jnp.bfloat16)

    def own_half(half, tile, len0):
        edge = jnp.clip(len0 - tile * LANES, 0, LANES)
        low = jnp.where(half == 1, edge, 0).astype(jnp.float32)
        high = jnp.where(half == 1, LANES, edge).astype(jnp.float32)
        spread_low = jnp.full((16, LANES), low, jnp.float32).astype(jnp.bfloat16)
        spread_high = jnp.full((16, LANES), high, jnp.float32).astype(jnp.bfloat16)
        return (lane16 >= spread_low) & (lane16 < spread_high)

    def finish(q, u, straddle, tile, total, carry):
        total = total + jnp.where(u == straddle + 1, carry, 0.0)
        at = pl.ds(pl.multiple_of(tile * LANES, LANES), LANES)
        y_s[q, :, at] = total.astype(jnp.bfloat16)
        head_s[q, :, at] = total[:head_s.shape[1]].astype(jnp.bfloat16)
        return total

    def near_units():
        def unit(q, u, carry):
            len0, straddle, half, tile, base, k0 = unit_scalars(q, u)
            at = pl.ds(pl.multiple_of(tile * LANES, LANES), LANES)
            mine = own_half(half, tile, len0)
            rows, weights = [], []
            for d in range(5):
                where_row = place_t[base + 3 * d]
                begin = place_t[base + 3 * d + 1] + place_t[base + 3 * d + 2] * k0
                s = begin & 127
                first_tile = pl.multiple_of((begin >> 7) * LANES, LANES)
                row = [packed(plan(d, i, q, at)) for i in range(10)]
                weights += spread(mine, row[:4], row[4:8], row[8], row[9])
                three = ext_s[where_row, :, pl.ds(first_tile, 3 * LANES)]
                rows += [jnp.where(lane >= s, three[:, :LANES], three[:, 2 * LANES:]), three[:, LANES:2 * LANES]]
            total = jnp.dot(jnp.concatenate(rows, axis=1), jnp.concatenate(weights, axis=0),
                            preferred_element_type=jnp.float32)
            return finish(q, u, straddle, tile, total, carry)

        lax.fori_loop(0, tiles + 1, lambda u, carry: tuple(unit(q, u, carry[q]) for q in range(pairs)),
                      (jnp.zeros((fields, LANES), jnp.float32),) * pairs)

    def any_units():
        def unit(q, u, carry):
            len0, straddle, half, tile, base, _ = unit_scalars(q, u)
            at = pl.ds(pl.multiple_of(tile * LANES, LANES), LANES)
            mine = own_half(half, tile, len0)

            def window(w, total):
                rows, weights = [], []
                for d in range(5):
                    where_row = place_t[base + 3 * d]
                    place = (plan(d, 10, q, at) + (LANES - 1)).astype(jnp.int32) - w * WIN
                    block = jnp.clip(place >> 4, -2, 18)
                    rest = [packed(((place + o) & 15).astype(jnp.float32)) for o in range(4)]
                    weight = [packed(plan(d, o, q, at)) for o in range(4)]
                    weights += spread(mine, weight, rest, packed(block.astype(jnp.float32)), packed((block + 1).astype(jnp.float32)))
                    rows.append(ext_s[where_row, :, pl.ds(pl.multiple_of(w * WIN, WIN), WIN)])
                return total + jnp.dot(jnp.concatenate(rows, axis=1), jnp.concatenate(weights, axis=0),
                                       preferred_element_type=jnp.float32)

            total = lax.fori_loop(0, EW // WIN, window, jnp.zeros((fields, LANES), jnp.float32))
            return finish(q, u, straddle, tile, total, carry)

        lax.fori_loop(0, tiles + 1, lambda u, carry: tuple(unit(q, u, carry[q]) for q in range(pairs)),
                      (jnp.zeros((fields, LANES), jnp.float32),) * pairs)

    def deliver(out_ref):
        for f in range(groups):
            for q in range(pairs):
                out_ref[f, q] = y_s[q, pl.ds(levels * f, levels), pl.ds(0, pair_length)]

    steps.clear, steps.fill, steps.close, steps.weigh_all, steps.locate = clear, fill, close, weigh_all, locate
    steps.near_units, steps.any_units, steps.deliver, steps.near = near_units, any_units, deliver, near
    return steps


def stencil_scratch(pairs, fields, pair_length):
    padded = pl.cdiv(pair_length, LANES) * LANES
    return [
        pltpu.SMEM((30 * pairs,), jnp.int32),
        pltpu.VMEM((2 * (pairs + 4), fields, EW), jnp.bfloat16),
        pltpu.VMEM((pairs * ROWS, 8, padded), jnp.float32),
        pltpu.VMEM((pairs, fields, padded), jnp.bfloat16),
    ]


def near_kernel(sizes, half_rows, pair_length, grid_hbm, row_hbm, lon_hbm, lonf_hbm, latf_hbm,
                out_ref, head_ref, far_ref, before_hbm, after_hbm,
                before_s, own_s, after_s, row_s, lon_s, lonf_s, latf_s, place_t, ext_s, plan_s, y_s,
                in_sem, send_sem, recv_sem, keep_sem):
    along, across = sizes
    devices = along * across
    pairs = own_s.shape[1]
    me = lax.axis_index("aa") * across + lax.axis_index("ba")
    up = lax.rem(me + 1, devices)
    down = lax.rem(me + devices - 1, devices)

    def where(device):
        return (device // across, lax.rem(device, across))

    barrier = pltpu.get_barrier_semaphore()
    for device in (up, down):
        pl.semaphore_signal(barrier, inc=1, device_id=where(device), device_id_type=pl.DeviceIdType.MESH)
    loads = [pltpu.make_async_copy(src, dst, in_sem.at[i]) for i, (src, dst) in enumerate((
        (row_hbm, row_s), (lon_hbm, lon_s), (lonf_hbm, lonf_s), (latf_hbm, latf_s), (grid_hbm, own_s)))]
    for load in loads:
        load.start()
    pl.semaphore_wait(barrier, 2)
    sends = []
    for i, (begin, dst, device) in enumerate(((pairs - 2, before_s, up), (0, after_s, down))):
        sends.append(pltpu.make_async_remote_copy(
            src_ref=grid_hbm.at[:, pl.ds(begin, 2)], dst_ref=dst, send_sem=send_sem.at[i], recv_sem=recv_sem.at[i],
            device_id=where(device), device_id_type=pl.DeviceIdType.MESH))
        sends[-1].start()

    steps = stencil_steps(half_rows, pair_length, me * pairs, (before_s, own_s, after_s), row_s, lon_s, lonf_s, latf_s,
                          place_t, ext_s, plan_s, y_s, head_ref)
    steps.locate()
    steps.clear()
    for load in loads:
        load.wait()
    far_ref[0] = jnp.max(steps.weigh_all())
    for j in range(2, 2 + pairs):
        steps.fill(j)
    for j in range(2, 2 + pairs):
        steps.close(j)
    for send in sends:
        send.wait()
    keeps = [pltpu.make_async_copy(before_s, before_hbm, keep_sem.at[0]), pltpu.make_async_copy(after_s, after_hbm, keep_sem.at[1])]
    for keep in keeps:
        keep.start()
    for j in (0, 1, 2 + pairs, 3 + pairs):
        steps.fill(j)
    for j in (0, 1, 2 + pairs, 3 + pairs):
        steps.close(j)
    steps.near_units()
    steps.deliver(out_ref)
    for keep in keeps:
        keep.wait()


def far_kernel(half_rows, pair_length, far_ref, first_ref, before_hbm, grid_hbm, after_hbm, row_hbm, lon_hbm, lonf_hbm, latf_hbm,
               out_in, head_in, out_hbm, head_hbm,
               before_s, own_s, after_s, row_s, lon_s, lonf_s, latf_s, place_t, ext_s, plan_s, y_s, out_s, head_s, sem):
    del out_in, head_in

    @pl.when(far_ref[0] > 0)
    def _():
        for src, dst in ((before_hbm, before_s), (grid_hbm, own_s), (after_hbm, after_s), (row_hbm, row_s), (lon_hbm, lon_s),
                         (lonf_hbm, lonf_s), (latf_hbm, latf_s)):
            copy = pltpu.make_async_copy(src, dst, sem)
            copy.start()
            copy.wait()
        steps = stencil_steps(half_rows, pair_length, first_ref[0], (before_s, own_s, after_s), row_s, lon_s, lonf_s, latf_s,
                              place_t, ext_s, plan_s, y_s, head_s)
        steps.locate()
        steps.clear()
        steps.weigh_all()
        for j in range(steps.near):
            steps.fill(j)
        for j in range(steps.near):
            steps.close(j)
        steps.any_units()
        steps.deliver(out_s)
        for src, dst in ((out_s, out_hbm), (head_s, head_hbm)):
            copy = pltpu.make_async_copy(src, dst, sem)
            copy.start()
            copy.wait()


def interpolate(first, grid, dep_row, dep_lon, lon_frac, lat_frac, half_rows, spectral_fields, sizes):
    groups, pairs, levels, pair_length = grid.shape
    fields = groups * levels
    padded = pl.cdiv(pair_length, LANES) * LANES
    b16, f32, i32 = jnp.bfloat16, jnp.float32, jnp.int32
    vm, anywhere, scalars = (pl.BlockSpec(memory_space=m) for m in (pltpu.VMEM, pl.ANY, pltpu.SMEM))
    halo = jax.ShapeDtypeStruct((groups, 2, levels, pair_length), b16)
    head = jax.ShapeDtypeStruct((pairs, spectral_fields, padded), b16)
    full = jax.ShapeDtypeStruct(grid.shape, b16)
    local = [
        pltpu.VMEM(halo.shape, b16), pltpu.VMEM(grid.shape, b16), pltpu.VMEM(halo.shape, b16),
        pltpu.VMEM(dep_row.shape, i32), pltpu.VMEM(dep_lon.shape, i32), pltpu.VMEM(lon_frac.shape, f32), pltpu.VMEM(lat_frac.shape, f32),
    ] + stencil_scratch(pairs, fields, pair_length)
    out, first_fields, far, before, after = pl.pallas_call(
        functools.partial(near_kernel, sizes, half_rows, pair_length),
        out_shape=(full, head, jax.ShapeDtypeStruct((1,), i32), halo, halo),
        in_specs=[anywhere] * 5,
        out_specs=(vm, vm, scalars, anywhere, anywhere),
        scratch_shapes=local + [pltpu.SemaphoreType.DMA((5,)), pltpu.SemaphoreType.DMA((2,)), pltpu.SemaphoreType.DMA((2,)),
                                pltpu.SemaphoreType.DMA((2,))],
        compiler_params=pltpu.CompilerParams(collective_id=1, has_side_effects=True),
        name="near",
    )(grid, dep_row, dep_lon, lon_frac, lat_frac)
    return pl.pallas_call(
        functools.partial(far_kernel, half_rows, pair_length),
        out_shape=(full, head),
        in_specs=[scalars, scalars] + [anywhere] * 9,
        out_specs=(anywhere, anywhere),
        scratch_shapes=local + [pltpu.VMEM(full.shape, b16), pltpu.VMEM(head.shape, b16), pltpu.SemaphoreType.DMA],
        input_output_aliases={9: 0, 10: 1},
        name="far",
    )(far, first, before, grid, after, dep_row, dep_lon, lon_frac, lat_frac, out, first_fields)


COS = (1, -19.7392087, 64.9393842, -85.4565372, 60.2407014, -26.3960673, 7.77462739, -1.42354417)
SIN = (6.28318531, -41.3417022, 81.6052456, -76.7057546, 42.0572162, -15.0833301, 3.7717259, -0.609657301)


def cos_sin_turns(prod, length, inverse):
    turns = jnp.floor(prod * inverse + 0.5)
    t = (prod - turns * length) * inverse
    x = t * t
    c = jnp.full_like(x, COS[-1])
    for a in COS[-2::-1]:
        c = c * x + a
    s = jnp.full_like(x, SIN[-1])
    for a in SIN[-2::-1]:
        s = s * x + a
    return c, s * t


def transform_kernel(sizes, pair_length, y_ref, order_ref, waves_ref, legendre_hbm, out_ref,
                     table_s, sums_s, four_s, mix_s, stage_s, send_s, got_s, plain_s, anti_s, kept_s, keptanti_s, turn_s, legendre_s,
                     legendre_sem, own_sem, send_sem, recv_sem):
    along, across = sizes
    devices = along * across
    pairs = y_ref.shape[0]
    slots = legendre_s.shape[0]
    half_rows = slots * devices
    rows = 2 * pairs
    tiles = pl.cdiv(pair_length, LANES)
    my_a = lax.axis_index("aa")
    my_b = lax.axis_index("ba")
    me = my_a * across + my_b
    first = me * pairs
    north = me < devices // 2
    parts = 8

    weights_in = pltpu.make_async_copy(legendre_hbm, legendre_s, legendre_sem)
    weights_in.start()

    columns = [lax.rem(my_b + i, across) for i in range(across)]

    def partners(act):
        for b in range(1, across):
            act(my_a, columns[b])

        def others(i, _):
            a = lax.rem(my_a + i, along)
            for b in range(across):
                act(a, columns[b])
            return 0

        lax.fori_loop(1, along, others, 0)

    barrier = pltpu.get_barrier_semaphore()
    partners(lambda a, b: pl.semaphore_signal(barrier, inc=1, device_id=(a, b), device_id_type=pl.DeviceIdType.MESH))

    def one(i, _):
        q = i // 2
        half = i - 2 * q
        pair = first + q
        inner = jnp.where(north, pair, half_rows - 1 - pair)
        len0 = 16 + 4 * (half_rows // 2 - inner)
        start = jnp.where(half == 1, len0, 0)
        whole = jnp.where(half == 1, 16 + 4 * (half_rows // 2 + 1 + inner), len0)
        length = jnp.full((1, LANES), whole, jnp.int32).astype(jnp.float32)
        inverse = 1.0 / length

        def line(n):
            return lax.broadcasted_iota(jnp.int32, (n, LANES), 0)

        def waves(n, w):
            return lax.broadcasted_iota(jnp.int32, (n, LANES), 1) + w * LANES

        for w in range(slots):
            fine_c, fine_s = cos_sin_turns((waves(16, w) * line(16)).astype(jnp.float32), length, inverse)
            step_c, step_s = cos_sin_turns((waves(8, w) * (16 * line(8))).astype(jnp.float32), length, inverse)
            for a in range(8):
                ca, sa = step_c[a:a + 1], step_s[a:a + 1]
                table_s[pl.ds(16 * a, 16), pl.ds(w * LANES, LANES)] = (ca * fine_c - sa * fine_s).astype(jnp.bfloat16)
                table_s[pl.ds(16 * a, 16), pl.ds(half_rows + w * LANES, LANES)] = (sa * fine_c + ca * fine_s).astype(jnp.bfloat16)
        lane = lax.broadcasted_iota(jnp.int32, (parts, LANES), 1)
        blocks = []
        for t in range(tiles):
            col = lane + t * LANES
            mine = (col >= start) & (col < start + whole)
            blocks.append(jnp.where(mine, y_ref[q, :, pl.ds(t * LANES, LANES)].astype(jnp.float32)[:parts], 0.0))
        stacked = jnp.concatenate(blocks, axis=0).astype(jnp.bfloat16)
        sums_s[...] = jnp.dot(stacked, table_s[...], preferred_element_type=jnp.float32)
        place = 2 * jnp.where(north, q, pairs - 1 - q) + half
        for w in range(slots):
            tile_c, tile_s = cos_sin_turns((waves(24, w) * (LANES * line(24) - start)).astype(jnp.float32), length, inverse)
            real = jnp.zeros((parts, LANES), jnp.float32)
            imag = jnp.zeros((parts, LANES), jnp.float32)
            for t in range(tiles):
                c = sums_s[pl.ds(parts * t, parts), pl.ds(w * LANES, LANES)]
                s = sums_s[pl.ds(parts * t, parts), pl.ds(half_rows + w * LANES, LANES)]
                tc, ts = tile_c[t:t + 1], tile_s[t:t + 1]
                real = real + (tc * c - ts * s)
                imag = imag - (ts * c + tc * s)
            keep = jnp.where(2 * waves(1, w) < whole, inverse, 0.0)
            four_s[pl.ds(pl.multiple_of(place * 16, 16), 16), pl.ds(w * LANES, LANES)] = jnp.concatenate(
                [real * keep, imag * keep], axis=0).astype(jnp.bfloat16)
        return 0

    lax.fori_loop(0, rows, one, 0)

    hot = (lax.broadcasted_iota(jnp.int32, (half_rows, half_rows), 0) == order_ref[...]).astype(jnp.float32).astype(jnp.bfloat16)
    moved = jnp.dot(four_s[...], hot, preferred_element_type=jnp.float32)
    mix_s[...] = jnp.zeros_like(mix_s)
    for r in range(8):
        for s in range(slots):
            mix_s[r, pl.ds(16 * s, 16), :] = moved[16 * r:16 * r + 16, s * LANES:(s + 1) * LANES]
        if r < slots:
            for e in range(rows - 8):
                mix_s[r, pl.ds(16 * (slots + e), 16), :] = moved[16 * (8 + e):16 * (8 + e) + 16, r * LANES:(r + 1) * LANES]
        stage_s[pl.ds(r, LANES, stride=8), :] = mix_s[r].T
    send_s[...] = stage_s[...].astype(jnp.bfloat16).reshape(send_s.shape)

    pl.semaphore_wait(barrier, devices - 1)

    def post(a, b):
        pltpu.make_async_remote_copy(
            src_ref=send_s.at[a * across + b], dst_ref=got_s.at[me], send_sem=send_sem, recv_sem=recv_sem,
            device_id=(a, b), device_id_type=pl.DeviceIdType.MESH).start()

    partners(post)
    own = pltpu.make_async_copy(send_s.at[me], got_s.at[me], own_sem)
    own.start()

    src = lax.broadcasted_iota(jnp.int32, (slots * LANES, 2 * LANES), 0)
    dst = lax.broadcasted_iota(jnp.int32, (slots * LANES, 2 * LANES), 1)
    unfold = (((dst & 127) >> 4) == (src >> 7)) & ((src & 127) == 16 * (slots + (dst >> 7)) + (dst & 15))
    unfold = unfold.astype(jnp.float32).astype(jnp.bfloat16)
    slot_of = (lax.broadcasted_iota(jnp.int32, (half_rows, LANES), 1) >> 4).astype(jnp.float32).astype(jnp.bfloat16)
    rest = pl.ds(0, devices - 1)
    every = pltpu.make_async_remote_copy(
        src_ref=send_s.at[rest], dst_ref=got_s.at[rest], send_sem=send_sem, recv_sem=recv_sem,
        device_id=(my_a, columns[1]), device_id_type=pl.DeviceIdType.MESH)
    every.wait_send()
    every.wait_recv()
    own.wait()

    for d in range(devices // 2):
        n = got_s[d].astype(jnp.float32)
        o = got_s[devices - 1 - d].astype(jnp.float32)
        plain_s[pl.ds(rows * d, 8), :] = n + o
        anti_s[pl.ds(rows * d, 8), :] = n - o
        kept_s[pl.ds(8 * d, 8), :] = n + o
        keptanti_s[pl.ds(8 * d, 8), :] = n - o
    weights_in.wait()
    for par, wide, kept in ((0, plain_s, kept_s), (1, anti_s, keptanti_s)):
        folded = jnp.concatenate([kept[pl.ds(s, devices // 2, stride=8), :] for s in range(slots)], axis=1).astype(jnp.bfloat16)
        extra = jnp.dot(folded, unfold, preferred_element_type=jnp.float32)
        for e in range(rows - 8):
            wide[pl.ds(8 + e, devices // 2, stride=rows), :] = extra[:, e * LANES:(e + 1) * LANES]
        values = wide[...].astype(jnp.bfloat16)
        zero = jnp.zeros_like(values)
        picked = jnp.concatenate([jnp.where(slot_of == jnp.bfloat16(s), values, zero) for s in range(slots)], axis=0)
        table = jnp.concatenate([legendre_s[s, par] for s in range(slots)], axis=1)
        turn_s[pl.ds(par, half_rows // 2, stride=2), :] = jnp.dot(table, picked, preferred_element_type=jnp.float32)
    z = turn_s[...].T
    degree = lax.broadcasted_iota(jnp.int32, (16, half_rows), 1)
    for s in range(slots):
        limit = half_rows - waves_ref[me * slots + s]
        out_ref[s] = jnp.where(degree < limit, z[16 * s:16 * s + 16], 0.0)


def transform(y, order, waves, legendre, half_rows, pair_length, sizes):
    pairs = y.shape[0]
    slots = legendre.shape[0]
    tiles = pl.cdiv(pair_length, LANES)
    vm = pl.BlockSpec(memory_space=pltpu.VMEM)
    f32, b16 = jnp.float32, jnp.bfloat16
    return pl.pallas_call(
        functools.partial(transform_kernel, sizes, pair_length),
        out_shape=jax.ShapeDtypeStruct((slots, 16, half_rows), f32),
        in_specs=[vm, vm, pl.BlockSpec(memory_space=pltpu.SMEM), pl.BlockSpec(memory_space=pl.ANY)],
        out_specs=vm,
        scratch_shapes=[
            pltpu.VMEM((LANES, 2 * half_rows), b16),
            pltpu.VMEM((8 * tiles, 2 * half_rows), f32),
            pltpu.VMEM((32 * pairs, half_rows), b16),
            pltpu.VMEM((8, LANES, LANES), f32),
            pltpu.VMEM((8 * LANES, LANES), f32),
            pltpu.VMEM((LANES, 8, LANES), b16),
            pltpu.VMEM((LANES, 8, LANES), b16),
            pltpu.VMEM((half_rows, LANES), f32),
            pltpu.VMEM((half_rows, LANES), f32),
            pltpu.VMEM((8 * LANES // 2, LANES), f32),
            pltpu.VMEM((8 * LANES // 2, LANES), f32),
            pltpu.VMEM((half_rows, LANES), f32),
            pltpu.VMEM(legendre.shape, b16),
            pltpu.SemaphoreType.DMA, pltpu.SemaphoreType.DMA, pltpu.SemaphoreType.DMA, pltpu.SemaphoreType.DMA,
        ],
        compiler_params=pltpu.CompilerParams(collective_id=0, has_side_effects=True),
        name="transform",
    )(y, order, waves, legendre)


def on_device(grid, dep_row, dep_lon, lon_frac, lat_frac, wave_slot, legendre):
    half_rows = wave_slot.shape[0]
    _, levels, pairs, pair_length = grid.shape
    slots = legendre.shape[0]
    axes = ("aa", "ba")
    sizes = (lax.axis_size("aa"), lax.axis_size("ba"))
    devices = sizes[0] * sizes[1]
    first = (lax.axis_index(axes) * pairs).astype(jnp.int32).reshape(1)
    own = jnp.transpose(grid, (0, 2, 1, 3))
    order = jnp.transpose(wave_slot.reshape(devices, slots)).reshape(1, half_rows)
    out, head = interpolate(first, own, dep_row, jnp.transpose(dep_lon, (1, 0, 2)), jnp.transpose(lon_frac, (1, 0, 2)),
                            lat_frac, half_rows, 2 * levels, sizes)
    result = transform(head, order, wave_slot, legendre, half_rows, pair_length, sizes)
    return (jnp.transpose(out, (0, 2, 1, 3)), jnp.transpose(result, (1, 0, 2)))


def solution(mesh):
    return jax.shard_map(
        on_device,
        mesh=mesh,
        in_specs=(
            P(None, None, ("aa", "ba"), None),
            P(("aa", "ba"), None),
            P(None, ("aa", "ba"), None),
            P(None, ("aa", "ba"), None),
            P(("aa", "ba"), None),
            P(),
            P(("aa", "ba"), None, None, None),
        ),
        out_specs=(P(None, None, ("aa", "ba"), None), P(None, ("aa", "ba"), None)),
        check_vma=False,
    )
```

```python
import functools

import jax
import jax.numpy as jnp
from jax import lax
from jax.experimental import pallas as pl
from jax.experimental.pallas import tpu as pltpu
from jax.sharding import PartitionSpec as P

LANES = 128
WIN = 256
ETILES = 24
EW = ETILES * LANES
MARGIN = 60
ROWS = 11
NOWHERE = 192.0


def row_place(global_row, half_rows):
    northern = global_row < half_rows
    number = jnp.where(northern, global_row + 1, 2 * half_rows - global_row)
    second = number > half_rows // 2
    inner = jnp.where(second, number - half_rows // 2 - 1, half_rows // 2 - number)
    begin = jnp.where(second, 16 + 4 * (half_rows // 2 - inner), 0)
    return jnp.where(northern, inner, half_rows - 1 - inner), begin, 16 + 4 * number


def cubic(t):
    return (
        -t * (t - 1.0) * (t - 2.0) * (1.0 / 6.0),
        (t + 1.0) * (t - 1.0) * (t - 2.0) * 0.5,
        -(t + 1.0) * t * (t - 2.0) * 0.5,
        (t + 1.0) * t * (t - 1.0) * (1.0 / 6.0),
    )


class Stencil:
    pass


def stencil_steps(half_rows, pair_length, first, sources, row_ref, lon_ref, lonf_ref, latf_ref, place_t, ext_s, plan_s, y_s, head_s):
    groups, pairs, levels, _ = sources[1].shape
    fields = groups * levels
    near = pairs + 4
    tiles = pl.cdiv(pair_length, LANES)
    steps = Stencil()

    lane = lax.broadcasted_iota(jnp.int32, (fields, LANES), 1)

    def half_lengths(pair):
        inner = jnp.where(pair < half_rows // 2, pair, half_rows - 1 - pair)
        return 16 + 4 * (half_rows // 2 - inner), 16 + 4 * (half_rows // 2 + 1 + inner)

    def clear():
        ext_s[:, :, pl.ds(0, LANES)] = jnp.zeros((2 * near, fields, LANES), jnp.bfloat16)
        ext_s[:, :, pl.ds(tiles * LANES, EW - tiles * LANES)] = jnp.zeros((2 * near, fields, EW - tiles * LANES), jnp.bfloat16)

    def fill(j):
        ref, at = (sources[0], j) if j < 2 else ((sources[1], j - 2) if j < 2 + pairs else (sources[2], j - 2 - pairs))
        for f in range(groups):
            src = ref[f, at]
            for copy in range(2):
                ext_s[2 * j + copy, pl.ds(levels * f, levels), pl.ds(LANES, pair_length)] = src

    def wrap(copy, tile, shift, low, edge):
        at = pl.ds(pl.multiple_of(tile * LANES, LANES), LANES)
        begin = tile * LANES + shift
        two = ext_s[copy, :, pl.ds(pl.multiple_of((begin >> 7) * LANES, LANES), 2 * LANES)].astype(jnp.float32)
        moved = pltpu.roll(two, (2 * LANES - (begin & 127)) & 255, 1)[:, :LANES]
        spot = lane + tile * LANES
        beyond = spot < edge if low else spot >= edge
        return copy, at, jnp.where(beyond, moved, ext_s[copy, :, at].astype(jnp.float32)).astype(jnp.bfloat16)

    def close(j):
        len0, len1 = half_lengths(first + j - 2)
        wraps = []
        for half in range(2):
            start, length = (len0, len1) if half else (0, len0)
            for i in range(1 + half):
                wraps.append(wrap(2 * j + half, ((start >> 7) if half else 0) + i, length, True, start + LANES))
            for i in range(3):
                wraps.append(wrap(2 * j + half, ((start + length) >> 7) + 1 + i, -length, False, start + length + LANES))
        for copy, at, tile in wraps:
            ext_s[copy, :, at] = tile

    sub8 = lax.broadcasted_iota(jnp.int32, (8, LANES), 0)
    lane8 = lax.broadcasted_iota(jnp.int32, (8, LANES), 1)

    def weigh(tile, fits, width=LANES):
        at = pl.ds(pl.multiple_of(tile * LANES, LANES), LANES)
        some = pl.ds(pl.multiple_of(tile * LANES, LANES), width)
        col = tile * LANES + lane8
        inside = col < pair_length

        def wide(x):
            if width < LANES:
                x = jnp.concatenate([x, jnp.zeros((x.shape[0], LANES - width), x.dtype)], axis=1)
            return x

        for q in range(pairs):
            pair = first + q
            northern = pair < half_rows // 2
            len0, _ = half_lengths(pair)
            second = col >= len0
            inner = jnp.where(northern, pair, half_rows - 1 - pair)

            def base_of(number):
                return jnp.clip(jnp.where(northern, number - 1, 2 * half_rows - number) - 2, 0, 2 * half_rows - 4)

            base = jnp.where(second, base_of(half_rows // 2 + 1 + inner), base_of(half_rows // 2 - inner))
            later = jnp.broadcast_to(wide(row_ref[pl.ds(q, 1), some]), (8, LANES)) > base
            base_k = jnp.where(second, jnp.maximum(tile * LANES - len0, 0), tile * LANES) - MARGIN
            lon = wide(lon_ref[q, :, some])
            lon = jnp.concatenate([lon, lon], axis=0)
            lon = jnp.where(later, pltpu.roll(lon, 1, 0), lon)
            frac = wide(lonf_ref[q, :, some])
            frac = jnp.concatenate([frac, frac], axis=0)
            frac = jnp.where(later, pltpu.roll(frac, 1, 0), frac)
            latw = cubic(jnp.broadcast_to(wide(latf_ref[pl.ds(q, 1), some]), (8, LANES)))
            r = jnp.where(later, sub8 - 1, sub8)
            lat = jnp.zeros((8, LANES), jnp.float32)
            for i in range(4):
                lat = jnp.where(inside & (r == i), latw[i], lat)
            _, begin, length = row_place(jnp.minimum(base + sub8, 2 * half_rows - 1), half_rows)
            rel = lon - 1 - base_k
            rel = jnp.where(rel < 0, rel + length, jnp.where(rel >= length, rel - length, rel))
            short = length <= WIN - 4
            rel = jnp.where(short, lon, rel)
            bad = (lat != 0.0) & ((rel < 0) | (rel > WIN - 4))
            fits = jnp.maximum(fits, bad.astype(jnp.int32))
            place = ((begin + jnp.where(short, -1, base_k) + LANES) & 127) + rel
            block = (place >> 4) & 15
            ws = cubic(frac)
            for o in range(4):
                plan_s[q * ROWS + o, :, at] = lat * ws[o]
                plan_s[q * ROWS + 4 + o, :, at] = ((place + o) & 15).astype(jnp.float32)
            plan_s[q * ROWS + 8, :, at] = block.astype(jnp.float32)
            plan_s[q * ROWS + 9, :, at] = ((block + 1) & 15).astype(jnp.float32)
            plan_s[q * ROWS + 10, :, at] = (lon + begin).astype(jnp.float32)
        return fits

    def weigh_all():
        worst = lax.fori_loop(0, pair_length // LANES, weigh, jnp.zeros((8, LANES), jnp.int32))
        if pair_length % LANES:
            worst = weigh(tiles - 1, worst, pair_length % LANES)
        return worst

    node = lax.broadcasted_iota(jnp.int32, (16, LANES), 0).astype(jnp.float32).astype(jnp.bfloat16)
    zero16 = jnp.zeros((16, LANES), jnp.bfloat16)

    def spread(mine, weight, rest, block, after):
        v = zero16
        for o in (3, 2, 1, 0):
            v = jnp.where(node == rest[o], weight[o], v)
        block = jnp.where(mine, jnp.where(node < rest[0], after, block), jnp.bfloat16(NOWHERE))
        return [jnp.where(block == jnp.bfloat16(a), v, zero16) for a in range(WIN // 16)]

    def plan(d, i, q, at):
        return jnp.broadcast_to(plan_s[q * ROWS + i, pl.ds(d, 1), at], (16, LANES))

    def packed(x):
        return x.astype(jnp.bfloat16)

    def locate():
        for q in range(pairs):
            pair = first + q
            northern = pair < half_rows // 2
            inner = jnp.where(northern, pair, half_rows - 1 - pair)
            for half in range(2):
                number = half_rows // 2 + 1 + inner if half else half_rows // 2 - inner
                g = jnp.where(northern, number - 1, 2 * half_rows - number)
                base = jnp.clip(g - 2, 0, 2 * half_rows - 4)
                for d in range(5):
                    pair_row, begin, length = row_place(jnp.minimum(base + d, 2 * half_rows - 1), half_rows)
                    short = length <= WIN - 4
                    copy = 2 * jnp.clip(pair_row - first + 2, 0, near - 1) + (begin > 0).astype(jnp.int32)
                    at = 3 * ((2 * q + half) * 5 + d)
                    place_t[at] = copy
                    place_t[at + 1] = begin + LANES + jnp.where(short, -1, -MARGIN)
                    place_t[at + 2] = jnp.where(short, 0, 1)

    def unit_scalars(q, u):
        len0, _ = half_lengths(first + q)
        straddle = len0 >> 7
        half = (u > straddle).astype(jnp.int32)
        tile = u - half
        k0 = jnp.where(half == 1, jnp.maximum(tile * LANES - len0, 0), tile * LANES)
        return len0, straddle, half, tile, 15 * (2 * q + half), k0

    lane16 = lax.broadcasted_iota(jnp.int32, (16, LANES), 1).astype(jnp.float32).astype(jnp.bfloat16)

    def own_half(half, tile, len0):
        edge = jnp.clip(len0 - tile * LANES, 0, LANES)
        low = jnp.where(half == 1, edge, 0).astype(jnp.float32)
        high = jnp.where(half == 1, LANES, edge).astype(jnp.float32)
        spread_low = jnp.full((16, LANES), low, jnp.float32).astype(jnp.bfloat16)
        spread_high = jnp.full((16, LANES), high, jnp.float32).astype(jnp.bfloat16)
        return (lane16 >= spread_low) & (lane16 < spread_high)

    def finish(q, u, straddle, tile, total, carry):
        total = total + jnp.where(u == straddle + 1, carry, 0.0)
        at = pl.ds(pl.multiple_of(tile * LANES, LANES), LANES)
        y_s[q, :, at] = total.astype(jnp.bfloat16)
        head_s[q, :, at] = total[:head_s.shape[1]].astype(jnp.bfloat16)
        return total

    def near_units():
        def unit(q, u, carry):
            len0, straddle, half, tile, base, k0 = unit_scalars(q, u)
            at = pl.ds(pl.multiple_of(tile * LANES, LANES), LANES)
            mine = own_half(half, tile, len0)
            rows, weights = [], []
            for d in range(5):
                where_row = place_t[base + 3 * d]
                begin = place_t[base + 3 * d + 1] + place_t[base + 3 * d + 2] * k0
                s = begin & 127
                first_tile = pl.multiple_of((begin >> 7) * LANES, LANES)
                row = [packed(plan(d, i, q, at)) for i in range(10)]
                weights += spread(mine, row[:4], row[4:8], row[8], row[9])
                three = ext_s[where_row, :, pl.ds(first_tile, 3 * LANES)]
                rows += [jnp.where(lane >= s, three[:, :LANES], three[:, 2 * LANES:]), three[:, LANES:2 * LANES]]
            total = jnp.dot(jnp.concatenate(rows, axis=1), jnp.concatenate(weights, axis=0),
                            preferred_element_type=jnp.float32)
            return finish(q, u, straddle, tile, total, carry)

        lax.fori_loop(0, tiles + 1, lambda u, carry: tuple(unit(q, u, carry[q]) for q in range(pairs)),
                      (jnp.zeros((fields, LANES), jnp.float32),) * pairs)

    def any_units():
        def unit(q, u, carry):
            len0, straddle, half, tile, base, _ = unit_scalars(q, u)
            at = pl.ds(pl.multiple_of(tile * LANES, LANES), LANES)
            mine = own_half(half, tile, len0)

            def window(w, total):
                rows, weights = [], []
                for d in range(5):
                    where_row = place_t[base + 3 * d]
                    place = (plan(d, 10, q, at) + (LANES - 1)).astype(jnp.int32) - w * WIN
                    block = jnp.clip(place >> 4, -2, 18)
                    rest = [packed(((place + o) & 15).astype(jnp.float32)) for o in range(4)]
                    weight = [packed(plan(d, o, q, at)) for o in range(4)]
                    weights += spread(mine, weight, rest, packed(block.astype(jnp.float32)), packed((block + 1).astype(jnp.float32)))
                    rows.append(ext_s[where_row, :, pl.ds(pl.multiple_of(w * WIN, WIN), WIN)])
                return total + jnp.dot(jnp.concatenate(rows, axis=1), jnp.concatenate(weights, axis=0),
                                       preferred_element_type=jnp.float32)

            total = lax.fori_loop(0, EW // WIN, window, jnp.zeros((fields, LANES), jnp.float32))
            return finish(q, u, straddle, tile, total, carry)

        lax.fori_loop(0, tiles + 1, lambda u, carry: tuple(unit(q, u, carry[q]) for q in range(pairs)),
                      (jnp.zeros((fields, LANES), jnp.float32),) * pairs)

    def deliver(out_ref):
        for f in range(groups):
            for q in range(pairs):
                out_ref[f, q] = y_s[q, pl.ds(levels * f, levels), pl.ds(0, pair_length)]

    steps.clear, steps.fill, steps.close, steps.weigh_all, steps.locate = clear, fill, close, weigh_all, locate
    steps.near_units, steps.any_units, steps.deliver, steps.near = near_units, any_units, deliver, near
    return steps


def stencil_scratch(pairs, fields, pair_length):
    padded = pl.cdiv(pair_length, LANES) * LANES
    return [
        pltpu.SMEM((30 * pairs,), jnp.int32),
        pltpu.VMEM((2 * (pairs + 4), fields, EW), jnp.bfloat16),
        pltpu.VMEM((pairs * ROWS, 8, padded), jnp.float32),
        pltpu.VMEM((pairs, fields, padded), jnp.bfloat16),
    ]


def by_slot_then_device(wave, devices):
    count = wave.shape[1]
    slots = count // devices
    wanted = lax.broadcasted_iota(jnp.int32, (1, count), 1)
    wanted = slots * (wanted % devices) + wanted // devices
    moves = (lax.broadcasted_iota(jnp.int32, (count, count), 0) == wanted).astype(jnp.float32).astype(jnp.bfloat16)
    high, low = wave // 8, wave % 8
    sub = lax.broadcasted_iota(jnp.int32, (16, count), 0)
    digits = jnp.where(sub == 0, high, jnp.where(sub == 1, low, 0)).astype(jnp.float32).astype(jnp.bfloat16)
    moved = jnp.dot(digits, moves, preferred_element_type=jnp.float32)
    return (8.0 * moved[0:1] + moved[1:2]).astype(jnp.int32)


def near_kernel(sizes, half_rows, pair_length, grid_hbm, row_hbm, lon_hbm, lonf_hbm, latf_hbm, wave_ref,
                out_ref, head_ref, far_ref, before_hbm, after_hbm, order_ref,
                before_s, own_s, after_s, row_s, lon_s, lonf_s, latf_s, place_t, ext_s, plan_s, y_s,
                in_sem, send_sem, recv_sem, keep_sem):
    along, across = sizes
    devices = along * across
    pairs = own_s.shape[1]
    me = lax.axis_index("aa") * across + lax.axis_index("ba")
    up = lax.rem(me + 1, devices)
    down = lax.rem(me + devices - 1, devices)

    def where(device):
        return (device // across, lax.rem(device, across))

    barrier = pltpu.get_barrier_semaphore()
    for device in (up, down):
        pl.semaphore_signal(barrier, inc=1, device_id=where(device), device_id_type=pl.DeviceIdType.MESH)
    loads = [pltpu.make_async_copy(src, dst, in_sem.at[i]) for i, (src, dst) in enumerate((
        (row_hbm, row_s), (lon_hbm, lon_s), (lonf_hbm, lonf_s), (latf_hbm, latf_s), (grid_hbm, own_s)))]
    for load in loads:
        load.start()
    pl.semaphore_wait(barrier, 2)
    sends = []
    for i, (begin, dst, device) in enumerate(((pairs - 2, before_s, up), (0, after_s, down))):
        sends.append(pltpu.make_async_remote_copy(
            src_ref=grid_hbm.at[:, pl.ds(begin, 2)], dst_ref=dst, send_sem=send_sem.at[i], recv_sem=recv_sem.at[i],
            device_id=where(device), device_id_type=pl.DeviceIdType.MESH))
        sends[-1].start()

    steps = stencil_steps(half_rows, pair_length, me * pairs, (before_s, own_s, after_s), row_s, lon_s, lonf_s, latf_s,
                          place_t, ext_s, plan_s, y_s, head_ref)
    steps.locate()
    steps.clear()
    for load in loads:
        load.wait()
    far_ref[0] = jnp.max(steps.weigh_all())
    for j in range(2, 2 + pairs):
        steps.fill(j)
    for j in range(2, 2 + pairs):
        steps.close(j)
    order_ref[...] = by_slot_then_device(wave_ref[...].reshape(1, half_rows), devices)
    for send in sends:
        send.wait()
    keeps = [pltpu.make_async_copy(before_s, before_hbm, keep_sem.at[0]), pltpu.make_async_copy(after_s, after_hbm, keep_sem.at[1])]
    for keep in keeps:
        keep.start()
    for j in (0, 1, 2 + pairs, 3 + pairs):
        steps.fill(j)
    for j in (0, 1, 2 + pairs, 3 + pairs):
        steps.close(j)
    steps.near_units()
    steps.deliver(out_ref)
    for keep in keeps:
        keep.wait()


def far_kernel(half_rows, pair_length, far_ref, first_ref, before_hbm, grid_hbm, after_hbm, row_hbm, lon_hbm, lonf_hbm, latf_hbm,
               out_in, head_in, out_hbm, head_hbm,
               before_s, own_s, after_s, row_s, lon_s, lonf_s, latf_s, place_t, ext_s, plan_s, y_s, out_s, head_s, sem):
    del out_in, head_in

    @pl.when(far_ref[0] > 0)
    def _():
        for src, dst in ((before_hbm, before_s), (grid_hbm, own_s), (after_hbm, after_s), (row_hbm, row_s), (lon_hbm, lon_s),
                         (lonf_hbm, lonf_s), (latf_hbm, latf_s)):
            copy = pltpu.make_async_copy(src, dst, sem)
            copy.start()
            copy.wait()
        steps = stencil_steps(half_rows, pair_length, first_ref[0], (before_s, own_s, after_s), row_s, lon_s, lonf_s, latf_s,
                              place_t, ext_s, plan_s, y_s, head_s)
        steps.locate()
        steps.clear()
        steps.weigh_all()
        for j in range(steps.near):
            steps.fill(j)
        for j in range(steps.near):
            steps.close(j)
        steps.any_units()
        steps.deliver(out_s)
        for src, dst in ((out_s, out_hbm), (head_s, head_hbm)):
            copy = pltpu.make_async_copy(src, dst, sem)
            copy.start()
            copy.wait()


def interpolate(first, grid, dep_row, dep_lon, lon_frac, lat_frac, wave_slot, half_rows, spectral_fields, sizes):
    groups, pairs, levels, pair_length = grid.shape
    fields = groups * levels
    padded = pl.cdiv(pair_length, LANES) * LANES
    b16, f32, i32 = jnp.bfloat16, jnp.float32, jnp.int32
    vm, anywhere, scalars = (pl.BlockSpec(memory_space=m) for m in (pltpu.VMEM, pl.ANY, pltpu.SMEM))
    halo = jax.ShapeDtypeStruct((groups, 2, levels, pair_length), b16)
    head = jax.ShapeDtypeStruct((pairs, spectral_fields, padded), b16)
    full = jax.ShapeDtypeStruct(grid.shape, b16)
    local = [
        pltpu.VMEM(halo.shape, b16), pltpu.VMEM(grid.shape, b16), pltpu.VMEM(halo.shape, b16),
        pltpu.VMEM(dep_row.shape, i32), pltpu.VMEM(dep_lon.shape, i32), pltpu.VMEM(lon_frac.shape, f32), pltpu.VMEM(lat_frac.shape, f32),
    ] + stencil_scratch(pairs, fields, pair_length)
    out, first_fields, far, before, after, order = pl.pallas_call(
        functools.partial(near_kernel, sizes, half_rows, pair_length),
        out_shape=(full, head, jax.ShapeDtypeStruct((1,), i32), halo, halo, jax.ShapeDtypeStruct((1, half_rows), i32)),
        in_specs=[anywhere] * 5 + [vm],
        out_specs=(vm, vm, scalars, anywhere, anywhere, vm),
        scratch_shapes=local + [pltpu.SemaphoreType.DMA((5,)), pltpu.SemaphoreType.DMA((2,)), pltpu.SemaphoreType.DMA((2,)),
                                pltpu.SemaphoreType.DMA((2,))],
        compiler_params=pltpu.CompilerParams(collective_id=1, has_side_effects=True),
        name="near",
    )(grid, dep_row, dep_lon, lon_frac, lat_frac, wave_slot)
    out, first_fields = pl.pallas_call(
        functools.partial(far_kernel, half_rows, pair_length),
        out_shape=(full, head),
        in_specs=[scalars, scalars] + [anywhere] * 9,
        out_specs=(anywhere, anywhere),
        scratch_shapes=local + [pltpu.VMEM(full.shape, b16), pltpu.VMEM(head.shape, b16), pltpu.SemaphoreType.DMA],
        input_output_aliases={9: 0, 10: 1},
        name="far",
    )(far, first, before, grid, after, dep_row, dep_lon, lon_frac, lat_frac, out, first_fields)
    return out, first_fields, order

WIDE = 256

COS = (1, -19.7392087, 64.9393842, -85.4565372, 60.2407014, -26.3960673, 7.77462739, -1.42354417)
SIN = (6.28318531, -41.3417022, 81.6052456, -76.7057546, 42.0572162, -15.0833301, 3.7717259, -0.609657301)


def cos_sin_turns(prod, length, inverse):
    turns = jnp.floor(prod * inverse + 0.5)
    t = (prod - turns * length) * inverse
    x = t * t
    c = jnp.full_like(x, COS[-1])
    for a in COS[-2::-1]:
        c = c * x + a
    s = jnp.full_like(x, SIN[-1])
    for a in SIN[-2::-1]:
        s = s * x + a
    return c, s * t


def transform_kernel(sizes, pair_length, y_ref, order_ref, waves_ref, legendre_hbm, out_ref,
                     table_s, sums_s, back_s, turn_c, turn_n, four_s, mix_s, stage_s, send_s, got_s, plain_s, anti_s, kept_s, keptanti_s, turn_s, legendre_s,
                     legendre_sem, own_sem, send_sem, recv_sem):
    along, across = sizes
    devices = along * across
    pairs = y_ref.shape[0]
    slots = legendre_s.shape[0]
    half_rows = slots * devices
    rows = 2 * pairs
    tiles = pl.cdiv(pair_length, LANES)
    my_a = lax.axis_index("aa")
    my_b = lax.axis_index("ba")
    me = my_a * across + my_b
    first = me * pairs
    north = me < devices // 2
    parts = 8
    wides = pl.cdiv(tiles * LANES, WIDE)

    weights_in = pltpu.make_async_copy(legendre_hbm, legendre_s, legendre_sem)
    weights_in.start()

    columns = [lax.rem(my_b + i, across) for i in range(across)]

    def partners(act):
        for b in range(1, across):
            act(my_a, columns[b])

        def others(i, _):
            a = lax.rem(my_a + i, along)
            for b in range(across):
                act(a, columns[b])
            return 0

        lax.fori_loop(1, along, others, 0)

    barrier = pltpu.get_barrier_semaphore()
    partners(lambda a, b: pl.semaphore_signal(barrier, inc=1, device_id=(a, b), device_id_type=pl.DeviceIdType.MESH))

    def one(i, _):
        q = i // 2
        half = i - 2 * q
        pair = first + q
        inner = jnp.where(north, pair, half_rows - 1 - pair)
        len0 = 16 + 4 * (half_rows // 2 - inner)
        start = jnp.where(half == 1, len0, 0)
        whole = jnp.where(half == 1, 16 + 4 * (half_rows // 2 + 1 + inner), len0)
        length = jnp.full((1, LANES), whole, jnp.int32).astype(jnp.float32)
        inverse = 1.0 / length

        def line(n):
            return lax.broadcasted_iota(jnp.int32, (n, LANES), 0)

        wave = lax.broadcasted_iota(jnp.int32, (16, LANES), 1)
        fine_c, fine_s = cos_sin_turns((wave * line(16)).astype(jnp.float32), length, inverse)
        step_c, step_s = cos_sin_turns((wave * (16 * line(16))).astype(jnp.float32), length, inverse)
        for a in range(WIDE // 16):
            ca, sa = step_c[a:a + 1], step_s[a:a + 1]
            cosine = ca * fine_c - sa * fine_s
            sine = sa * fine_c + ca * fine_s
            top, bottom = pl.ds(16 * a, 16), pl.ds(WIDE + 16 * a, 16)
            left, right = pl.ds(0, LANES), pl.ds(LANES, LANES)
            table_s[top, left] = cosine.astype(jnp.bfloat16)
            table_s[top, right] = sine.astype(jnp.bfloat16)
            table_s[bottom, left] = (-sine).astype(jnp.bfloat16)
            table_s[bottom, right] = cosine.astype(jnp.bfloat16)
        tile_c, tile_s = cos_sin_turns((wave * (WIDE * line(16) - start)).astype(jnp.float32), length, inverse)
        back_s[0], back_s[1] = tile_c, tile_s
        lane = lax.broadcasted_iota(jnp.int32, (parts, LANES), 1)
        part_c, part_s = cos_sin_turns((LANES * line(8) * (WIDE * lane - start)).astype(jnp.float32), length, inverse)
        shifts = [cos_sin_turns((LANES * line(8) * (lane + i * LANES)).astype(jnp.float32), length, inverse) for i in range(2)]
        for t in range(wides):
            pc, ps = part_c[:, t:t + 1], part_s[:, t:t + 1]
            for i in range(2):
                sc, ss = shifts[i]
                at = pl.ds(t * WIDE + i * LANES, LANES)
                turn_c[:, at] = pc * sc - ps * ss
                turn_n[:, at] = ps * sc + pc * ss
        blocks = [[None] * (2 * 2) for _ in range(wides * slots)]
        for t in range(wides):
            for i in range(2):
                at = t * WIDE + i * LANES
                if at < tiles * LANES:
                    col = lane + at
                    mine = (col >= start) & (col < start + whole)
                    v = jnp.where(mine, y_ref[q, :, pl.ds(at, LANES)].astype(jnp.float32)[:parts], 0.0)
                for w in range(slots):
                    row = blocks[w * wides + t]
                    if at < tiles * LANES:
                        row[i] = v * turn_c[pl.ds(w, 1), pl.ds(at, LANES)]
                        row[2 + i] = v * turn_n[pl.ds(w, 1), pl.ds(at, LANES)]
                    else:
                        row[i] = row[2 + i] = jnp.zeros((parts, LANES), jnp.float32)
        stacked = jnp.concatenate([jnp.concatenate(row, axis=1) for row in blocks], axis=0).astype(jnp.bfloat16)
        sums_s[...] = jnp.dot(stacked, table_s[...], preferred_element_type=jnp.float32)
        place = 2 * jnp.where(north, q, pairs - 1 - q) + half
        for w in range(slots):
            real = jnp.zeros((parts, LANES), jnp.float32)
            imag = jnp.zeros((parts, LANES), jnp.float32)
            for t in range(wides):
                at = pl.ds(parts * (w * wides + t), parts)
                c, s = sums_s[at, pl.ds(0, LANES)], sums_s[at, pl.ds(LANES, LANES)]
                tc, ts = back_s[0, pl.ds(t, 1), :], back_s[1, pl.ds(t, 1), :]
                real = real + (tc * c - ts * s)
                imag = imag - (ts * c + tc * s)
            waves = lax.broadcasted_iota(jnp.int32, (1, LANES), 1) + w * LANES
            keep = jnp.where(2 * waves < whole, inverse, 0.0)
            four_s[pl.ds(pl.multiple_of(place * 16, 16), 16), pl.ds(w * LANES, LANES)] = jnp.concatenate(
                [real * keep, imag * keep], axis=0).astype(jnp.bfloat16)
        return 0

    lax.fori_loop(0, rows, one, 0)

    hot = (lax.broadcasted_iota(jnp.int32, (half_rows, half_rows), 0) == order_ref[...]).astype(jnp.float32).astype(jnp.bfloat16)
    moved = jnp.dot(four_s[...], hot, preferred_element_type=jnp.float32)
    mix_s[...] = jnp.zeros_like(mix_s)
    for r in range(8):
        for s in range(slots):
            mix_s[r, pl.ds(16 * s, 16), :] = moved[16 * r:16 * r + 16, s * LANES:(s + 1) * LANES]
        if r < slots:
            for e in range(rows - 8):
                mix_s[r, pl.ds(16 * (slots + e), 16), :] = moved[16 * (8 + e):16 * (8 + e) + 16, r * LANES:(r + 1) * LANES]
        stage_s[pl.ds(r, LANES, stride=8), :] = mix_s[r].T
    send_s[...] = stage_s[...].astype(jnp.bfloat16).reshape(send_s.shape)

    pl.semaphore_wait(barrier, devices - 1)

    def post(a, b):
        pltpu.make_async_remote_copy(
            src_ref=send_s.at[a * across + b], dst_ref=got_s.at[me], send_sem=send_sem, recv_sem=recv_sem,
            device_id=(a, b), device_id_type=pl.DeviceIdType.MESH).start()

    partners(post)
    own = pltpu.make_async_copy(send_s.at[me], got_s.at[me], own_sem)
    own.start()

    src = lax.broadcasted_iota(jnp.int32, (slots * LANES, 2 * LANES), 0)
    dst = lax.broadcasted_iota(jnp.int32, (slots * LANES, 2 * LANES), 1)
    unfold = (((dst & 127) >> 4) == (src >> 7)) & ((src & 127) == 16 * (slots + (dst >> 7)) + (dst & 15))
    unfold = unfold.astype(jnp.float32).astype(jnp.bfloat16)
    slot_of = (lax.broadcasted_iota(jnp.int32, (half_rows, LANES), 1) >> 4).astype(jnp.float32).astype(jnp.bfloat16)
    rest = pl.ds(0, devices - 1)
    every = pltpu.make_async_remote_copy(
        src_ref=send_s.at[rest], dst_ref=got_s.at[rest], send_sem=send_sem, recv_sem=recv_sem,
        device_id=(my_a, columns[1]), device_id_type=pl.DeviceIdType.MESH)
    every.wait_send()
    every.wait_recv()
    own.wait()

    for d in range(devices // 2):
        n = got_s[d].astype(jnp.float32)
        o = got_s[devices - 1 - d].astype(jnp.float32)
        plain_s[pl.ds(rows * d, 8), :] = n + o
        anti_s[pl.ds(rows * d, 8), :] = n - o
        kept_s[pl.ds(8 * d, 8), :] = n + o
        keptanti_s[pl.ds(8 * d, 8), :] = n - o
    weights_in.wait()
    for par, wide, kept in ((0, plain_s, kept_s), (1, anti_s, keptanti_s)):
        folded = jnp.concatenate([kept[pl.ds(s, devices // 2, stride=8), :] for s in range(slots)], axis=1).astype(jnp.bfloat16)
        extra = jnp.dot(folded, unfold, preferred_element_type=jnp.float32)
        for e in range(rows - 8):
            wide[pl.ds(8 + e, devices // 2, stride=rows), :] = extra[:, e * LANES:(e + 1) * LANES]
        values = wide[...].astype(jnp.bfloat16)
        zero = jnp.zeros_like(values)
        picked = jnp.concatenate([jnp.where(slot_of == jnp.bfloat16(s), values, zero) for s in range(slots)], axis=0)
        table = jnp.concatenate([legendre_s[s, par] for s in range(slots)], axis=1)
        turn_s[pl.ds(par, half_rows // 2, stride=2), :] = jnp.dot(table, picked, preferred_element_type=jnp.float32)
    z = turn_s[...].T
    degree = lax.broadcasted_iota(jnp.int32, (16, half_rows), 1)
    for s in range(slots):
        limit = half_rows - waves_ref[me * slots + s]
        out_ref[s] = jnp.where(degree < limit, z[16 * s:16 * s + 16], 0.0)


def transform(y, order, waves, legendre, half_rows, pair_length, sizes):
    pairs = y.shape[0]
    slots = legendre.shape[0]
    tiles = pl.cdiv(pair_length, LANES)
    wides = pl.cdiv(tiles * LANES, WIDE)
    vm = pl.BlockSpec(memory_space=pltpu.VMEM)
    f32, b16 = jnp.float32, jnp.bfloat16
    return pl.pallas_call(
        functools.partial(transform_kernel, sizes, pair_length),
        out_shape=jax.ShapeDtypeStruct((slots, 16, half_rows), f32),
        in_specs=[vm, vm, pl.BlockSpec(memory_space=pltpu.SMEM), pl.BlockSpec(memory_space=pl.ANY)],
        out_specs=vm,
        scratch_shapes=[
            pltpu.VMEM((2 * WIDE, 2 * LANES), b16),
            pltpu.VMEM((8 * wides * slots, 2 * LANES), f32),
            pltpu.VMEM((2, 16, LANES), f32),
            pltpu.VMEM((8, WIDE * wides), f32),
            pltpu.VMEM((8, WIDE * wides), f32),
            pltpu.VMEM((32 * pairs, half_rows), b16),
            pltpu.VMEM((8, LANES, LANES), f32),
            pltpu.VMEM((8 * LANES, LANES), f32),
            pltpu.VMEM((LANES, 8, LANES), b16),
            pltpu.VMEM((LANES, 8, LANES), b16),
            pltpu.VMEM((half_rows, LANES), f32),
            pltpu.VMEM((half_rows, LANES), f32),
            pltpu.VMEM((8 * LANES // 2, LANES), f32),
            pltpu.VMEM((8 * LANES // 2, LANES), f32),
            pltpu.VMEM((half_rows, LANES), f32),
            pltpu.VMEM(legendre.shape, b16),
            pltpu.SemaphoreType.DMA, pltpu.SemaphoreType.DMA, pltpu.SemaphoreType.DMA, pltpu.SemaphoreType.DMA,
        ],
        compiler_params=pltpu.CompilerParams(collective_id=0, has_side_effects=True),
        name="transform",
    )(y, order, waves, legendre)


def on_device(grid, dep_row, dep_lon, lon_frac, lat_frac, wave_slot, legendre):
    half_rows = wave_slot.shape[0]
    _, levels, pairs, pair_length = grid.shape
    slots = legendre.shape[0]
    axes = ("aa", "ba")
    sizes = (lax.axis_size("aa"), lax.axis_size("ba"))
    devices = sizes[0] * sizes[1]
    first = (lax.axis_index(axes) * pairs).astype(jnp.int32).reshape(1)
    own = jnp.transpose(grid, (0, 2, 1, 3))
    out, head, order = interpolate(first, own, dep_row, jnp.transpose(dep_lon, (1, 0, 2)), jnp.transpose(lon_frac, (1, 0, 2)),
                                   lat_frac, wave_slot, half_rows, 2 * levels, sizes)
    result = transform(head, order, wave_slot, legendre, half_rows, pair_length, sizes)
    return (jnp.transpose(out, (0, 2, 1, 3)), jnp.transpose(result, (1, 0, 2)))


def solution(mesh):
    return jax.shard_map(
        on_device,
        mesh=mesh,
        in_specs=(
            P(None, None, ("aa", "ba"), None),
            P(("aa", "ba"), None),
            P(None, ("aa", "ba"), None),
            P(None, ("aa", "ba"), None),
            P(("aa", "ba"), None),
            P(),
            P(("aa", "ba"), None, None, None),
        ),
        out_specs=(P(None, None, ("aa", "ba"), None), P(None, ("aa", "ba"), None)),
        check_vma=False,
    )
```

```python
import functools

import jax
import jax.numpy as jnp
from jax import lax
from jax.experimental import pallas as pl
from jax.experimental.pallas import tpu as pltpu
from jax.sharding import PartitionSpec as P

LANES = 128
WIN = 256
ETILES = 24
EW = ETILES * LANES
MARGIN = 60
ROWS = 11
NOWHERE = 192.0


def row_place(global_row, half_rows):
    northern = global_row < half_rows
    number = jnp.where(northern, global_row + 1, 2 * half_rows - global_row)
    second = number > half_rows // 2
    inner = jnp.where(second, number - half_rows // 2 - 1, half_rows // 2 - number)
    begin = jnp.where(second, 16 + 4 * (half_rows // 2 - inner), 0)
    return jnp.where(northern, inner, half_rows - 1 - inner), begin, 16 + 4 * number


def cubic(t):
    return (
        -t * (t - 1.0) * (t - 2.0) * (1.0 / 6.0),
        (t + 1.0) * (t - 1.0) * (t - 2.0) * 0.5,
        -(t + 1.0) * t * (t - 2.0) * 0.5,
        (t + 1.0) * t * (t - 1.0) * (1.0 / 6.0),
    )


class Stencil:
    pass


def stencil_steps(half_rows, pair_length, first, sources, row_ref, lon_ref, lonf_ref, latf_ref, place_t, ext_s, plan_s, y_s, head_s):
    groups, pairs, levels, _ = sources[1].shape
    fields = groups * levels
    near = pairs + 4
    tiles = pl.cdiv(pair_length, LANES)
    steps = Stencil()

    lane = lax.broadcasted_iota(jnp.int32, (fields, LANES), 1)

    def half_lengths(pair):
        inner = jnp.where(pair < half_rows // 2, pair, half_rows - 1 - pair)
        return 16 + 4 * (half_rows // 2 - inner), 16 + 4 * (half_rows // 2 + 1 + inner)

    def clear():
        ext_s[:, :, pl.ds(0, LANES)] = jnp.zeros((2 * near, fields, LANES), jnp.bfloat16)
        ext_s[:, :, pl.ds(tiles * LANES, EW - tiles * LANES)] = jnp.zeros((2 * near, fields, EW - tiles * LANES), jnp.bfloat16)

    def fill(j):
        ref, at = (sources[0], j) if j < 2 else ((sources[1], j - 2) if j < 2 + pairs else (sources[2], j - 2 - pairs))
        for f in range(groups):
            src = ref[f, at]
            for copy in range(2):
                ext_s[2 * j + copy, pl.ds(levels * f, levels), pl.ds(LANES, pair_length)] = src

    def wrap(copy, tile, shift, low, edge):
        at = pl.ds(pl.multiple_of(tile * LANES, LANES), LANES)
        begin = tile * LANES + shift
        two = ext_s[copy, :, pl.ds(pl.multiple_of((begin >> 7) * LANES, LANES), 2 * LANES)].astype(jnp.float32)
        moved = pltpu.roll(two, (2 * LANES - (begin & 127)) & 255, 1)[:, :LANES]
        spot = lane + tile * LANES
        beyond = spot < edge if low else spot >= edge
        return copy, at, jnp.where(beyond, moved, ext_s[copy, :, at].astype(jnp.float32)).astype(jnp.bfloat16)

    def close(j):
        len0, len1 = half_lengths(first + j - 2)
        wraps = []
        for half in range(2):
            start, length = (len0, len1) if half else (0, len0)
            for i in range(1 + half):
                wraps.append(wrap(2 * j + half, ((start >> 7) if half else 0) + i, length, True, start + LANES))
            for i in range(3):
                wraps.append(wrap(2 * j + half, ((start + length) >> 7) + 1 + i, -length, False, start + length + LANES))
        for copy, at, tile in wraps:
            ext_s[copy, :, at] = tile

    sub8 = lax.broadcasted_iota(jnp.int32, (8, LANES), 0)
    lane8 = lax.broadcasted_iota(jnp.int32, (8, LANES), 1)

    def weigh(tile, fits, width=LANES):
        at = pl.ds(pl.multiple_of(tile * LANES, LANES), LANES)
        some = pl.ds(pl.multiple_of(tile * LANES, LANES), width)
        col = tile * LANES + lane8
        inside = col < pair_length

        def wide(x):
            if width < LANES:
                x = jnp.concatenate([x, jnp.zeros((x.shape[0], LANES - width), x.dtype)], axis=1)
            return x

        for q in range(pairs):
            pair = first + q
            northern = pair < half_rows // 2
            len0, _ = half_lengths(pair)
            second = col >= len0
            inner = jnp.where(northern, pair, half_rows - 1 - pair)

            def base_of(number):
                return jnp.clip(jnp.where(northern, number - 1, 2 * half_rows - number) - 2, 0, 2 * half_rows - 4)

            base = jnp.where(second, base_of(half_rows // 2 + 1 + inner), base_of(half_rows // 2 - inner))
            later = jnp.broadcast_to(wide(row_ref[pl.ds(q, 1), some]), (8, LANES)) > base
            base_k = jnp.where(second, jnp.maximum(tile * LANES - len0, 0), tile * LANES) - MARGIN
            lon = wide(lon_ref[q, :, some])
            lon = jnp.concatenate([lon, lon], axis=0)
            lon = jnp.where(later, pltpu.roll(lon, 1, 0), lon)
            frac = wide(lonf_ref[q, :, some])
            frac = jnp.concatenate([frac, frac], axis=0)
            frac = jnp.where(later, pltpu.roll(frac, 1, 0), frac)
            latw = cubic(jnp.broadcast_to(wide(latf_ref[pl.ds(q, 1), some]), (8, LANES)))
            r = jnp.where(later, sub8 - 1, sub8)
            lat = jnp.zeros((8, LANES), jnp.float32)
            for i in range(4):
                lat = jnp.where(inside & (r == i), latw[i], lat)
            _, begin, length = row_place(jnp.minimum(base + sub8, 2 * half_rows - 1), half_rows)
            rel = lon - 1 - base_k
            rel = jnp.where(rel < 0, rel + length, jnp.where(rel >= length, rel - length, rel))
            short = length <= WIN - 4
            rel = jnp.where(short, lon, rel)
            bad = (lat != 0.0) & ((rel < 0) | (rel > WIN - 4))
            fits = jnp.maximum(fits, bad.astype(jnp.int32))
            place = ((begin + jnp.where(short, -1, base_k) + LANES) & 127) + rel
            block = (place >> 4) & 15
            ws = cubic(frac)
            for o in range(4):
                plan_s[q * ROWS + o, :, at] = lat * ws[o]
                plan_s[q * ROWS + 4 + o, :, at] = ((place + o) & 15).astype(jnp.float32)
            plan_s[q * ROWS + 8, :, at] = block.astype(jnp.float32)
            plan_s[q * ROWS + 9, :, at] = ((block + 1) & 15).astype(jnp.float32)
            plan_s[q * ROWS + 10, :, at] = (lon + begin).astype(jnp.float32)
        return fits

    def weigh_all():
        worst = lax.fori_loop(0, pair_length // LANES, weigh, jnp.zeros((8, LANES), jnp.int32))
        if pair_length % LANES:
            worst = weigh(tiles - 1, worst, pair_length % LANES)
        return worst

    node = lax.broadcasted_iota(jnp.int32, (16, LANES), 0).astype(jnp.float32).astype(jnp.bfloat16)
    zero16 = jnp.zeros((16, LANES), jnp.bfloat16)

    def spread(mine, weight, rest, block, after):
        v = zero16
        for o in (3, 2, 1, 0):
            v = jnp.where(node == rest[o], weight[o], v)
        block = jnp.where(mine, jnp.where(node < rest[0], after, block), jnp.bfloat16(NOWHERE))
        return [jnp.where(block == jnp.bfloat16(a), v, zero16) for a in range(WIN // 16)]

    def plan(d, i, q, at):
        return jnp.broadcast_to(plan_s[q * ROWS + i, pl.ds(d, 1), at], (16, LANES))

    def packed(x):
        return x.astype(jnp.bfloat16)

    def locate():
        for q in range(pairs):
            pair = first + q
            northern = pair < half_rows // 2
            inner = jnp.where(northern, pair, half_rows - 1 - pair)
            for half in range(2):
                number = half_rows // 2 + 1 + inner if half else half_rows // 2 - inner
                g = jnp.where(northern, number - 1, 2 * half_rows - number)
                base = jnp.clip(g - 2, 0, 2 * half_rows - 4)
                for d in range(5):
                    pair_row, begin, length = row_place(jnp.minimum(base + d, 2 * half_rows - 1), half_rows)
                    short = length <= WIN - 4
                    copy = 2 * jnp.clip(pair_row - first + 2, 0, near - 1) + (begin > 0).astype(jnp.int32)
                    at = 3 * ((2 * q + half) * 5 + d)
                    place_t[at] = copy
                    place_t[at + 1] = begin + LANES + jnp.where(short, -1, -MARGIN)
                    place_t[at + 2] = jnp.where(short, 0, 1)

    def unit_scalars(q, u):
        len0, _ = half_lengths(first + q)
        straddle = len0 >> 7
        half = (u > straddle).astype(jnp.int32)
        tile = u - half
        k0 = jnp.where(half == 1, jnp.maximum(tile * LANES - len0, 0), tile * LANES)
        return len0, straddle, half, tile, 15 * (2 * q + half), k0

    lane16 = lax.broadcasted_iota(jnp.int32, (16, LANES), 1).astype(jnp.float32).astype(jnp.bfloat16)

    def own_half(half, tile, len0):
        edge = jnp.clip(len0 - tile * LANES, 0, LANES)
        low = jnp.where(half == 1, edge, 0).astype(jnp.float32)
        high = jnp.where(half == 1, LANES, edge).astype(jnp.float32)
        spread_low = jnp.full((16, LANES), low, jnp.float32).astype(jnp.bfloat16)
        spread_high = jnp.full((16, LANES), high, jnp.float32).astype(jnp.bfloat16)
        return (lane16 >= spread_low) & (lane16 < spread_high)

    def finish(q, u, straddle, tile, total, carry):
        total = total + jnp.where(u == straddle + 1, carry, 0.0)
        at = pl.ds(pl.multiple_of(tile * LANES, LANES), LANES)
        y_s[q, :, at] = total.astype(jnp.bfloat16)
        head_s[q, :, at] = total[:head_s.shape[1]].astype(jnp.bfloat16)
        return total

    def near_units(chosen):
        def unit(q, u, carry):
            len0, straddle, half, tile, base, k0 = unit_scalars(q, u)
            at = pl.ds(pl.multiple_of(tile * LANES, LANES), LANES)
            mine = own_half(half, tile, len0)
            rows, weights = [], []
            for d in range(5):
                where_row = place_t[base + 3 * d]
                begin = place_t[base + 3 * d + 1] + place_t[base + 3 * d + 2] * k0
                s = begin & 127
                first_tile = pl.multiple_of((begin >> 7) * LANES, LANES)
                row = [packed(plan(d, i, q, at)) for i in range(10)]
                weights += spread(mine, row[:4], row[4:8], row[8], row[9])
                three = ext_s[where_row, :, pl.ds(first_tile, 3 * LANES)]
                rows += [jnp.where(lane >= s, three[:, :LANES], three[:, 2 * LANES:]), three[:, LANES:2 * LANES]]
            total = jnp.dot(jnp.concatenate(rows, axis=1), jnp.concatenate(weights, axis=0),
                            preferred_element_type=jnp.float32)
            return finish(q, u, straddle, tile, total, carry)

        lax.fori_loop(0, tiles + 1, lambda u, carry: tuple(unit(q, u, c) for q, c in zip(chosen, carry)),
                      (jnp.zeros((fields, LANES), jnp.float32),) * len(chosen))

    def any_units():
        def unit(q, u, carry):
            len0, straddle, half, tile, base, _ = unit_scalars(q, u)
            at = pl.ds(pl.multiple_of(tile * LANES, LANES), LANES)
            mine = own_half(half, tile, len0)

            def window(w, total):
                rows, weights = [], []
                for d in range(5):
                    where_row = place_t[base + 3 * d]
                    place = (plan(d, 10, q, at) + (LANES - 1)).astype(jnp.int32) - w * WIN
                    block = jnp.clip(place >> 4, -2, 18)
                    rest = [packed(((place + o) & 15).astype(jnp.float32)) for o in range(4)]
                    weight = [packed(plan(d, o, q, at)) for o in range(4)]
                    weights += spread(mine, weight, rest, packed(block.astype(jnp.float32)), packed((block + 1).astype(jnp.float32)))
                    rows.append(ext_s[where_row, :, pl.ds(pl.multiple_of(w * WIN, WIN), WIN)])
                return total + jnp.dot(jnp.concatenate(rows, axis=1), jnp.concatenate(weights, axis=0),
                                       preferred_element_type=jnp.float32)

            total = lax.fori_loop(0, EW // WIN, window, jnp.zeros((fields, LANES), jnp.float32))
            return finish(q, u, straddle, tile, total, carry)

        lax.fori_loop(0, tiles + 1, lambda u, carry: tuple(unit(q, u, carry[q]) for q in range(pairs)),
                      (jnp.zeros((fields, LANES), jnp.float32),) * pairs)

    def deliver(out_ref):
        for f in range(groups):
            for q in range(pairs):
                out_ref[f, q] = y_s[q, pl.ds(levels * f, levels), pl.ds(0, pair_length)]

    steps.clear, steps.fill, steps.close, steps.weigh_all, steps.locate = clear, fill, close, weigh_all, locate
    steps.near_units, steps.any_units, steps.deliver, steps.near = near_units, any_units, deliver, near
    return steps


def stencil_scratch(pairs, fields, pair_length):
    padded = pl.cdiv(pair_length, LANES) * LANES
    return [
        pltpu.SMEM((30 * pairs,), jnp.int32),
        pltpu.VMEM((2 * (pairs + 4), fields, EW), jnp.bfloat16),
        pltpu.VMEM((pairs * ROWS, 8, padded), jnp.float32),
        pltpu.VMEM((pairs, fields, padded), jnp.bfloat16),
    ]


def by_slot_then_device(wave, devices):
    count = wave.shape[1]
    slots = count // devices
    wanted = lax.broadcasted_iota(jnp.int32, (1, count), 1)
    wanted = slots * (wanted % devices) + wanted // devices
    moves = (lax.broadcasted_iota(jnp.int32, (count, count), 0) == wanted).astype(jnp.float32).astype(jnp.bfloat16)
    high, low = wave // 8, wave % 8
    sub = lax.broadcasted_iota(jnp.int32, (16, count), 0)
    digits = jnp.where(sub == 0, high, jnp.where(sub == 1, low, 0)).astype(jnp.float32).astype(jnp.bfloat16)
    moved = jnp.dot(digits, moves, preferred_element_type=jnp.float32)
    return (8.0 * moved[0:1] + moved[1:2]).astype(jnp.int32)


def whole_kernel(sizes, half_rows, pair_length, grid_hbm, row_hbm, lon_hbm, lonf_hbm, latf_hbm, wave_ref, waves_ref, legendre_hbm,
                 out_ref, result_ref, far_ref, before_hbm, after_hbm, order_ref,
                 before_s, own_s, after_s, row_s, lon_s, lonf_s, latf_s, place_t, ext_s, plan_s, y_s, head_s,
                 in_sem, halo_send_sem, halo_recv_sem, keep_sem, *refs):
    along, across = sizes
    devices = along * across
    pairs = own_s.shape[1]
    me = lax.axis_index("aa") * across + lax.axis_index("ba")
    up = lax.rem(me + 1, devices)
    down = lax.rem(me + devices - 1, devices)

    def where(device):
        return (device // across, lax.rem(device, across))

    after_steps = transform_steps(sizes, pair_length, head_s, waves_ref, legendre_hbm, result_ref, refs[:16], refs[16:])
    barrier = pltpu.get_barrier_semaphore()
    loads = [pltpu.make_async_copy(src, dst, in_sem.at[i]) for i, (src, dst) in enumerate((
        (row_hbm, row_s), (lon_hbm, lon_s), (lonf_hbm, lonf_s), (latf_hbm, latf_s), (grid_hbm, own_s)))]
    for load in loads:
        load.start()
    after_steps.greet(barrier)

    steps = stencil_steps(half_rows, pair_length, me * pairs, (before_s, own_s, after_s), row_s, lon_s, lonf_s, latf_s,
                          place_t, ext_s, plan_s, y_s, head_s)
    steps.locate()
    steps.clear()
    for load in loads:
        load.wait()
    flag = jnp.max(steps.weigh_all())

    pl.semaphore_wait(barrier, devices - 1)
    sends = []
    for i, (begin, dst, device) in enumerate(((pairs - 2, before_s, up), (0, after_s, down))):
        sends.append(pltpu.make_async_remote_copy(
            src_ref=grid_hbm.at[:, pl.ds(begin, 2)], dst_ref=dst, send_sem=halo_send_sem.at[i], recv_sem=halo_recv_sem.at[i],
            device_id=where(device), device_id_type=pl.DeviceIdType.MESH))
        sends[-1].start()
    for j in range(2, 2 + pairs):
        steps.fill(j)
    for j in range(2, 2 + pairs):
        steps.close(j)
    order = by_slot_then_device(wave_ref[...].reshape(1, half_rows), devices)
    order_ref[...] = order
    inner = tuple(range(2, pairs - 2))
    steps.near_units(inner)
    for send in sends:
        send.wait()
    keeps = [pltpu.make_async_copy(before_s, before_hbm, keep_sem.at[0]), pltpu.make_async_copy(after_s, after_hbm, keep_sem.at[1])]
    for keep in keeps:
        keep.start()
    for j in (0, 1, 2 + pairs, 3 + pairs):
        steps.fill(j)
    for j in (0, 1, 2 + pairs, 3 + pairs):
        steps.close(j)
    steps.near_units(tuple(q for q in range(pairs) if q not in inner))
    after_steps.sums()
    after_steps.lay_out(order_ref[...], flag)
    own = after_steps.trade()
    steps.deliver(out_ref)
    far_ref[0] = (after_steps.finish(own) > 0.0).astype(jnp.int32)
    for keep in keeps:
        keep.wait()


def far_kernel(half_rows, pair_length, first_ref, before_ref, own_ref, after_ref, row_ref, lon_ref, lonf_ref, latf_ref,
               out_ref, head_ref, place_t, ext_s, plan_s, y_s):
    steps = stencil_steps(half_rows, pair_length, first_ref[0], (before_ref, own_ref, after_ref), row_ref, lon_ref, lonf_ref, latf_ref,
                          place_t, ext_s, plan_s, y_s, head_ref)
    steps.locate()
    steps.clear()
    steps.weigh_all()
    for j in range(steps.near):
        steps.fill(j)
    for j in range(steps.near):
        steps.close(j)
    steps.any_units()
    steps.deliver(out_ref)


def both(first, grid, dep_row, dep_lon, lon_frac, lat_frac, wave_slot, legendre, half_rows, spectral_fields, sizes):
    groups, pairs, levels, pair_length = grid.shape
    fields = groups * levels
    slots = legendre.shape[0]
    padded = pl.cdiv(pair_length, LANES) * LANES
    b16, f32, i32 = jnp.bfloat16, jnp.float32, jnp.int32
    vm, anywhere, scalars = (pl.BlockSpec(memory_space=m) for m in (pltpu.VMEM, pl.ANY, pltpu.SMEM))
    halo = jax.ShapeDtypeStruct((groups, 2, levels, pair_length), b16)
    head = jax.ShapeDtypeStruct((pairs, spectral_fields, padded), b16)
    full = jax.ShapeDtypeStruct(grid.shape, b16)
    stencil = stencil_scratch(pairs, fields, pair_length)
    local = [
        pltpu.VMEM(halo.shape, b16), pltpu.VMEM(grid.shape, b16), pltpu.VMEM(halo.shape, b16),
        pltpu.VMEM(dep_row.shape, i32), pltpu.VMEM(dep_lon.shape, i32), pltpu.VMEM(lon_frac.shape, f32), pltpu.VMEM(lat_frac.shape, f32),
    ] + stencil + [pltpu.VMEM(head.shape, b16)]
    out, result, far, before, after, order = pl.pallas_call(
        functools.partial(whole_kernel, sizes, half_rows, pair_length),
        out_shape=(full, jax.ShapeDtypeStruct((slots, 16, half_rows), f32), jax.ShapeDtypeStruct((1,), i32), halo, halo,
                   jax.ShapeDtypeStruct((1, half_rows), i32)),
        in_specs=[anywhere] * 5 + [vm, scalars, anywhere],
        out_specs=(vm, vm, scalars, anywhere, anywhere, vm),
        scratch_shapes=local + [pltpu.SemaphoreType.DMA((5,)), pltpu.SemaphoreType.DMA((2,)), pltpu.SemaphoreType.DMA((2,)),
                                pltpu.SemaphoreType.DMA((2,))] + transform_scratch(pairs, slots, half_rows, pair_length, legendre),
        compiler_params=pltpu.CompilerParams(collective_id=1, has_side_effects=True),
        name="whole",
    )(grid, dep_row, dep_lon, lon_frac, lat_frac, wave_slot, wave_slot, legendre)

    def again():
        redone, first_fields = pl.pallas_call(
            functools.partial(far_kernel, half_rows, pair_length),
            out_shape=(full, head),
            in_specs=[scalars] + [vm] * 7,
            out_specs=(vm, vm),
            scratch_shapes=stencil,
            name="far",
        )(first, before, grid, after, dep_row, dep_lon, lon_frac, lat_frac)
        return redone, transform(first_fields, order, wave_slot, legendre, half_rows, pair_length, sizes)

    return lax.cond(far[0] > 0, again, lambda: (out, result))

WIDE = 256

COS = (1, -19.7392087, 64.9393842, -85.4565372, 60.2407014, -26.3960673, 7.77462739, -1.42354417)
SIN = (6.28318531, -41.3417022, 81.6052456, -76.7057546, 42.0572162, -15.0833301, 3.7717259, -0.609657301)


def cos_sin_turns(prod, length, inverse):
    turns = jnp.floor(prod * inverse + 0.5)
    t = (prod - turns * length) * inverse
    x = t * t
    c = jnp.full_like(x, COS[-1])
    for a in COS[-2::-1]:
        c = c * x + a
    s = jnp.full_like(x, SIN[-1])
    for a in SIN[-2::-1]:
        s = s * x + a
    return c, s * t


def transform_steps(sizes, pair_length, y_ref, waves_ref, legendre_hbm, result_ref, scratch, sems):
    (table_s, sums_s, back_s, turn_c, turn_n, four_s, mix_s, stage_s, send_s, got_s, plain_s, anti_s, kept_s, keptanti_s, turn_s, legendre_s) = scratch
    legendre_sem, own_sem, send_sem, recv_sem = sems
    along, across = sizes
    devices = along * across
    pairs = y_ref.shape[0]
    slots = legendre_s.shape[0]
    half_rows = slots * devices
    rows = 2 * pairs
    tiles = pl.cdiv(pair_length, LANES)
    my_a = lax.axis_index("aa")
    my_b = lax.axis_index("ba")
    me = my_a * across + my_b
    first = me * pairs
    north = me < devices // 2
    parts = 8
    wides = pl.cdiv(tiles * LANES, WIDE)

    steps = Stencil()

    weights_in = pltpu.make_async_copy(legendre_hbm, legendre_s, legendre_sem)

    columns = [lax.rem(my_b + i, across) for i in range(across)]

    def partners(act):
        for b in range(1, across):
            act(my_a, columns[b])

        def others(i, _):
            a = lax.rem(my_a + i, along)
            for b in range(across):
                act(a, columns[b])
            return 0

        lax.fori_loop(1, along, others, 0)

    def greet(barrier):
        weights_in.start()
        partners(lambda a, b: pl.semaphore_signal(barrier, inc=1, device_id=(a, b), device_id_type=pl.DeviceIdType.MESH))

    def one(i, _):
        q = i // 2
        half = i - 2 * q
        pair = first + q
        inner = jnp.where(north, pair, half_rows - 1 - pair)
        len0 = 16 + 4 * (half_rows // 2 - inner)
        start = jnp.where(half == 1, len0, 0)
        whole = jnp.where(half == 1, 16 + 4 * (half_rows // 2 + 1 + inner), len0)
        length = jnp.full((1, LANES), whole, jnp.int32).astype(jnp.float32)
        inverse = 1.0 / length

        def line(n):
            return lax.broadcasted_iota(jnp.int32, (n, LANES), 0)

        wave = lax.broadcasted_iota(jnp.int32, (16, LANES), 1)
        fine_c, fine_s = cos_sin_turns((wave * line(16)).astype(jnp.float32), length, inverse)
        step_c, step_s = cos_sin_turns((wave * (16 * line(16))).astype(jnp.float32), length, inverse)
        for a in range(WIDE // 16):
            ca, sa = step_c[a:a + 1], step_s[a:a + 1]
            cosine = ca * fine_c - sa * fine_s
            sine = sa * fine_c + ca * fine_s
            top, bottom = pl.ds(16 * a, 16), pl.ds(WIDE + 16 * a, 16)
            left, right = pl.ds(0, LANES), pl.ds(LANES, LANES)
            table_s[top, left] = cosine.astype(jnp.bfloat16)
            table_s[top, right] = sine.astype(jnp.bfloat16)
            table_s[bottom, left] = (-sine).astype(jnp.bfloat16)
            table_s[bottom, right] = cosine.astype(jnp.bfloat16)
        tile_c, tile_s = cos_sin_turns((wave * (WIDE * line(16) - start)).astype(jnp.float32), length, inverse)
        back_s[0], back_s[1] = tile_c, tile_s
        lane = lax.broadcasted_iota(jnp.int32, (parts, LANES), 1)
        part_c, part_s = cos_sin_turns((LANES * line(8) * (WIDE * lane - start)).astype(jnp.float32), length, inverse)
        shifts = [cos_sin_turns((LANES * line(8) * (lane + i * LANES)).astype(jnp.float32), length, inverse) for i in range(2)]
        for t in range(wides):
            pc, ps = part_c[:, t:t + 1], part_s[:, t:t + 1]
            for i in range(2):
                sc, ss = shifts[i]
                at = pl.ds(t * WIDE + i * LANES, LANES)
                turn_c[:, at] = pc * sc - ps * ss
                turn_n[:, at] = ps * sc + pc * ss
        blocks = [[None] * (2 * 2) for _ in range(wides * slots)]
        for t in range(wides):
            for i in range(2):
                at = t * WIDE + i * LANES
                if at < tiles * LANES:
                    col = lane + at
                    mine = (col >= start) & (col < start + whole)
                    v = jnp.where(mine, y_ref[q, :, pl.ds(at, LANES)].astype(jnp.float32)[:parts], 0.0)
                for w in range(slots):
                    row = blocks[w * wides + t]
                    if at < tiles * LANES:
                        row[i] = v * turn_c[pl.ds(w, 1), pl.ds(at, LANES)]
                        row[2 + i] = v * turn_n[pl.ds(w, 1), pl.ds(at, LANES)]
                    else:
                        row[i] = row[2 + i] = jnp.zeros((parts, LANES), jnp.float32)
        stacked = jnp.concatenate([jnp.concatenate(row, axis=1) for row in blocks], axis=0).astype(jnp.bfloat16)
        sums_s[...] = jnp.dot(stacked, table_s[...], preferred_element_type=jnp.float32)
        place = 2 * jnp.where(north, q, pairs - 1 - q) + half
        for w in range(slots):
            real = jnp.zeros((parts, LANES), jnp.float32)
            imag = jnp.zeros((parts, LANES), jnp.float32)
            for t in range(wides):
                at = pl.ds(parts * (w * wides + t), parts)
                c, s = sums_s[at, pl.ds(0, LANES)], sums_s[at, pl.ds(LANES, LANES)]
                tc, ts = back_s[0, pl.ds(t, 1), :], back_s[1, pl.ds(t, 1), :]
                real = real + (tc * c - ts * s)
                imag = imag - (ts * c + tc * s)
            waves = lax.broadcasted_iota(jnp.int32, (1, LANES), 1) + w * LANES
            keep = jnp.where(2 * waves < whole, inverse, 0.0)
            four_s[pl.ds(pl.multiple_of(place * 16, 16), 16), pl.ds(w * LANES, LANES)] = jnp.concatenate(
                [real * keep, imag * keep], axis=0).astype(jnp.bfloat16)
        return 0

    def sums():
        lax.fori_loop(0, rows, one, 0)

    def lay_out(order, flag):
        hot = (lax.broadcasted_iota(jnp.int32, (half_rows, half_rows), 0) == order).astype(jnp.float32).astype(jnp.bfloat16)
        moved = jnp.dot(four_s[...], hot, preferred_element_type=jnp.float32)
        mix_s[...] = jnp.zeros_like(mix_s)
        raised = jnp.full((16, LANES), flag, jnp.int32).astype(jnp.float32)
        for r in range(8):
            for s in range(slots):
                mix_s[r, pl.ds(16 * s, 16), :] = moved[16 * r:16 * r + 16, s * LANES:(s + 1) * LANES]
            mix_s[r, pl.ds(LANES - 16, 16), :] = raised
            if r < slots:
                for e in range(rows - 8):
                    mix_s[r, pl.ds(16 * (slots + e), 16), :] = moved[16 * (8 + e):16 * (8 + e) + 16, r * LANES:(r + 1) * LANES]
            stage_s[pl.ds(r, LANES, stride=8), :] = mix_s[r].T
        send_s[...] = stage_s[...].astype(jnp.bfloat16).reshape(send_s.shape)

    def post(a, b):
        pltpu.make_async_remote_copy(
            src_ref=send_s.at[a * across + b], dst_ref=got_s.at[me], send_sem=send_sem, recv_sem=recv_sem,
            device_id=(a, b), device_id_type=pl.DeviceIdType.MESH).start()

    def trade():
        partners(post)
        own = pltpu.make_async_copy(send_s.at[me], got_s.at[me], own_sem)
        own.start()
        return own

    def finish(own):
        src = lax.broadcasted_iota(jnp.int32, (slots * LANES, 2 * LANES), 0)
        dst = lax.broadcasted_iota(jnp.int32, (slots * LANES, 2 * LANES), 1)
        unfold = (((dst & 127) >> 4) == (src >> 7)) & ((src & 127) == 16 * (slots + (dst >> 7)) + (dst & 15))
        unfold = unfold.astype(jnp.float32).astype(jnp.bfloat16)
        slot_of = (lax.broadcasted_iota(jnp.int32, (half_rows, LANES), 1) >> 4).astype(jnp.float32).astype(jnp.bfloat16)
        rest = pl.ds(0, devices - 1)
        every = pltpu.make_async_remote_copy(
            src_ref=send_s.at[rest], dst_ref=got_s.at[rest], send_sem=send_sem, recv_sem=recv_sem,
            device_id=(my_a, columns[1]), device_id_type=pl.DeviceIdType.MESH)
        every.wait_send()
        every.wait_recv()
        own.wait()

        highest = jnp.zeros((8, LANES), jnp.float32)
        for d in range(devices // 2):
            n = got_s[d].astype(jnp.float32)
            o = got_s[devices - 1 - d].astype(jnp.float32)
            highest = jnp.maximum(highest, jnp.maximum(n, o))
            plain_s[pl.ds(rows * d, 8), :] = n + o
            anti_s[pl.ds(rows * d, 8), :] = n - o
            kept_s[pl.ds(8 * d, 8), :] = n + o
            keptanti_s[pl.ds(8 * d, 8), :] = n - o
        weights_in.wait()
        for par, wide, kept in ((0, plain_s, kept_s), (1, anti_s, keptanti_s)):
            folded = jnp.concatenate([kept[pl.ds(s, devices // 2, stride=8), :] for s in range(slots)], axis=1).astype(jnp.bfloat16)
            extra = jnp.dot(folded, unfold, preferred_element_type=jnp.float32)
            for e in range(rows - 8):
                wide[pl.ds(8 + e, devices // 2, stride=rows), :] = extra[:, e * LANES:(e + 1) * LANES]
            values = wide[...].astype(jnp.bfloat16)
            zero = jnp.zeros_like(values)
            picked = jnp.concatenate([jnp.where(slot_of == jnp.bfloat16(s), values, zero) for s in range(slots)], axis=0)
            table = jnp.concatenate([legendre_s[s, par] for s in range(slots)], axis=1)
            turn_s[pl.ds(par, half_rows // 2, stride=2), :] = jnp.dot(table, picked, preferred_element_type=jnp.float32)
        z = turn_s[...].T
        degree = lax.broadcasted_iota(jnp.int32, (16, half_rows), 1)
        for s in range(slots):
            limit = half_rows - waves_ref[me * slots + s]
            result_ref[s] = jnp.where(degree < limit, z[16 * s:16 * s + 16], 0.0)
        lanes = lax.broadcasted_iota(jnp.int32, (8, LANES), 1)
        return jnp.max(jnp.where(lanes >= LANES - 16, highest, 0.0))

    steps.greet, steps.sums, steps.lay_out, steps.trade, steps.finish, steps.others = greet, sums, lay_out, trade, finish, devices - 1
    return steps


def transform_kernel(sizes, pair_length, y_ref, order_ref, waves_ref, legendre_hbm, out_ref, *refs):
    steps = transform_steps(sizes, pair_length, y_ref, waves_ref, legendre_hbm, out_ref, refs[:16], refs[16:])
    barrier = pltpu.get_barrier_semaphore()
    steps.greet(barrier)
    steps.sums()
    steps.lay_out(order_ref[...], 0)
    pl.semaphore_wait(barrier, steps.others)
    steps.finish(steps.trade())


def transform_scratch(pairs, slots, half_rows, pair_length, legendre):
    tiles = pl.cdiv(pair_length, LANES)
    wides = pl.cdiv(tiles * LANES, WIDE)
    f32, b16 = jnp.float32, jnp.bfloat16
    return [
        pltpu.VMEM((2 * WIDE, 2 * LANES), b16),
        pltpu.VMEM((8 * wides * slots, 2 * LANES), f32),
        pltpu.VMEM((2, 16, LANES), f32),
        pltpu.VMEM((8, WIDE * wides), f32),
        pltpu.VMEM((8, WIDE * wides), f32),
        pltpu.VMEM((32 * pairs, half_rows), b16),
        pltpu.VMEM((8, LANES, LANES), f32),
        pltpu.VMEM((8 * LANES, LANES), f32),
        pltpu.VMEM((LANES, 8, LANES), b16),
        pltpu.VMEM((LANES, 8, LANES), b16),
        pltpu.VMEM((half_rows, LANES), f32),
        pltpu.VMEM((half_rows, LANES), f32),
        pltpu.VMEM((8 * LANES // 2, LANES), f32),
        pltpu.VMEM((8 * LANES // 2, LANES), f32),
        pltpu.VMEM((half_rows, LANES), f32),
        pltpu.VMEM(legendre.shape, b16),
        pltpu.SemaphoreType.DMA, pltpu.SemaphoreType.DMA, pltpu.SemaphoreType.DMA, pltpu.SemaphoreType.DMA,
    ]


def transform(y, order, waves, legendre, half_rows, pair_length, sizes):
    pairs = y.shape[0]
    slots = legendre.shape[0]
    vm = pl.BlockSpec(memory_space=pltpu.VMEM)
    f32 = jnp.float32
    return pl.pallas_call(
        functools.partial(transform_kernel, sizes, pair_length),
        out_shape=jax.ShapeDtypeStruct((slots, 16, half_rows), f32),
        in_specs=[vm, vm, pl.BlockSpec(memory_space=pltpu.SMEM), pl.BlockSpec(memory_space=pl.ANY)],
        out_specs=vm,
        scratch_shapes=transform_scratch(pairs, slots, half_rows, pair_length, legendre),
        compiler_params=pltpu.CompilerParams(collective_id=0, has_side_effects=True),
        name="transform",
    )(y, order, waves, legendre)


def on_device(grid, dep_row, dep_lon, lon_frac, lat_frac, wave_slot, legendre):
    half_rows = wave_slot.shape[0]
    _, levels, pairs, pair_length = grid.shape
    axes = ("aa", "ba")
    sizes = (lax.axis_size("aa"), lax.axis_size("ba"))
    devices = sizes[0] * sizes[1]
    first = (lax.axis_index(axes) * pairs).astype(jnp.int32).reshape(1)
    own = jnp.transpose(grid, (0, 2, 1, 3))
    out, result = both(first, own, dep_row, jnp.transpose(dep_lon, (1, 0, 2)), jnp.transpose(lon_frac, (1, 0, 2)),
                       lat_frac, wave_slot, legendre, half_rows, 2 * levels, sizes)
    return (jnp.transpose(out, (0, 2, 1, 3)), jnp.transpose(result, (1, 0, 2)))


def solution(mesh):
    return jax.shard_map(
        on_device,
        mesh=mesh,
        in_specs=(
            P(None, None, ("aa", "ba"), None),
            P(("aa", "ba"), None),
            P(None, ("aa", "ba"), None),
            P(None, ("aa", "ba"), None),
            P(("aa", "ba"), None),
            P(),
            P(("aa", "ba"), None, None, None),
        ),
        out_specs=(P(None, None, ("aa", "ba"), None), P(None, ("aa", "ba"), None)),
        check_vma=False,
    )
```

```python
import functools

import jax
import jax.numpy as jnp
from jax import lax
from jax.experimental import pallas as pl
from jax.experimental.pallas import tpu as pltpu
from jax.sharding import PartitionSpec as P

LANES = 128
WIN = 256
ETILES = 24
EW = ETILES * LANES
MARGIN = 60
ROWS = 11
NOWHERE = 192.0


def row_place(global_row, half_rows):
    northern = global_row < half_rows
    number = jnp.where(northern, global_row + 1, 2 * half_rows - global_row)
    second = number > half_rows // 2
    inner = jnp.where(second, number - half_rows // 2 - 1, half_rows // 2 - number)
    begin = jnp.where(second, 16 + 4 * (half_rows // 2 - inner), 0)
    return jnp.where(northern, inner, half_rows - 1 - inner), begin, 16 + 4 * number


def cubic(t):
    return (
        -t * (t - 1.0) * (t - 2.0) * (1.0 / 6.0),
        (t + 1.0) * (t - 1.0) * (t - 2.0) * 0.5,
        -(t + 1.0) * t * (t - 2.0) * 0.5,
        (t + 1.0) * t * (t - 1.0) * (1.0 / 6.0),
    )


class Stencil:
    pass


def stencil_steps(half_rows, pair_length, first, sources, row_ref, lon_ref, lonf_ref, latf_ref, place_t, ext_s, plan_s, y_s, head_s):
    groups, pairs, levels, _ = sources[1].shape
    fields = groups * levels
    near = pairs + 4
    tiles = pl.cdiv(pair_length, LANES)
    steps = Stencil()

    lane = lax.broadcasted_iota(jnp.int32, (fields, LANES), 1)

    def half_lengths(pair):
        inner = jnp.where(pair < half_rows // 2, pair, half_rows - 1 - pair)
        return 16 + 4 * (half_rows // 2 - inner), 16 + 4 * (half_rows // 2 + 1 + inner)

    def clear():
        ext_s[:, :, pl.ds(0, LANES)] = jnp.zeros((2 * near, fields, LANES), jnp.bfloat16)
        ext_s[:, :, pl.ds(tiles * LANES, EW - tiles * LANES)] = jnp.zeros((2 * near, fields, EW - tiles * LANES), jnp.bfloat16)

    def fill(j):
        ref, at = (sources[0], j) if j < 2 else ((sources[1], j - 2) if j < 2 + pairs else (sources[2], j - 2 - pairs))
        for f in range(groups):
            src = ref[f, at]
            for copy in range(2):
                ext_s[2 * j + copy, pl.ds(levels * f, levels), pl.ds(LANES, pair_length)] = src

    def wrap(copy, tile, shift, low, edge):
        at = pl.ds(pl.multiple_of(tile * LANES, LANES), LANES)
        begin = tile * LANES + shift
        two = ext_s[copy, :, pl.ds(pl.multiple_of((begin >> 7) * LANES, LANES), 2 * LANES)].astype(jnp.float32)
        moved = pltpu.roll(two, (2 * LANES - (begin & 127)) & 255, 1)[:, :LANES]
        spot = lane + tile * LANES
        beyond = spot < edge if low else spot >= edge
        return copy, at, jnp.where(beyond, moved, ext_s[copy, :, at].astype(jnp.float32)).astype(jnp.bfloat16)

    def close(j):
        len0, len1 = half_lengths(first + j - 2)
        wraps = []
        for half in range(2):
            start, length = (len0, len1) if half else (0, len0)
            for i in range(1 + half):
                wraps.append(wrap(2 * j + half, ((start >> 7) if half else 0) + i, length, True, start + LANES))
            for i in range(3):
                wraps.append(wrap(2 * j + half, ((start + length) >> 7) + 1 + i, -length, False, start + length + LANES))
        for copy, at, tile in wraps:
            ext_s[copy, :, at] = tile

    sub8 = lax.broadcasted_iota(jnp.int32, (8, LANES), 0)
    lane8 = lax.broadcasted_iota(jnp.int32, (8, LANES), 1)

    def weigh(tile, fits, width=LANES):
        at = pl.ds(pl.multiple_of(tile * LANES, LANES), LANES)
        some = pl.ds(pl.multiple_of(tile * LANES, LANES), width)
        col = tile * LANES + lane8
        inside = col < pair_length

        def wide(x):
            if width < LANES:
                x = jnp.concatenate([x, jnp.zeros((x.shape[0], LANES - width), x.dtype)], axis=1)
            return x

        for q in range(pairs):
            pair = first + q
            northern = pair < half_rows // 2
            len0, _ = half_lengths(pair)
            second = col >= len0
            inner = jnp.where(northern, pair, half_rows - 1 - pair)

            def base_of(number):
                return jnp.clip(jnp.where(northern, number - 1, 2 * half_rows - number) - 2, 0, 2 * half_rows - 4)

            base = jnp.where(second, base_of(half_rows // 2 + 1 + inner), base_of(half_rows // 2 - inner))
            later = jnp.broadcast_to(wide(row_ref[pl.ds(q, 1), some]), (8, LANES)) > base
            base_k = jnp.where(second, jnp.maximum(tile * LANES - len0, 0), tile * LANES) - MARGIN
            lon = wide(lon_ref[q, :, some])
            lon = jnp.concatenate([lon, lon], axis=0)
            lon = jnp.where(later, pltpu.roll(lon, 1, 0), lon)
            frac = wide(lonf_ref[q, :, some])
            frac = jnp.concatenate([frac, frac], axis=0)
            frac = jnp.where(later, pltpu.roll(frac, 1, 0), frac)
            latw = cubic(jnp.broadcast_to(wide(latf_ref[pl.ds(q, 1), some]), (8, LANES)))
            r = jnp.where(later, sub8 - 1, sub8)
            lat = jnp.zeros((8, LANES), jnp.float32)
            for i in range(4):
                lat = jnp.where(inside & (r == i), latw[i], lat)
            _, begin, length = row_place(jnp.minimum(base + sub8, 2 * half_rows - 1), half_rows)
            rel = lon - 1 - base_k
            rel = jnp.where(rel < 0, rel + length, jnp.where(rel >= length, rel - length, rel))
            short = length <= WIN - 4
            rel = jnp.where(short, lon, rel)
            bad = (lat != 0.0) & ((rel < 0) | (rel > WIN - 4))
            fits = jnp.maximum(fits, bad.astype(jnp.int32))
            place = ((begin + jnp.where(short, -1, base_k) + LANES) & 127) + rel
            block = (place >> 4) & 15
            ws = cubic(frac)
            for o in range(4):
                plan_s[q * ROWS + o, :, at] = lat * ws[o]
                plan_s[q * ROWS + 4 + o, :, at] = ((place + o) & 15).astype(jnp.float32)
            plan_s[q * ROWS + 8, :, at] = block.astype(jnp.float32)
            plan_s[q * ROWS + 9, :, at] = ((block + 1) & 15).astype(jnp.float32)
            plan_s[q * ROWS + 10, :, at] = (lon + begin).astype(jnp.float32)
        return fits

    def weigh_all():
        worst = lax.fori_loop(0, pair_length // LANES, weigh, jnp.zeros((8, LANES), jnp.int32))
        if pair_length % LANES:
            worst = weigh(tiles - 1, worst, pair_length % LANES)
        return worst

    node = lax.broadcasted_iota(jnp.int32, (16, LANES), 0).astype(jnp.float32).astype(jnp.bfloat16)
    zero16 = jnp.zeros((16, LANES), jnp.bfloat16)

    def spread(mine, weight, rest, block, after):
        v = zero16
        for o in (3, 2, 1, 0):
            v = jnp.where(node == rest[o], weight[o], v)
        block = jnp.where(mine, jnp.where(node < rest[0], after, block), jnp.bfloat16(NOWHERE))
        return [jnp.where(block == jnp.bfloat16(a), v, zero16) for a in range(WIN // 16)]

    def plan(d, i, q, at):
        return jnp.broadcast_to(plan_s[q * ROWS + i, pl.ds(d, 1), at], (16, LANES))

    def packed(x):
        return x.astype(jnp.bfloat16)

    def locate():
        for q in range(pairs):
            pair = first + q
            northern = pair < half_rows // 2
            inner = jnp.where(northern, pair, half_rows - 1 - pair)
            for half in range(2):
                number = half_rows // 2 + 1 + inner if half else half_rows // 2 - inner
                g = jnp.where(northern, number - 1, 2 * half_rows - number)
                base = jnp.clip(g - 2, 0, 2 * half_rows - 4)
                for d in range(5):
                    pair_row, begin, length = row_place(jnp.minimum(base + d, 2 * half_rows - 1), half_rows)
                    short = length <= WIN - 4
                    copy = 2 * jnp.clip(pair_row - first + 2, 0, near - 1) + (begin > 0).astype(jnp.int32)
                    at = 3 * ((2 * q + half) * 5 + d)
                    place_t[at] = copy
                    place_t[at + 1] = begin + LANES + jnp.where(short, -1, -MARGIN)
                    place_t[at + 2] = jnp.where(short, 0, 1)

    def unit_scalars(q, u):
        len0, _ = half_lengths(first + q)
        straddle = len0 >> 7
        half = (u > straddle).astype(jnp.int32)
        tile = u - half
        k0 = jnp.where(half == 1, jnp.maximum(tile * LANES - len0, 0), tile * LANES)
        return len0, straddle, half, tile, 15 * (2 * q + half), k0

    lane16 = lax.broadcasted_iota(jnp.int32, (16, LANES), 1).astype(jnp.float32).astype(jnp.bfloat16)

    def own_half(half, tile, len0):
        edge = jnp.clip(len0 - tile * LANES, 0, LANES)
        low = jnp.where(half == 1, edge, 0).astype(jnp.float32)
        high = jnp.where(half == 1, LANES, edge).astype(jnp.float32)
        spread_low = jnp.full((16, LANES), low, jnp.float32).astype(jnp.bfloat16)
        spread_high = jnp.full((16, LANES), high, jnp.float32).astype(jnp.bfloat16)
        return (lane16 >= spread_low) & (lane16 < spread_high)

    def finish(q, u, straddle, tile, total, carry):
        total = total + jnp.where(u == straddle + 1, carry, 0.0)
        at = pl.ds(pl.multiple_of(tile * LANES, LANES), LANES)
        y_s[q, :, at] = total.astype(jnp.bfloat16)
        head_s[q, :, at] = total[:head_s.shape[1]].astype(jnp.bfloat16)
        return total

    def near_units(chosen):
        def unit(q, u, carry):
            len0, straddle, half, tile, base, k0 = unit_scalars(q, u)
            at = pl.ds(pl.multiple_of(tile * LANES, LANES), LANES)
            mine = own_half(half, tile, len0)
            rows, weights = [], []
            for d in range(5):
                where_row = place_t[base + 3 * d]
                begin = place_t[base + 3 * d + 1] + place_t[base + 3 * d + 2] * k0
                s = begin & 127
                first_tile = pl.multiple_of((begin >> 7) * LANES, LANES)
                row = [packed(plan(d, i, q, at)) for i in range(10)]
                weights += spread(mine, row[:4], row[4:8], row[8], row[9])
                three = ext_s[where_row, :, pl.ds(first_tile, 3 * LANES)]
                rows += [jnp.where(lane >= s, three[:, :LANES], three[:, 2 * LANES:]), three[:, LANES:2 * LANES]]
            total = jnp.dot(jnp.concatenate(rows, axis=1), jnp.concatenate(weights, axis=0),
                            preferred_element_type=jnp.float32)
            return finish(q, u, straddle, tile, total, carry)

        lax.fori_loop(0, tiles + 1, lambda u, carry: tuple(unit(q, u, c) for q, c in zip(chosen, carry)),
                      (jnp.zeros((fields, LANES), jnp.float32),) * len(chosen))

    def any_units():
        def unit(q, u, carry):
            len0, straddle, half, tile, base, _ = unit_scalars(q, u)
            at = pl.ds(pl.multiple_of(tile * LANES, LANES), LANES)
            mine = own_half(half, tile, len0)

            def window(w, total):
                rows, weights = [], []
                for d in range(5):
                    where_row = place_t[base + 3 * d]
                    place = (plan(d, 10, q, at) + (LANES - 1)).astype(jnp.int32) - w * WIN
                    block = jnp.clip(place >> 4, -2, 18)
                    rest = [packed(((place + o) & 15).astype(jnp.float32)) for o in range(4)]
                    weight = [packed(plan(d, o, q, at)) for o in range(4)]
                    weights += spread(mine, weight, rest, packed(block.astype(jnp.float32)), packed((block + 1).astype(jnp.float32)))
                    rows.append(ext_s[where_row, :, pl.ds(pl.multiple_of(w * WIN, WIN), WIN)])
                return total + jnp.dot(jnp.concatenate(rows, axis=1), jnp.concatenate(weights, axis=0),
                                       preferred_element_type=jnp.float32)

            total = lax.fori_loop(0, EW // WIN, window, jnp.zeros((fields, LANES), jnp.float32))
            return finish(q, u, straddle, tile, total, carry)

        lax.fori_loop(0, tiles + 1, lambda u, carry: tuple(unit(q, u, carry[q]) for q in range(pairs)),
                      (jnp.zeros((fields, LANES), jnp.float32),) * pairs)

    def deliver(out_ref):
        for f in range(groups):
            for q in range(pairs):
                out_ref[f, q] = y_s[q, pl.ds(levels * f, levels), pl.ds(0, pair_length)]

    steps.clear, steps.fill, steps.close, steps.weigh_all, steps.locate = clear, fill, close, weigh_all, locate
    steps.near_units, steps.any_units, steps.deliver, steps.near = near_units, any_units, deliver, near
    return steps


def stencil_scratch(pairs, fields, pair_length):
    padded = pl.cdiv(pair_length, LANES) * LANES
    return [
        pltpu.SMEM((30 * pairs,), jnp.int32),
        pltpu.VMEM((2 * (pairs + 4), fields, EW), jnp.bfloat16),
        pltpu.VMEM((pairs * ROWS, 8, padded), jnp.float32),
        pltpu.VMEM((pairs, fields, padded), jnp.bfloat16),
    ]


def by_slot_then_device(wave, devices):
    count = wave.shape[1]
    slots = count // devices
    wanted = lax.broadcasted_iota(jnp.int32, (1, count), 1)
    wanted = slots * (wanted % devices) + wanted // devices
    moves = (lax.broadcasted_iota(jnp.int32, (count, count), 0) == wanted).astype(jnp.float32).astype(jnp.bfloat16)
    high, low = wave // 8, wave % 8
    sub = lax.broadcasted_iota(jnp.int32, (16, count), 0)
    digits = jnp.where(sub == 0, high, jnp.where(sub == 1, low, 0)).astype(jnp.float32).astype(jnp.bfloat16)
    moved = jnp.dot(digits, moves, preferred_element_type=jnp.float32)
    return (8.0 * moved[0:1] + moved[1:2]).astype(jnp.int32)


def whole_kernel(sizes, half_rows, pair_length, grid_hbm, row_hbm, lon_hbm, lonf_hbm, latf_hbm, wave_ref, waves_ref, legendre_hbm,
                 out_ref, result_ref, far_ref, before_s, after_s, order_ref,
                 own_s, row_s, lon_s, lonf_s, latf_s, place_t, ext_s, plan_s, y_s, head_s,
                 in_sem, halo_send_sem, halo_recv_sem, *refs):
    along, across = sizes
    devices = along * across
    pairs = own_s.shape[1]
    me = lax.axis_index("aa") * across + lax.axis_index("ba")
    up = lax.rem(me + 1, devices)
    down = lax.rem(me + devices - 1, devices)

    def where(device):
        return (device // across, lax.rem(device, across))

    after_steps = transform_steps(sizes, pair_length, head_s, waves_ref, legendre_hbm, result_ref, refs[:14], refs[14:])
    barrier = pltpu.get_barrier_semaphore()
    loads = [pltpu.make_async_copy(src, dst, in_sem.at[i]) for i, (src, dst) in enumerate((
        (row_hbm, row_s), (lon_hbm, lon_s), (lonf_hbm, lonf_s), (latf_hbm, latf_s), (grid_hbm, own_s)))]
    for load in loads:
        load.start()
    after_steps.greet(barrier)

    steps = stencil_steps(half_rows, pair_length, me * pairs, (before_s, own_s, after_s), row_s, lon_s, lonf_s, latf_s,
                          place_t, ext_s, plan_s, y_s, head_s)
    steps.clear()
    for load in loads:
        load.wait()
    flag = jnp.max(steps.weigh_all())

    pl.semaphore_wait(barrier, devices - 1)
    sends = []
    for i, (begin, dst, device) in enumerate(((pairs - 2, before_s, up), (0, after_s, down))):
        sends.append(pltpu.make_async_remote_copy(
            src_ref=grid_hbm.at[:, pl.ds(begin, 2)], dst_ref=dst, send_sem=halo_send_sem.at[i], recv_sem=halo_recv_sem.at[i],
            device_id=where(device), device_id_type=pl.DeviceIdType.MESH))
        sends[-1].start()
    for j in range(2, 2 + pairs):
        steps.fill(j)
    for j in range(2, 2 + pairs):
        steps.close(j)
    order = by_slot_then_device(wave_ref[...].reshape(1, half_rows), devices)
    order_ref[...] = order
    steps.locate()
    inner = tuple(range(2, pairs - 2))
    steps.near_units(inner)
    for send in sends:
        send.wait()
    for j in (0, 1, 2 + pairs, 3 + pairs):
        steps.fill(j)
    for j in (0, 1, 2 + pairs, 3 + pairs):
        steps.close(j)
    steps.near_units(tuple(q for q in range(pairs) if q not in inner))
    after_steps.sums()
    after_steps.lay_out(order_ref[...], flag)
    own = after_steps.trade()
    steps.deliver(out_ref)
    far_ref[0] = (after_steps.finish(own) > 0.0).astype(jnp.int32)


def far_kernel(half_rows, pair_length, first_ref, before_ref, own_ref, after_ref, row_ref, lon_ref, lonf_ref, latf_ref,
               out_ref, head_ref, place_t, ext_s, plan_s, y_s):
    steps = stencil_steps(half_rows, pair_length, first_ref[0], (before_ref, own_ref, after_ref), row_ref, lon_ref, lonf_ref, latf_ref,
                          place_t, ext_s, plan_s, y_s, head_ref)
    steps.locate()
    steps.clear()
    steps.weigh_all()
    for j in range(steps.near):
        steps.fill(j)
    for j in range(steps.near):
        steps.close(j)
    steps.any_units()
    steps.deliver(out_ref)


def both(first, grid, dep_row, dep_lon, lon_frac, lat_frac, wave_slot, legendre, half_rows, spectral_fields, sizes):
    groups, pairs, levels, pair_length = grid.shape
    fields = groups * levels
    slots = legendre.shape[0]
    padded = pl.cdiv(pair_length, LANES) * LANES
    b16, f32, i32 = jnp.bfloat16, jnp.float32, jnp.int32
    vm, anywhere, scalars = (pl.BlockSpec(memory_space=m) for m in (pltpu.VMEM, pl.ANY, pltpu.SMEM))
    halo = jax.ShapeDtypeStruct((groups, 2, levels, pair_length), b16)
    head = jax.ShapeDtypeStruct((pairs, spectral_fields, padded), b16)
    full = jax.ShapeDtypeStruct(grid.shape, b16)
    stencil = stencil_scratch(pairs, fields, pair_length)
    local = [
        pltpu.VMEM(grid.shape, b16), pltpu.VMEM(dep_row.shape, i32), pltpu.VMEM(dep_lon.shape, i32), pltpu.VMEM(lon_frac.shape, f32), pltpu.VMEM(lat_frac.shape, f32),
    ] + stencil + [pltpu.VMEM(head.shape, b16)]
    out, result, far, before, after, order = pl.pallas_call(
        functools.partial(whole_kernel, sizes, half_rows, pair_length),
        out_shape=(full, jax.ShapeDtypeStruct((slots, 16, half_rows), f32), jax.ShapeDtypeStruct((1,), i32), halo, halo,
                   jax.ShapeDtypeStruct((1, half_rows), i32)),
        in_specs=[anywhere] * 5 + [vm, scalars, anywhere],
        out_specs=(vm, vm, scalars, vm, vm, vm),
        scratch_shapes=local + [pltpu.SemaphoreType.DMA((5,)), pltpu.SemaphoreType.DMA((2,)), pltpu.SemaphoreType.DMA((2,))] + transform_scratch(pairs, slots, half_rows, pair_length, legendre),
        compiler_params=pltpu.CompilerParams(collective_id=1, has_side_effects=True),
        name="whole",
    )(grid, dep_row, dep_lon, lon_frac, lat_frac, wave_slot, wave_slot, legendre)

    def again():
        redone, first_fields = pl.pallas_call(
            functools.partial(far_kernel, half_rows, pair_length),
            out_shape=(full, head),
            in_specs=[scalars] + [vm] * 7,
            out_specs=(vm, vm),
            scratch_shapes=stencil,
            name="far",
        )(first, before, grid, after, dep_row, dep_lon, lon_frac, lat_frac)
        return redone, transform(first_fields, order, wave_slot, legendre, half_rows, pair_length, sizes)

    return lax.cond(far[0] > 0, again, lambda: (out, result))

WIDE = 256

COS = (1, -19.7392087, 64.9393842, -85.4565372, 60.2407014, -26.3960673, 7.77462739, -1.42354417)
SIN = (6.28318531, -41.3417022, 81.6052456, -76.7057546, 42.0572162, -15.0833301, 3.7717259, -0.609657301)


def cos_sin_turns(prod, length, inverse):
    turns = jnp.floor(prod * inverse + 0.5)
    t = (prod - turns * length) * inverse
    x = t * t
    c = jnp.full_like(x, COS[-1])
    for a in COS[-2::-1]:
        c = c * x + a
    s = jnp.full_like(x, SIN[-1])
    for a in SIN[-2::-1]:
        s = s * x + a
    return c, s * t


def transform_steps(sizes, pair_length, y_ref, waves_ref, legendre_hbm, result_ref, scratch, sems):
    (table_s, sums_s, back_s, turn_c, turn_n, four_s, mix_s, stage_s, send_s, got_s, plain_s, anti_s, turn_s, legendre_s) = scratch
    legendre_sem, own_sem, send_sem, recv_sem = sems
    along, across = sizes
    devices = along * across
    pairs = y_ref.shape[0]
    slots = legendre_s.shape[0]
    half_rows = slots * devices
    rows = 2 * pairs
    tiles = pl.cdiv(pair_length, LANES)
    my_a = lax.axis_index("aa")
    my_b = lax.axis_index("ba")
    me = my_a * across + my_b
    first = me * pairs
    north = me < devices // 2
    parts = 8
    wides = pl.cdiv(tiles * LANES, WIDE)

    steps = Stencil()

    weights_in = pltpu.make_async_copy(legendre_hbm, legendre_s, legendre_sem)

    columns = [lax.rem(my_b + i, across) for i in range(across)]

    def partners(act):
        def others(i, _):
            a = lax.rem(my_a + along // 2 + (1 - 2 * lax.rem(i, 2)) * ((i + 1) // 2), along)
            for b in range(across):
                act(a, columns[b])
            return 0

        lax.fori_loop(0, along - 1, others, 0)
        for b in range(1, across):
            act(my_a, columns[b])

    def greet(barrier):
        weights_in.start()
        partners(lambda a, b: pl.semaphore_signal(barrier, inc=1, device_id=(a, b), device_id_type=pl.DeviceIdType.MESH))

    def one(q, half):
        table, sums_of, back, turns_c, turns_n = (x.at[half] for x in (table_s, sums_s, back_s, turn_c, turn_n))
        pair = first + q
        inner = jnp.where(north, pair, half_rows - 1 - pair)
        len0 = 16 + 4 * (half_rows // 2 - inner)
        start = len0 if half else 0
        whole = 16 + 4 * (half_rows // 2 + 1 + inner) if half else len0
        length = jnp.full((1, LANES), whole, jnp.int32).astype(jnp.float32)
        inverse = 1.0 / length

        def line(n):
            return lax.broadcasted_iota(jnp.int32, (n, LANES), 0)

        wave = lax.broadcasted_iota(jnp.int32, (16, LANES), 1)
        fine_c, fine_s = cos_sin_turns((wave * line(16)).astype(jnp.float32), length, inverse)
        step_c, step_s = cos_sin_turns((wave * (16 * line(16))).astype(jnp.float32), length, inverse)
        for a in range(WIDE // 16):
            ca, sa = step_c[a:a + 1], step_s[a:a + 1]
            cosine = ca * fine_c - sa * fine_s
            sine = sa * fine_c + ca * fine_s
            top, bottom = pl.ds(16 * a, 16), pl.ds(WIDE + 16 * a, 16)
            left, right = pl.ds(0, LANES), pl.ds(LANES, LANES)
            table[top, left] = cosine.astype(jnp.bfloat16)
            table[top, right] = sine.astype(jnp.bfloat16)
            table[bottom, left] = (-sine).astype(jnp.bfloat16)
            table[bottom, right] = cosine.astype(jnp.bfloat16)
        tile_c, tile_s = cos_sin_turns((wave * (WIDE * line(16) - start)).astype(jnp.float32), length, inverse)
        back[0], back[1] = tile_c, tile_s
        lane = lax.broadcasted_iota(jnp.int32, (parts, LANES), 1)
        part_c, part_s = cos_sin_turns((LANES * line(8) * (WIDE * lane - start)).astype(jnp.float32), length, inverse)
        shifts = [cos_sin_turns((LANES * line(8) * (lane + i * LANES)).astype(jnp.float32), length, inverse) for i in range(2)]
        for t in range(wides):
            pc, ps = part_c[:, t:t + 1], part_s[:, t:t + 1]
            for i in range(2):
                sc, ss = shifts[i]
                at = pl.ds(t * WIDE + i * LANES, LANES)
                turns_c[:, at] = pc * sc - ps * ss
                turns_n[:, at] = ps * sc + pc * ss
        blocks = [[None] * (2 * 2) for _ in range(wides * slots)]
        for t in range(wides):
            for i in range(2):
                at = t * WIDE + i * LANES
                if at < tiles * LANES:
                    col = lane + at
                    mine = (col >= start) & (col < start + whole)
                    v = jnp.where(mine, y_ref[q, :, pl.ds(at, LANES)].astype(jnp.float32)[:parts], 0.0)
                for w in range(slots):
                    row = blocks[w * wides + t]
                    if at < tiles * LANES:
                        row[i] = v * turns_c[pl.ds(w, 1), pl.ds(at, LANES)]
                        row[2 + i] = v * turns_n[pl.ds(w, 1), pl.ds(at, LANES)]
                    else:
                        row[i] = row[2 + i] = jnp.zeros((parts, LANES), jnp.float32)
        stacked = jnp.concatenate([jnp.concatenate(row, axis=1) for row in blocks], axis=0).astype(jnp.bfloat16)
        sums_of[...] = jnp.dot(stacked, table[...], preferred_element_type=jnp.float32)
        place = 2 * jnp.where(north, q, pairs - 1 - q) + half
        for w in range(slots):
            real = jnp.zeros((parts, LANES), jnp.float32)
            imag = jnp.zeros((parts, LANES), jnp.float32)
            for t in range(wides):
                at = pl.ds(parts * (w * wides + t), parts)
                c, s = sums_of[at, pl.ds(0, LANES)], sums_of[at, pl.ds(LANES, LANES)]
                tc, ts = back[0, pl.ds(t, 1), :], back[1, pl.ds(t, 1), :]
                real = real + (tc * c - ts * s)
                imag = imag - (ts * c + tc * s)
            waves = lax.broadcasted_iota(jnp.int32, (1, LANES), 1) + w * LANES
            keep = jnp.where(2 * waves < whole, inverse, 0.0)
            four_s[pl.ds(pl.multiple_of(place * 16, 16), 16), pl.ds(w * LANES, LANES)] = jnp.concatenate(
                [real * keep, imag * keep], axis=0).astype(jnp.bfloat16)

    def sums():
        def step(q, _):
            for half in range(2):
                one(q, half)
            return 0

        lax.fori_loop(0, pairs, step, 0)

    def lay_out(order, flag):
        hot = (lax.broadcasted_iota(jnp.int32, (half_rows, half_rows), 0) == order).astype(jnp.float32).astype(jnp.bfloat16)
        moved = jnp.dot(four_s[...], hot, preferred_element_type=jnp.float32)
        mix_s[...] = jnp.zeros_like(mix_s)
        raised = jnp.full((16, LANES), flag, jnp.int32).astype(jnp.float32)
        for r in range(8):
            for s in range(slots):
                mix_s[r, pl.ds(16 * s, 16), :] = moved[16 * r:16 * r + 16, s * LANES:(s + 1) * LANES]
            mix_s[r, pl.ds(LANES - 16, 16), :] = raised
            if r < slots:
                for e in range(rows - 8):
                    mix_s[r, pl.ds(16 * (slots + e), 16), :] = moved[16 * (8 + e):16 * (8 + e) + 16, r * LANES:(r + 1) * LANES]
            stage_s[pl.ds(r, LANES, stride=8), :] = mix_s[r].T
        send_s[...] = stage_s[...].astype(jnp.bfloat16).reshape(send_s.shape)

    def post(a, b):
        pltpu.make_async_remote_copy(
            src_ref=send_s.at[a * across + b], dst_ref=got_s.at[me], send_sem=send_sem, recv_sem=recv_sem,
            device_id=(a, b), device_id_type=pl.DeviceIdType.MESH).start()

    def trade():
        partners(post)
        own = pltpu.make_async_copy(send_s.at[me], got_s.at[me], own_sem)
        own.start()
        return own

    def finish(own):
        src = lax.broadcasted_iota(jnp.int32, (slots * LANES, 2 * LANES), 0)
        dst = lax.broadcasted_iota(jnp.int32, (slots * LANES, 2 * LANES), 1)
        unfold = (((dst & 127) >> 4) == (src >> 7)) & ((src & 127) == 16 * (slots + (dst >> 7)) + (dst & 15))
        unfold = unfold.astype(jnp.float32).astype(jnp.bfloat16)
        slot_of = (lax.broadcasted_iota(jnp.int32, (half_rows, LANES), 1) >> 4).astype(jnp.float32).astype(jnp.bfloat16)
        rest = pl.ds(0, devices - 1)
        every = pltpu.make_async_remote_copy(
            src_ref=send_s.at[rest], dst_ref=got_s.at[rest], send_sem=send_sem, recv_sem=recv_sem,
            device_id=(my_a, columns[1]), device_id_type=pl.DeviceIdType.MESH)
        every.wait_send()
        every.wait_recv()
        own.wait()

        highest = jnp.zeros((8, LANES), jnp.float32)
        for d in range(devices // 2):
            n = got_s[d].astype(jnp.float32)
            o = got_s[devices - 1 - d].astype(jnp.float32)
            highest = jnp.maximum(highest, jnp.maximum(n, o))
            plain_s[pl.ds(rows * d, 8), :] = n + o
            anti_s[pl.ds(rows * d, 8), :] = n - o
        weights_in.wait()
        for par, wide in ((0, plain_s), (1, anti_s)):
            folded = jnp.concatenate([wide[pl.ds(s, devices // 2, stride=rows), :] for s in range(slots)], axis=1).astype(jnp.bfloat16)
            extra = jnp.dot(folded, unfold, preferred_element_type=jnp.float32)
            for e in range(rows - 8):
                wide[pl.ds(8 + e, devices // 2, stride=rows), :] = extra[:, e * LANES:(e + 1) * LANES]
            values = wide[...].astype(jnp.bfloat16)
            zero = jnp.zeros_like(values)
            picked = jnp.concatenate([jnp.where(slot_of == jnp.bfloat16(s), values, zero) for s in range(slots)], axis=0)
            table = jnp.concatenate([legendre_s[s, par] for s in range(slots)], axis=1)
            turn_s[pl.ds(par, half_rows // 2, stride=2), :] = jnp.dot(table, picked, preferred_element_type=jnp.float32)
        z = turn_s[...].T
        degree = lax.broadcasted_iota(jnp.int32, (16, half_rows), 1)
        for s in range(slots):
            limit = half_rows - waves_ref[me * slots + s]
            result_ref[s] = jnp.where(degree < limit, z[16 * s:16 * s + 16], 0.0)
        lanes = lax.broadcasted_iota(jnp.int32, (8, LANES), 1)
        return jnp.max(jnp.where(lanes >= LANES - 16, highest, 0.0))

    steps.greet, steps.sums, steps.lay_out, steps.trade, steps.finish, steps.others = greet, sums, lay_out, trade, finish, devices - 1
    return steps


def transform_kernel(sizes, pair_length, y_ref, order_ref, waves_ref, legendre_hbm, out_ref, *refs):
    steps = transform_steps(sizes, pair_length, y_ref, waves_ref, legendre_hbm, out_ref, refs[:14], refs[14:])
    barrier = pltpu.get_barrier_semaphore()
    steps.greet(barrier)
    steps.sums()
    steps.lay_out(order_ref[...], 0)
    pl.semaphore_wait(barrier, steps.others)
    steps.finish(steps.trade())


def transform_scratch(pairs, slots, half_rows, pair_length, legendre):
    tiles = pl.cdiv(pair_length, LANES)
    wides = pl.cdiv(tiles * LANES, WIDE)
    f32, b16 = jnp.float32, jnp.bfloat16
    return [
        pltpu.VMEM((2, 2 * WIDE, 2 * LANES), b16),
        pltpu.VMEM((2, 8 * wides * slots, 2 * LANES), f32),
        pltpu.VMEM((2, 2, 16, LANES), f32),
        pltpu.VMEM((2, 8, WIDE * wides), f32),
        pltpu.VMEM((2, 8, WIDE * wides), f32),
        pltpu.VMEM((32 * pairs, half_rows), b16),
        pltpu.VMEM((8, LANES, LANES), f32),
        pltpu.VMEM((8 * LANES, LANES), f32),
        pltpu.VMEM((LANES, 8, LANES), b16),
        pltpu.VMEM((LANES, 8, LANES), b16),
        pltpu.VMEM((half_rows, LANES), f32),
        pltpu.VMEM((half_rows, LANES), f32),
        pltpu.VMEM((half_rows, LANES), f32),
        pltpu.VMEM(legendre.shape, b16),
        pltpu.SemaphoreType.DMA, pltpu.SemaphoreType.DMA, pltpu.SemaphoreType.DMA, pltpu.SemaphoreType.DMA,
    ]


def transform(y, order, waves, legendre, half_rows, pair_length, sizes):
    pairs = y.shape[0]
    slots = legendre.shape[0]
    vm = pl.BlockSpec(memory_space=pltpu.VMEM)
    f32 = jnp.float32
    return pl.pallas_call(
        functools.partial(transform_kernel, sizes, pair_length),
        out_shape=jax.ShapeDtypeStruct((slots, 16, half_rows), f32),
        in_specs=[vm, vm, pl.BlockSpec(memory_space=pltpu.SMEM), pl.BlockSpec(memory_space=pl.ANY)],
        out_specs=vm,
        scratch_shapes=transform_scratch(pairs, slots, half_rows, pair_length, legendre),
        compiler_params=pltpu.CompilerParams(collective_id=0, has_side_effects=True),
        name="transform",
    )(y, order, waves, legendre)


def on_device(grid, dep_row, dep_lon, lon_frac, lat_frac, wave_slot, legendre):
    half_rows = wave_slot.shape[0]
    _, levels, pairs, pair_length = grid.shape
    axes = ("aa", "ba")
    sizes = (lax.axis_size("aa"), lax.axis_size("ba"))
    devices = sizes[0] * sizes[1]
    first = (lax.axis_index(axes) * pairs).astype(jnp.int32).reshape(1)
    own = jnp.transpose(grid, (0, 2, 1, 3))
    out, result = both(first, own, dep_row, jnp.transpose(dep_lon, (1, 0, 2)), jnp.transpose(lon_frac, (1, 0, 2)),
                       lat_frac, wave_slot, legendre, half_rows, 2 * levels, sizes)
    return (jnp.transpose(out, (0, 2, 1, 3)), jnp.transpose(result, (1, 0, 2)))


def solution(mesh):
    return jax.shard_map(
        on_device,
        mesh=mesh,
        in_specs=(
            P(None, None, ("aa", "ba"), None),
            P(("aa", "ba"), None),
            P(None, ("aa", "ba"), None),
            P(None, ("aa", "ba"), None),
            P(("aa", "ba"), None),
            P(),
            P(("aa", "ba"), None, None, None),
        ),
        out_specs=(P(None, None, ("aa", "ba"), None), P(None, ("aa", "ba"), None)),
        check_vma=False,
    )
```

```python
import functools

import jax
import jax.numpy as jnp
from jax import lax
from jax.experimental import pallas as pl
from jax.experimental.pallas import tpu as pltpu
from jax.sharding import PartitionSpec as P

LANES = 128
WIN = 256
ETILES = 24
EW = ETILES * LANES
MARGIN = 60
ROWS = 11
NOWHERE = 192.0


def row_place(global_row, half_rows):
    northern = global_row < half_rows
    number = jnp.where(northern, global_row + 1, 2 * half_rows - global_row)
    second = number > half_rows // 2
    inner = jnp.where(second, number - half_rows // 2 - 1, half_rows // 2 - number)
    begin = jnp.where(second, 16 + 4 * (half_rows // 2 - inner), 0)
    return jnp.where(northern, inner, half_rows - 1 - inner), begin, 16 + 4 * number


def cubic(t):
    return (
        -t * (t - 1.0) * (t - 2.0) * (1.0 / 6.0),
        (t + 1.0) * (t - 1.0) * (t - 2.0) * 0.5,
        -(t + 1.0) * t * (t - 2.0) * 0.5,
        (t + 1.0) * t * (t - 1.0) * (1.0 / 6.0),
    )


class Stencil:
    pass


def stencil_steps(half_rows, pair_length, first, sources, row_ref, lon_ref, lonf_ref, latf_ref, place_t, ext_s, plan_s, y_s, head_s):
    groups, pairs, levels, _ = sources[1].shape
    fields = groups * levels
    near = pairs + 4
    tiles = pl.cdiv(pair_length, LANES)
    steps = Stencil()

    lane = lax.broadcasted_iota(jnp.int32, (fields, LANES), 1)

    def half_lengths(pair):
        inner = jnp.where(pair < half_rows // 2, pair, half_rows - 1 - pair)
        return 16 + 4 * (half_rows // 2 - inner), 16 + 4 * (half_rows // 2 + 1 + inner)

    def clear():
        ext_s[:, :, pl.ds(0, LANES)] = jnp.zeros((2 * near, fields, LANES), jnp.bfloat16)
        ext_s[:, :, pl.ds(tiles * LANES, EW - tiles * LANES)] = jnp.zeros((2 * near, fields, EW - tiles * LANES), jnp.bfloat16)

    def fill(j):
        ref, at = (sources[0], j) if j < 2 else ((sources[1], j - 2) if j < 2 + pairs else (sources[2], j - 2 - pairs))
        for f in range(groups):
            src = ref[f, at]
            for copy in range(2):
                ext_s[2 * j + copy, pl.ds(levels * f, levels), pl.ds(LANES, pair_length)] = src

    def wrap(copy, tile, shift, low, edge):
        at = pl.ds(pl.multiple_of(tile * LANES, LANES), LANES)
        begin = tile * LANES + shift
        two = ext_s[copy, :, pl.ds(pl.multiple_of((begin >> 7) * LANES, LANES), 2 * LANES)].astype(jnp.float32)
        moved = pltpu.roll(two, (2 * LANES - (begin & 127)) & 255, 1)[:, :LANES]
        spot = lane + tile * LANES
        beyond = spot < edge if low else spot >= edge
        return copy, at, jnp.where(beyond, moved, ext_s[copy, :, at].astype(jnp.float32)).astype(jnp.bfloat16)

    def close(j):
        len0, len1 = half_lengths(first + j - 2)
        wraps = []
        for half in range(2):
            start, length = (len0, len1) if half else (0, len0)
            for i in range(1 + half):
                wraps.append(wrap(2 * j + half, ((start >> 7) if half else 0) + i, length, True, start + LANES))
            for i in range(3):
                wraps.append(wrap(2 * j + half, ((start + length) >> 7) + 1 + i, -length, False, start + length + LANES))
        for copy, at, tile in wraps:
            ext_s[copy, :, at] = tile

    sub8 = lax.broadcasted_iota(jnp.int32, (8, LANES), 0)
    lane8 = lax.broadcasted_iota(jnp.int32, (8, LANES), 1)

    def weigh(tile, fits, width=LANES):
        at = pl.ds(pl.multiple_of(tile * LANES, LANES), LANES)
        some = pl.ds(pl.multiple_of(tile * LANES, LANES), width)
        col = tile * LANES + lane8
        inside = col < pair_length

        def wide(x):
            if width < LANES:
                x = jnp.concatenate([x, jnp.zeros((x.shape[0], LANES - width), x.dtype)], axis=1)
            return x

        for q in range(pairs):
            pair = first + q
            northern = pair < half_rows // 2
            len0, _ = half_lengths(pair)
            second = col >= len0
            inner = jnp.where(northern, pair, half_rows - 1 - pair)

            def base_of(number):
                return jnp.clip(jnp.where(northern, number - 1, 2 * half_rows - number) - 2, 0, 2 * half_rows - 4)

            base = jnp.where(second, base_of(half_rows // 2 + 1 + inner), base_of(half_rows // 2 - inner))
            later = jnp.broadcast_to(wide(row_ref[pl.ds(q, 1), some]), (8, LANES)) > base
            base_k = jnp.where(second, jnp.maximum(tile * LANES - len0, 0), tile * LANES) - MARGIN
            lon = wide(lon_ref[q, :, some])
            lon = jnp.concatenate([lon, lon], axis=0)
            lon = jnp.where(later, pltpu.roll(lon, 1, 0), lon)
            frac = wide(lonf_ref[q, :, some])
            frac = jnp.concatenate([frac, frac], axis=0)
            frac = jnp.where(later, pltpu.roll(frac, 1, 0), frac)
            latw = cubic(jnp.broadcast_to(wide(latf_ref[pl.ds(q, 1), some]), (8, LANES)))
            r = jnp.where(later, sub8 - 1, sub8)
            lat = jnp.zeros((8, LANES), jnp.float32)
            for i in range(4):
                lat = jnp.where(inside & (r == i), latw[i], lat)
            _, begin, length = row_place(jnp.minimum(base + sub8, 2 * half_rows - 1), half_rows)
            rel = lon - 1 - base_k
            rel = jnp.where(rel < 0, rel + length, jnp.where(rel >= length, rel - length, rel))
            short = length <= WIN - 4
            rel = jnp.where(short, lon, rel)
            bad = (lat != 0.0) & ((rel < 0) | (rel > WIN - 4))
            fits = jnp.maximum(fits, bad.astype(jnp.int32))
            place = ((begin + jnp.where(short, -1, base_k) + LANES) & 127) + rel
            block = (place >> 4) & 15
            ws = cubic(frac)
            for o in range(4):
                plan_s[q * ROWS + o, :, at] = lat * ws[o]
                plan_s[q * ROWS + 4 + o, :, at] = ((place + o) & 15).astype(jnp.float32)
            plan_s[q * ROWS + 8, :, at] = block.astype(jnp.float32)
            plan_s[q * ROWS + 9, :, at] = ((block + 1) & 15).astype(jnp.float32)
            plan_s[q * ROWS + 10, :, at] = (lon + begin).astype(jnp.float32)
        return fits

    def weigh_all():
        worst = lax.fori_loop(0, pair_length // LANES, weigh, jnp.zeros((8, LANES), jnp.int32))
        if pair_length % LANES:
            worst = weigh(tiles - 1, worst, pair_length % LANES)
        return worst

    node = lax.broadcasted_iota(jnp.int32, (16, LANES), 0).astype(jnp.float32).astype(jnp.bfloat16)
    zero16 = jnp.zeros((16, LANES), jnp.bfloat16)

    def spread(mine, weight, rest, block, after):
        v = zero16
        for o in (3, 2, 1, 0):
            v = jnp.where(node == rest[o], weight[o], v)
        block = jnp.where(mine, jnp.where(node < rest[0], after, block), jnp.bfloat16(NOWHERE))
        return [jnp.where(block == jnp.bfloat16(a), v, zero16) for a in range(WIN // 16)]

    def plan(d, i, q, at):
        return jnp.broadcast_to(plan_s[q * ROWS + i, pl.ds(d, 1), at], (16, LANES))

    def packed(x):
        return x.astype(jnp.bfloat16)

    def locate():
        for q in range(pairs):
            pair = first + q
            northern = pair < half_rows // 2
            inner = jnp.where(northern, pair, half_rows - 1 - pair)
            for half in range(2):
                number = half_rows // 2 + 1 + inner if half else half_rows // 2 - inner
                g = jnp.where(northern, number - 1, 2 * half_rows - number)
                base = jnp.clip(g - 2, 0, 2 * half_rows - 4)
                for d in range(5):
                    pair_row, begin, length = row_place(jnp.minimum(base + d, 2 * half_rows - 1), half_rows)
                    short = length <= WIN - 4
                    copy = 2 * jnp.clip(pair_row - first + 2, 0, near - 1) + (begin > 0).astype(jnp.int32)
                    at = 3 * ((2 * q + half) * 5 + d)
                    place_t[at] = copy
                    place_t[at + 1] = begin + LANES + jnp.where(short, -1, -MARGIN)
                    place_t[at + 2] = jnp.where(short, 0, 1)

    def unit_scalars(q, u):
        len0, _ = half_lengths(first + q)
        straddle = len0 >> 7
        half = (u > straddle).astype(jnp.int32)
        tile = u - half
        k0 = jnp.where(half == 1, jnp.maximum(tile * LANES - len0, 0), tile * LANES)
        return len0, straddle, half, tile, 15 * (2 * q + half), k0

    lane16 = lax.broadcasted_iota(jnp.int32, (16, LANES), 1).astype(jnp.float32).astype(jnp.bfloat16)

    def own_half(half, tile, len0):
        edge = jnp.clip(len0 - tile * LANES, 0, LANES)
        low = jnp.where(half == 1, edge, 0).astype(jnp.float32)
        high = jnp.where(half == 1, LANES, edge).astype(jnp.float32)
        spread_low = jnp.full((16, LANES), low, jnp.float32).astype(jnp.bfloat16)
        spread_high = jnp.full((16, LANES), high, jnp.float32).astype(jnp.bfloat16)
        return (lane16 >= spread_low) & (lane16 < spread_high)

    def finish(q, u, straddle, tile, total, carry):
        total = total + jnp.where(u == straddle + 1, carry, 0.0)
        at = pl.ds(pl.multiple_of(tile * LANES, LANES), LANES)
        y_s[q, :, at] = total.astype(jnp.bfloat16)
        head_s[q, :, at] = total[:head_s.shape[1]].astype(jnp.bfloat16)
        return total

    def near_units(chosen):
        def unit(q, u, carry):
            len0, straddle, half, tile, base, k0 = unit_scalars(q, u)
            at = pl.ds(pl.multiple_of(tile * LANES, LANES), LANES)
            mine = own_half(half, tile, len0)
            rows, weights = [], []
            for d in range(5):
                where_row = place_t[base + 3 * d]
                begin = place_t[base + 3 * d + 1] + place_t[base + 3 * d + 2] * k0
                s = begin & 127
                first_tile = pl.multiple_of((begin >> 7) * LANES, LANES)
                row = [packed(plan(d, i, q, at)) for i in range(10)]
                weights += spread(mine, row[:4], row[4:8], row[8], row[9])
                three = ext_s[where_row, :, pl.ds(first_tile, 3 * LANES)]
                rows += [jnp.where(lane >= s, three[:, :LANES], three[:, 2 * LANES:]), three[:, LANES:2 * LANES]]
            total = jnp.dot(jnp.concatenate(rows, axis=1), jnp.concatenate(weights, axis=0),
                            preferred_element_type=jnp.float32)
            return finish(q, u, straddle, tile, total, carry)

        lax.fori_loop(0, tiles + 1, lambda u, carry: tuple(unit(q, u, c) for q, c in zip(chosen, carry)),
                      (jnp.zeros((fields, LANES), jnp.float32),) * len(chosen))

    def any_units():
        def unit(q, u, carry):
            len0, straddle, half, tile, base, _ = unit_scalars(q, u)
            at = pl.ds(pl.multiple_of(tile * LANES, LANES), LANES)
            mine = own_half(half, tile, len0)

            def window(w, total):
                rows, weights = [], []
                for d in range(5):
                    where_row = place_t[base + 3 * d]
                    place = (plan(d, 10, q, at) + (LANES - 1)).astype(jnp.int32) - w * WIN
                    block = jnp.clip(place >> 4, -2, 18)
                    rest = [packed(((place + o) & 15).astype(jnp.float32)) for o in range(4)]
                    weight = [packed(plan(d, o, q, at)) for o in range(4)]
                    weights += spread(mine, weight, rest, packed(block.astype(jnp.float32)), packed((block + 1).astype(jnp.float32)))
                    rows.append(ext_s[where_row, :, pl.ds(pl.multiple_of(w * WIN, WIN), WIN)])
                return total + jnp.dot(jnp.concatenate(rows, axis=1), jnp.concatenate(weights, axis=0),
                                       preferred_element_type=jnp.float32)

            total = lax.fori_loop(0, EW // WIN, window, jnp.zeros((fields, LANES), jnp.float32))
            return finish(q, u, straddle, tile, total, carry)

        lax.fori_loop(0, tiles + 1, lambda u, carry: tuple(unit(q, u, carry[q]) for q in range(pairs)),
                      (jnp.zeros((fields, LANES), jnp.float32),) * pairs)

    def deliver(out_ref):
        for f in range(groups):
            for q in range(pairs):
                out_ref[f, q] = y_s[q, pl.ds(levels * f, levels), pl.ds(0, pair_length)]

    steps.clear, steps.fill, steps.close, steps.weigh_all, steps.locate = clear, fill, close, weigh_all, locate
    steps.near_units, steps.any_units, steps.deliver, steps.near = near_units, any_units, deliver, near
    return steps


def stencil_scratch(pairs, fields, pair_length):
    padded = pl.cdiv(pair_length, LANES) * LANES
    return [
        pltpu.SMEM((30 * pairs,), jnp.int32),
        pltpu.VMEM((2 * (pairs + 4), fields, EW), jnp.bfloat16),
        pltpu.VMEM((pairs * ROWS, 8, padded), jnp.float32),
        pltpu.VMEM((pairs, fields, padded), jnp.bfloat16),
    ]


def by_slot_then_device(wave, devices):
    count = wave.shape[1]
    slots = count // devices
    wanted = lax.broadcasted_iota(jnp.int32, (1, count), 1)
    wanted = slots * (wanted % devices) + wanted // devices
    moves = (lax.broadcasted_iota(jnp.int32, (count, count), 0) == wanted).astype(jnp.float32).astype(jnp.bfloat16)
    high, low = wave // 8, wave % 8
    sub = lax.broadcasted_iota(jnp.int32, (16, count), 0)
    digits = jnp.where(sub == 0, high, jnp.where(sub == 1, low, 0)).astype(jnp.float32).astype(jnp.bfloat16)
    moved = jnp.dot(digits, moves, preferred_element_type=jnp.float32)
    return (8.0 * moved[0:1] + moved[1:2]).astype(jnp.int32)


def whole_kernel(sizes, half_rows, pair_length, grid_hbm, row_hbm, lon_hbm, lonf_hbm, latf_hbm, wave_ref, waves_ref, legendre_hbm,
                 out_ref, result_ref, far_ref, before_s, after_s, order_ref,
                 own_s, row_s, lon_s, lonf_s, latf_s, place_t, ext_s, plan_s, y_s, head_s,
                 in_sem, halo_send_sem, halo_recv_sem, *refs):
    along, across = sizes
    devices = along * across
    pairs = own_s.shape[1]
    me = lax.axis_index("aa") * across + lax.axis_index("ba")
    up = lax.rem(me + 1, devices)
    down = lax.rem(me + devices - 1, devices)

    def where(device):
        return (device // across, lax.rem(device, across))

    after_steps = transform_steps(sizes, pair_length, head_s, waves_ref, legendre_hbm, result_ref, refs[:14], refs[14:])
    barrier = pltpu.get_barrier_semaphore()
    loads = [pltpu.make_async_copy(src, dst, in_sem.at[i]) for i, (src, dst) in enumerate((
        (row_hbm, row_s), (lon_hbm, lon_s), (lonf_hbm, lonf_s), (latf_hbm, latf_s), (grid_hbm, own_s)))]
    for load in loads:
        load.start()
    after_steps.greet(barrier)

    steps = stencil_steps(half_rows, pair_length, me * pairs, (before_s, own_s, after_s), row_s, lon_s, lonf_s, latf_s,
                          place_t, ext_s, plan_s, y_s, head_s)
    steps.clear()
    for load in loads:
        load.wait()
    flag = jnp.max(steps.weigh_all())

    pl.semaphore_wait(barrier, devices - 1)
    sends = []
    for i, (row, dst, slot, device) in enumerate((
            (pairs - 1, before_s, 1, up), (0, after_s, 0, down), (pairs - 2, before_s, 0, up), (1, after_s, 1, down))):
        sends.append(pltpu.make_async_remote_copy(
            src_ref=grid_hbm.at[:, pl.ds(row, 1)], dst_ref=dst.at[:, pl.ds(slot, 1)], send_sem=halo_send_sem.at[i],
            recv_sem=halo_recv_sem.at[i], device_id=where(device), device_id_type=pl.DeviceIdType.MESH))
        sends[-1].start()
    for j in range(2, 2 + pairs):
        steps.fill(j)
    for j in range(2, 2 + pairs):
        steps.close(j)
    order = by_slot_then_device(wave_ref[...].reshape(1, half_rows), devices)
    order_ref[...] = order
    steps.locate()
    inner = tuple(range(2, pairs - 2))
    steps.near_units(inner)
    for arriving, rows, units in ((sends[:2], (1, 2 + pairs), (1, pairs - 2)), (sends[2:], (0, 3 + pairs), (0, pairs - 1))):
        for send in arriving:
            send.wait()
        for j in rows:
            steps.fill(j)
        for j in rows:
            steps.close(j)
        steps.near_units(units)
    after_steps.sums()
    after_steps.lay_out(order_ref[...], flag)
    own = after_steps.trade()
    steps.deliver(out_ref)
    far_ref[0] = (after_steps.finish(own) > 0.0).astype(jnp.int32)


def far_kernel(half_rows, pair_length, first_ref, before_ref, own_ref, after_ref, row_ref, lon_ref, lonf_ref, latf_ref,
               out_ref, head_ref, place_t, ext_s, plan_s, y_s):
    steps = stencil_steps(half_rows, pair_length, first_ref[0], (before_ref, own_ref, after_ref), row_ref, lon_ref, lonf_ref, latf_ref,
                          place_t, ext_s, plan_s, y_s, head_ref)
    steps.locate()
    steps.clear()
    steps.weigh_all()
    for j in range(steps.near):
        steps.fill(j)
    for j in range(steps.near):
        steps.close(j)
    steps.any_units()
    steps.deliver(out_ref)


def both(first, grid, dep_row, dep_lon, lon_frac, lat_frac, wave_slot, legendre, half_rows, spectral_fields, sizes):
    groups, pairs, levels, pair_length = grid.shape
    fields = groups * levels
    slots = legendre.shape[0]
    padded = pl.cdiv(pair_length, LANES) * LANES
    b16, f32, i32 = jnp.bfloat16, jnp.float32, jnp.int32
    vm, anywhere, scalars = (pl.BlockSpec(memory_space=m) for m in (pltpu.VMEM, pl.ANY, pltpu.SMEM))
    halo = jax.ShapeDtypeStruct((groups, 2, levels, pair_length), b16)
    head = jax.ShapeDtypeStruct((pairs, spectral_fields, padded), b16)
    full = jax.ShapeDtypeStruct(grid.shape, b16)
    stencil = stencil_scratch(pairs, fields, pair_length)
    local = [
        pltpu.VMEM(grid.shape, b16), pltpu.VMEM(dep_row.shape, i32), pltpu.VMEM(dep_lon.shape, i32), pltpu.VMEM(lon_frac.shape, f32), pltpu.VMEM(lat_frac.shape, f32),
    ] + stencil + [pltpu.VMEM(head.shape, b16)]
    out, result, far, before, after, order = pl.pallas_call(
        functools.partial(whole_kernel, sizes, half_rows, pair_length),
        out_shape=(full, jax.ShapeDtypeStruct((slots, 16, half_rows), f32), jax.ShapeDtypeStruct((1,), i32), halo, halo,
                   jax.ShapeDtypeStruct((1, half_rows), i32)),
        in_specs=[anywhere] * 5 + [vm, scalars, anywhere],
        out_specs=(vm, vm, scalars, vm, vm, vm),
        scratch_shapes=local + [pltpu.SemaphoreType.DMA((5,)), pltpu.SemaphoreType.DMA((4,)), pltpu.SemaphoreType.DMA((4,))] + transform_scratch(pairs, slots, half_rows, pair_length, legendre),
        compiler_params=pltpu.CompilerParams(collective_id=1, has_side_effects=True),
        name="whole",
    )(grid, dep_row, dep_lon, lon_frac, lat_frac, wave_slot, wave_slot, legendre)

    def again():
        redone, first_fields = pl.pallas_call(
            functools.partial(far_kernel, half_rows, pair_length),
            out_shape=(full, head),
            in_specs=[scalars] + [vm] * 7,
            out_specs=(vm, vm),
            scratch_shapes=stencil,
            name="far",
        )(first, before, grid, after, dep_row, dep_lon, lon_frac, lat_frac)
        return redone, transform(first_fields, order, wave_slot, legendre, half_rows, pair_length, sizes)

    return lax.cond(far[0] > 0, again, lambda: (out, result))

WIDE = 256

COS = (1, -19.7392087, 64.9393842, -85.4565372, 60.2407014, -26.3960673, 7.77462739, -1.42354417)
SIN = (6.28318531, -41.3417022, 81.6052456, -76.7057546, 42.0572162, -15.0833301, 3.7717259, -0.609657301)


def cos_sin_turns(prod, length, inverse):
    turns = jnp.floor(prod * inverse + 0.5)
    t = (prod - turns * length) * inverse
    x = t * t
    c = jnp.full_like(x, COS[-1])
    for a in COS[-2::-1]:
        c = c * x + a
    s = jnp.full_like(x, SIN[-1])
    for a in SIN[-2::-1]:
        s = s * x + a
    return c, s * t


def transform_steps(sizes, pair_length, y_ref, waves_ref, legendre_hbm, result_ref, scratch, sems):
    (table_s, sums_s, back_s, turn_c, turn_n, four_s, mix_s, stage_s, send_s, got_s, plain_s, anti_s, turn_s, legendre_s) = scratch
    legendre_sem, own_sem, send_sem, recv_sem = sems
    along, across = sizes
    devices = along * across
    pairs = y_ref.shape[0]
    slots = legendre_s.shape[0]
    half_rows = slots * devices
    rows = 2 * pairs
    tiles = pl.cdiv(pair_length, LANES)
    my_a = lax.axis_index("aa")
    my_b = lax.axis_index("ba")
    me = my_a * across + my_b
    first = me * pairs
    north = me < devices // 2
    parts = 8
    wides = pl.cdiv(tiles * LANES, WIDE)

    steps = Stencil()

    weights_in = pltpu.make_async_copy(legendre_hbm, legendre_s, legendre_sem)

    columns = [lax.rem(my_b + i, across) for i in range(across)]

    def partners(act):
        def others(i, _):
            a = lax.rem(my_a + along // 2 + (1 - 2 * lax.rem(i, 2)) * ((i + 1) // 2), along)
            for b in range(across):
                act(a, columns[b])
            return 0

        lax.fori_loop(0, along - 1, others, 0)
        for b in range(1, across):
            act(my_a, columns[b])

    def greet(barrier):
        weights_in.start()
        partners(lambda a, b: pl.semaphore_signal(barrier, inc=1, device_id=(a, b), device_id_type=pl.DeviceIdType.MESH))

    def one(q, half):
        table, sums_of, back, turns_c, turns_n = (x.at[half] for x in (table_s, sums_s, back_s, turn_c, turn_n))
        pair = first + q
        inner = jnp.where(north, pair, half_rows - 1 - pair)
        len0 = 16 + 4 * (half_rows // 2 - inner)
        start = len0 if half else 0
        whole = 16 + 4 * (half_rows // 2 + 1 + inner) if half else len0
        length = jnp.full((1, LANES), whole, jnp.int32).astype(jnp.float32)
        inverse = 1.0 / length

        def line(n):
            return lax.broadcasted_iota(jnp.int32, (n, LANES), 0)

        wave = lax.broadcasted_iota(jnp.int32, (16, LANES), 1)
        fine_c, fine_s = cos_sin_turns((wave * line(16)).astype(jnp.float32), length, inverse)
        step_c, step_s = cos_sin_turns((wave * (16 * line(16))).astype(jnp.float32), length, inverse)
        for a in range(WIDE // 16):
            ca, sa = step_c[a:a + 1], step_s[a:a + 1]
            cosine = ca * fine_c - sa * fine_s
            sine = sa * fine_c + ca * fine_s
            top, bottom = pl.ds(16 * a, 16), pl.ds(WIDE + 16 * a, 16)
            left, right = pl.ds(0, LANES), pl.ds(LANES, LANES)
            table[top, left] = cosine.astype(jnp.bfloat16)
            table[top, right] = sine.astype(jnp.bfloat16)
            table[bottom, left] = (-sine).astype(jnp.bfloat16)
            table[bottom, right] = cosine.astype(jnp.bfloat16)
        tile_c, tile_s = cos_sin_turns((wave * (WIDE * line(16) - start)).astype(jnp.float32), length, inverse)
        back[0], back[1] = tile_c, tile_s
        lane = lax.broadcasted_iota(jnp.int32, (parts, LANES), 1)
        part_c, part_s = cos_sin_turns((LANES * line(8) * (WIDE * lane - start)).astype(jnp.float32), length, inverse)
        shifts = [cos_sin_turns((LANES * line(8) * (lane + i * LANES)).astype(jnp.float32), length, inverse) for i in range(2)]
        for t in range(wides):
            pc, ps = part_c[:, t:t + 1], part_s[:, t:t + 1]
            for i in range(2):
                sc, ss = shifts[i]
                at = pl.ds(t * WIDE + i * LANES, LANES)
                turns_c[:, at] = pc * sc - ps * ss
                turns_n[:, at] = ps * sc + pc * ss
        blocks = [[None] * (2 * 2) for _ in range(wides * slots)]
        for t in range(wides):
            for i in range(2):
                at = t * WIDE + i * LANES
                if at < tiles * LANES:
                    col = lane + at
                    mine = (col >= start) & (col < start + whole)
                    v = jnp.where(mine, y_ref[q, :, pl.ds(at, LANES)].astype(jnp.float32)[:parts], 0.0)
                for w in range(slots):
                    row = blocks[w * wides + t]
                    if at < tiles * LANES:
                        row[i] = v * turns_c[pl.ds(w, 1), pl.ds(at, LANES)]
                        row[2 + i] = v * turns_n[pl.ds(w, 1), pl.ds(at, LANES)]
                    else:
                        row[i] = row[2 + i] = jnp.zeros((parts, LANES), jnp.float32)
        stacked = jnp.concatenate([jnp.concatenate(row, axis=1) for row in blocks], axis=0).astype(jnp.bfloat16)
        sums_of[...] = jnp.dot(stacked, table[...], preferred_element_type=jnp.float32)
        place = 2 * jnp.where(north, q, pairs - 1 - q) + half
        for w in range(slots):
            real = jnp.zeros((parts, LANES), jnp.float32)
            imag = jnp.zeros((parts, LANES), jnp.float32)
            for t in range(wides):
                at = pl.ds(parts * (w * wides + t), parts)
                c, s = sums_of[at, pl.ds(0, LANES)], sums_of[at, pl.ds(LANES, LANES)]
                tc, ts = back[0, pl.ds(t, 1), :], back[1, pl.ds(t, 1), :]
                real = real + (tc * c - ts * s)
                imag = imag - (ts * c + tc * s)
            waves = lax.broadcasted_iota(jnp.int32, (1, LANES), 1) + w * LANES
            keep = jnp.where(2 * waves < whole, inverse, 0.0)
            four_s[pl.ds(pl.multiple_of(place * 16, 16), 16), pl.ds(w * LANES, LANES)] = jnp.concatenate(
                [real * keep, imag * keep], axis=0).astype(jnp.bfloat16)

    def sums():
        def step(q, _):
            for half in range(2):
                one(q, half)
            return 0

        lax.fori_loop(0, pairs, step, 0)

    def lay_out(order, flag):
        hot = (lax.broadcasted_iota(jnp.int32, (half_rows, half_rows), 0) == order).astype(jnp.float32).astype(jnp.bfloat16)
        moved = jnp.dot(four_s[...], hot, preferred_element_type=jnp.float32)
        mix_s[...] = jnp.zeros_like(mix_s)
        raised = jnp.full((16, LANES), flag, jnp.int32).astype(jnp.float32)
        for r in range(8):
            for s in range(slots):
                mix_s[r, pl.ds(16 * s, 16), :] = moved[16 * r:16 * r + 16, s * LANES:(s + 1) * LANES]
            mix_s[r, pl.ds(LANES - 16, 16), :] = raised
            if r < slots:
                for e in range(rows - 8):
                    mix_s[r, pl.ds(16 * (slots + e), 16), :] = moved[16 * (8 + e):16 * (8 + e) + 16, r * LANES:(r + 1) * LANES]
            stage_s[pl.ds(r, LANES, stride=8), :] = mix_s[r].T
        send_s[...] = stage_s[...].astype(jnp.bfloat16).reshape(send_s.shape)

    def post(a, b):
        pltpu.make_async_remote_copy(
            src_ref=send_s.at[a * across + b], dst_ref=got_s.at[me], send_sem=send_sem, recv_sem=recv_sem,
            device_id=(a, b), device_id_type=pl.DeviceIdType.MESH).start()

    def trade():
        partners(post)
        own = pltpu.make_async_copy(send_s.at[me], got_s.at[me], own_sem)
        own.start()
        return own

    def finish(own):
        src = lax.broadcasted_iota(jnp.int32, (slots * LANES, 2 * LANES), 0)
        dst = lax.broadcasted_iota(jnp.int32, (slots * LANES, 2 * LANES), 1)
        unfold = (((dst & 127) >> 4) == (src >> 7)) & ((src & 127) == 16 * (slots + (dst >> 7)) + (dst & 15))
        unfold = unfold.astype(jnp.float32).astype(jnp.bfloat16)
        slot_of = (lax.broadcasted_iota(jnp.int32, (half_rows, LANES), 1) >> 4).astype(jnp.float32).astype(jnp.bfloat16)
        rest = pl.ds(0, devices - 1)
        every = pltpu.make_async_remote_copy(
            src_ref=send_s.at[rest], dst_ref=got_s.at[rest], send_sem=send_sem, recv_sem=recv_sem,
            device_id=(my_a, columns[1]), device_id_type=pl.DeviceIdType.MESH)
        every.wait_send()
        every.wait_recv()
        own.wait()

        highest = jnp.zeros((8, LANES), jnp.float32)
        for d in range(devices // 2):
            n = got_s[d].astype(jnp.float32)
            o = got_s[devices - 1 - d].astype(jnp.float32)
            highest = jnp.maximum(highest, jnp.maximum(n, o))
            plain_s[pl.ds(rows * d, 8), :] = n + o
            anti_s[pl.ds(rows * d, 8), :] = n - o
        weights_in.wait()
        for par, wide in ((0, plain_s), (1, anti_s)):
            folded = jnp.concatenate([wide[pl.ds(s, devices // 2, stride=rows), :] for s in range(slots)], axis=1).astype(jnp.bfloat16)
            extra = jnp.dot(folded, unfold, preferred_element_type=jnp.float32)
            for e in range(rows - 8):
                wide[pl.ds(8 + e, devices // 2, stride=rows), :] = extra[:, e * LANES:(e + 1) * LANES]
            values = wide[...].astype(jnp.bfloat16)
            zero = jnp.zeros_like(values)
            picked = jnp.concatenate([jnp.where(slot_of == jnp.bfloat16(s), values, zero) for s in range(slots)], axis=0)
            table = jnp.concatenate([legendre_s[s, par] for s in range(slots)], axis=1)
            turn_s[pl.ds(par, half_rows // 2, stride=2), :] = jnp.dot(table, picked, preferred_element_type=jnp.float32)
        z = turn_s[...].T
        degree = lax.broadcasted_iota(jnp.int32, (16, half_rows), 1)
        for s in range(slots):
            limit = half_rows - waves_ref[me * slots + s]
            result_ref[s] = jnp.where(degree < limit, z[16 * s:16 * s + 16], 0.0)
        lanes = lax.broadcasted_iota(jnp.int32, (8, LANES), 1)
        return jnp.max(jnp.where(lanes >= LANES - 16, highest, 0.0))

    steps.greet, steps.sums, steps.lay_out, steps.trade, steps.finish, steps.others = greet, sums, lay_out, trade, finish, devices - 1
    return steps


def transform_kernel(sizes, pair_length, y_ref, order_ref, waves_ref, legendre_hbm, out_ref, *refs):
    steps = transform_steps(sizes, pair_length, y_ref, waves_ref, legendre_hbm, out_ref, refs[:14], refs[14:])
    barrier = pltpu.get_barrier_semaphore()
    steps.greet(barrier)
    steps.sums()
    steps.lay_out(order_ref[...], 0)
    pl.semaphore_wait(barrier, steps.others)
    steps.finish(steps.trade())


def transform_scratch(pairs, slots, half_rows, pair_length, legendre):
    tiles = pl.cdiv(pair_length, LANES)
    wides = pl.cdiv(tiles * LANES, WIDE)
    f32, b16 = jnp.float32, jnp.bfloat16
    return [
        pltpu.VMEM((2, 2 * WIDE, 2 * LANES), b16),
        pltpu.VMEM((2, 8 * wides * slots, 2 * LANES), f32),
        pltpu.VMEM((2, 2, 16, LANES), f32),
        pltpu.VMEM((2, 8, WIDE * wides), f32),
        pltpu.VMEM((2, 8, WIDE * wides), f32),
        pltpu.VMEM((32 * pairs, half_rows), b16),
        pltpu.VMEM((8, LANES, LANES), f32),
        pltpu.VMEM((8 * LANES, LANES), f32),
        pltpu.VMEM((LANES, 8, LANES), b16),
        pltpu.VMEM((LANES, 8, LANES), b16),
        pltpu.VMEM((half_rows, LANES), f32),
        pltpu.VMEM((half_rows, LANES), f32),
        pltpu.VMEM((half_rows, LANES), f32),
        pltpu.VMEM(legendre.shape, b16),
        pltpu.SemaphoreType.DMA, pltpu.SemaphoreType.DMA, pltpu.SemaphoreType.DMA, pltpu.SemaphoreType.DMA,
    ]


def transform(y, order, waves, legendre, half_rows, pair_length, sizes):
    pairs = y.shape[0]
    slots = legendre.shape[0]
    vm = pl.BlockSpec(memory_space=pltpu.VMEM)
    f32 = jnp.float32
    return pl.pallas_call(
        functools.partial(transform_kernel, sizes, pair_length),
        out_shape=jax.ShapeDtypeStruct((slots, 16, half_rows), f32),
        in_specs=[vm, vm, pl.BlockSpec(memory_space=pltpu.SMEM), pl.BlockSpec(memory_space=pl.ANY)],
        out_specs=vm,
        scratch_shapes=transform_scratch(pairs, slots, half_rows, pair_length, legendre),
        compiler_params=pltpu.CompilerParams(collective_id=0, has_side_effects=True),
        name="transform",
    )(y, order, waves, legendre)


def on_device(grid, dep_row, dep_lon, lon_frac, lat_frac, wave_slot, legendre):
    half_rows = wave_slot.shape[0]
    _, levels, pairs, pair_length = grid.shape
    axes = ("aa", "ba")
    sizes = (lax.axis_size("aa"), lax.axis_size("ba"))
    devices = sizes[0] * sizes[1]
    first = (lax.axis_index(axes) * pairs).astype(jnp.int32).reshape(1)
    own = jnp.transpose(grid, (0, 2, 1, 3))
    out, result = both(first, own, dep_row, jnp.transpose(dep_lon, (1, 0, 2)), jnp.transpose(lon_frac, (1, 0, 2)),
                       lat_frac, wave_slot, legendre, half_rows, 2 * levels, sizes)
    return (jnp.transpose(out, (0, 2, 1, 3)), jnp.transpose(result, (1, 0, 2)))


def solution(mesh):
    return jax.shard_map(
        on_device,
        mesh=mesh,
        in_specs=(
            P(None, None, ("aa", "ba"), None),
            P(("aa", "ba"), None),
            P(None, ("aa", "ba"), None),
            P(None, ("aa", "ba"), None),
            P(("aa", "ba"), None),
            P(),
            P(("aa", "ba"), None, None, None),
        ),
        out_specs=(P(None, None, ("aa", "ba"), None), P(None, ("aa", "ba"), None)),
        check_vma=False,
    )
```
